32 devices in a mesh: grid: 4 (over z), dom: 8 (over y, x, core).
Axes of the slice: x: 2, y: 2, z: 4, core: 2. Of those that a mesh axis runs over, the one named last changes fastest.
Arguments:
- columns: bfloat16 [65536, 128], P(('grid', 'dom')), may hold values from -6 to 6
- column_live: int32 [65536], P(('grid', 'dom')), may hold values 0 or 1
- col_weight: float32 [65536], P(('grid', 'dom')), may hold values from 0.2 to 1
- col_slot: int32 [65536], P(('grid', 'dom')), may hold values from 0 to 511
- node_static: bfloat16 [16384, 256], P(('grid', 'dom')), may hold values from -6 to 6
- boundary_idx: int32 [8192], P(('grid', 'dom')), may hold values from 0 to 511
- edge_src: int32 [65536], P(('grid', 'dom')), may hold values from 0 to 1535
- edge_dst: int32 [65536], P(('grid', 'dom')), may hold values from 0 to 511
- edge_live: int32 [65536], P(('grid', 'dom')), may hold values from 0 to 1, as said below
- edge_weight: float32 [65536], P(('grid', 'dom')), may hold values from 0.2 to 1
- enc_in: bfloat16 [128, 256], replicated, may hold values from -0.5 to 0.5
- enc_out: bfloat16 [256, 256], replicated, may hold values from -0.375 to 0.375
- src_proj: bfloat16 [2, 256, 256], replicated, may hold values from -0.375 to 0.375
- dst_proj: bfloat16 [2, 256, 256], replicated, may hold values from -0.375 to 0.375
- msg_proj: bfloat16 [2, 256, 256], replicated, may hold values from -0.375 to 0.375
- node_cotangent: bfloat16 [16384, 256], P(('grid', 'dom')), may hold values from -6 to 6
Outputs:
- node_out: bfloat16 [16384, 256], P(('grid', 'dom'))
- enc_in_grad: float32 [128, 256], replicated
- enc_out_grad: float32 [256, 256], replicated
- src_grad: float32 [2, 256, 256], replicated
- dst_grad: float32 [2, 256, 256], replicated
- msg_grad: float32 [2, 256, 256], replicated
The draws below stay inside these ranges and needn't reach their ends.
Inputs may be any that keep to these rules, and one draw needn't show every extreme that they name: `col_slot`: column slot j of a partition, with k * 64 <= j < (k + 1) * 64, is bound for partition k. `edge_src`: values below 512 are the partition's own nodes; 512 + r * 256 + i is boundary entry i of neighbour r (r = 0 to 3 as in the reference program). `edge_live`: in each partition the live edge slots come first; some partition has all 2048 live.
All inputs are finite; a program needn't handle non-finite values. No bound on the sum of `column_live` on one device may be relied on, other than what follows from the above.
Results may differ from the reference program's by a relative error of at most 0.0095.
Values may be sent and summed in bfloat16 or wider, within the bound.
No kernel may reach another device: no remote copies, remote signals or barrier semaphores. Data moves between devices by JAX's collectives and lax.ppermute only.
A program may use at most 128 MiB of HBM per device.

```python
import jax
import jax.numpy as jnp
from jax import lax

H = 256
FIN = 128
LAYERS = 2
NODE_DEV = 512
E_DEV = 2048
BND = 256
COL_DEV = 2048
NODES = 16384
EDGES = 65536
BOUNDS = 8192
COLUMNS = 65536
EXT = 1536
N_GRID = 4
N_DOM = 8
DEVICES = 32


def draw_edge_live(key, part):
    first_key, second_key = jax.random.split(jax.random.fold_in(key, 11))
    raw_counts = jax.random.randint(first_key, (DEVICES,), 0, E_DEV + 1)
    counts = jnp.maximum(raw_counts * raw_counts // E_DEV, E_DEV // 16)
    fullest = jax.random.randint(second_key, (), 0, DEVICES)
    counts = jnp.where(jnp.arange(DEVICES) == fullest, E_DEV, counts)
    positions = jnp.arange(E_DEV)
    return (positions[None, :] < counts[:, None]).astype(jnp.int32).reshape(DEVICES * E_DEV)


def set_ends(result, own_key, low, top_value):
    extent = result.shape
    index_at = [jax.random.randint(jax.random.fold_in(own_key, axis), (), 0, extent[axis]) for axis in range(len(extent))]
    result = result.at[tuple(index_at)].set(low)
    longest = extent.index(max(extent))
    index_at[longest] = (index_at[longest] + 1) % extent[longest]
    return result.at[tuple(index_at)].set(top_value)


def levels(stream_key, dims, cuts, smallest, largest):
    def one(dim, blocks):
        heights = jax.random.uniform(jax.random.fold_in(jax.random.fold_in(stream_key, 6), dim), (blocks,), jnp.float32, smallest / len(cuts), largest / len(cuts))
        return jnp.repeat(jnp.exp(heights), dims[dim] // blocks).reshape((-1,) + (1,) * (len(dims) - dim - 1))

    loudness = one(*cuts[0])
    for cut in cuts[1:]:
        loudness = loudness * one(*cut)
    return loudness


def bell_draw(stream_key, dims, spread, bound, cuts=(), held_as=jnp.bfloat16):
    level = levels(stream_key, dims, cuts, -0.22, 0.18) if cuts else 1.0
    entries = jax.random.normal(stream_key, dims, jnp.float32) * spread * level
    return jnp.minimum(jnp.maximum(entries, -bound), bound).astype(held_as)


def setup_inputs(seed: int = 0) -> dict:
    arg_keys = jax.random.split(jax.random.key(seed), 17)
    return {
        "columns": bell_draw(arg_keys[0], (COLUMNS, FIN), 1.0, 6.0, ((0, 32),)),
        "column_live": set_ends((jax.random.randint(arg_keys[1], (COLUMNS,), 0, 2) < 1).astype(jnp.int32), jax.random.fold_in(arg_keys[1], 1), 0, 1),
        "col_weight": jnp.clip(0.2 + 0.8 * jax.random.uniform(arg_keys[2], (COLUMNS,), jnp.float32) ** levels(arg_keys[2], (COLUMNS,), ((0, 32),), -0.2, 0.2), 0.2, 1.0),
        "col_slot": set_ends(jax.random.randint(arg_keys[3], (COLUMNS,), 0, NODE_DEV), jax.random.fold_in(arg_keys[3], 1), 0, NODE_DEV - 1).astype(jnp.int32),
        "node_static": bell_draw(arg_keys[4], (NODES, H), 1.0, 6.0, ((0, 32),)),
        "boundary_idx": set_ends(jax.random.randint(arg_keys[5], (BOUNDS,), 0, NODE_DEV), jax.random.fold_in(arg_keys[5], 1), 0, NODE_DEV - 1).astype(jnp.int32),
        "edge_src": set_ends(jax.random.randint(arg_keys[6], (EDGES,), 0, EXT), jax.random.fold_in(arg_keys[6], 1), 0, EXT - 1).astype(jnp.int32),
        "edge_dst": set_ends(jax.random.randint(arg_keys[7], (EDGES,), 0, NODE_DEV), jax.random.fold_in(arg_keys[7], 1), 0, NODE_DEV - 1).astype(jnp.int32),
        "edge_live": draw_edge_live(jax.random.fold_in(arg_keys[16], 71), 0),
        "edge_weight": jnp.clip(0.2 + 0.8 * jax.random.uniform(arg_keys[9], (EDGES,), jnp.float32) ** levels(arg_keys[9], (EDGES,), ((0, 32),), -0.2, 0.2), 0.2, 1.0),
        "enc_in": bell_draw(arg_keys[10], (FIN, H), FIN ** -0.5, 0.5),
        "enc_out": bell_draw(arg_keys[11], (H, H), H ** -0.5, 0.375),
        "src_proj": bell_draw(arg_keys[12], (LAYERS, H, H), H ** -0.5, 0.375),
        "dst_proj": bell_draw(arg_keys[13], (LAYERS, H, H), H ** -0.5, 0.375),
        "msg_proj": bell_draw(arg_keys[14], (LAYERS, H, H), H ** -0.5, 0.375),
        "node_cotangent": bell_draw(arg_keys[15], (NODES, H), 1.0, 6.0, ((0, 32),)),
    }


def silu_grad(inputs):
    sigmoid_val = jax.nn.sigmoid(inputs)
    return sigmoid_val * (1.0 + inputs * (1.0 - sigmoid_val))

def outer_sum(left_side, right_side):
    return lax.dot_general(left_side, right_side, (((0,), (0,)), ((), ())), preferred_element_type=jnp.float32)

def times_transpose(left_side, right_side):
    return lax.dot_general(left_side, right_side, (((1,), (1,)), ((), ())), preferred_element_type=jnp.float32)

def pick_rows(rows_all, indices):
    return rows_all[indices]

def scatter_rows(values, indices):
    return jax.ops.segment_sum(values, indices, num_segments=NODE_DEV)

def grid_view(blocks):
    return blocks.reshape((N_GRID, N_DOM) + blocks.shape[1:])

def shifted(blocks, axis_pos, offset):
    length = blocks.shape[axis_pos]
    blank_row = jnp.zeros_like(lax.slice_in_dim(blocks, 0, 1, axis=axis_pos))
    if offset > 0:
        return jnp.concatenate([blank_row, lax.slice_in_dim(blocks, 0, length - 1, axis=axis_pos)], axis_pos)
    return jnp.concatenate([lax.slice_in_dim(blocks, 1, length, axis=axis_pos), blank_row], axis_pos)

def neighbour_rims(node_state, rim_idx):
    rims = grid_view(jax.vmap(pick_rows)(node_state, rim_idx))
    stacked = jnp.stack([shifted(rims, 0, 1), shifted(rims, 0, -1), shifted(rims, 1, 1), shifted(rims, 1, -1)], 2)
    return stacked.reshape(DEVICES, 4 * BND, H)

def reference(columns, column_live, col_weight, col_slot, node_static, boundary_idx, edge_src, edge_dst, edge_live, edge_weight, enc_in, enc_out, src_proj, dst_proj, msg_proj, node_cotangent):
    bucket = COL_DEV // DEVICES
    col_blocks = columns.reshape(DEVICES, COL_DEV, FIN)
    scale_blocks = (col_weight * column_live.astype(jnp.float32)).reshape(DEVICES, COL_DEV)
    edge_scale = (edge_weight * edge_live.astype(jnp.float32)).reshape(DEVICES, E_DEV)
    src_blocks = edge_src.reshape(DEVICES, E_DEV)
    dst_blocks = edge_dst.reshape(DEVICES, E_DEV)
    rim_idx = boundary_idx.reshape(DEVICES, BND)

    def encode_one(pieces):
        col_rows, col_scale = pieces
        enc_pre = jnp.dot(col_rows, enc_in, preferred_element_type=jnp.float32)
        enc_act = jax.nn.silu(enc_pre).astype(jnp.bfloat16)
        return (jnp.dot(enc_act, enc_out, preferred_element_type=jnp.float32) * col_scale[:, None]).astype(jnp.bfloat16)
    col_embed = lax.map(encode_one, (col_blocks, scale_blocks))
    arrived = col_embed.reshape(DEVICES, DEVICES, bucket, H).transpose(1, 0, 2, 3).reshape(DEVICES, COL_DEV, H)
    arrived_slots = col_slot.reshape(DEVICES, DEVICES, bucket).transpose(1, 0, 2).reshape(DEVICES, COL_DEV)

    def pool_one(pieces):
        rows_in, slots_in, static_rows = pieces
        pooled = jax.ops.segment_sum(rows_in.astype(jnp.float32), slots_in, num_segments=NODE_DEV)
        return (static_rows.astype(jnp.float32) + pooled).astype(jnp.bfloat16)
    node_state = lax.map(pool_one, (arrived, arrived_slots, node_static.reshape(DEVICES, NODE_DEV, H)))
    states = []
    for layer_idx in range(LAYERS):
        src_w = src_proj[layer_idx]
        dst_w = dst_proj[layer_idx]
        msg_w = msg_proj[layer_idx]

        def forward_one(pieces):
            own_rows, rim_rows, src_idx, dst_idx, scale_row = pieces
            src_table = jnp.concatenate([own_rows, rim_rows], 0)
            from_src = jnp.dot(src_table, src_w, preferred_element_type=jnp.float32)
            from_dst = jnp.dot(own_rows, dst_w, preferred_element_type=jnp.float32)
            pre_edge = from_src[src_idx] + from_dst[dst_idx]
            act_edge = jax.nn.silu(pre_edge).astype(jnp.bfloat16)
            message = jnp.dot(act_edge, msg_w, preferred_element_type=jnp.float32) * scale_row[:, None]
            gathered = jax.ops.segment_sum(message, dst_idx, num_segments=NODE_DEV)
            return (own_rows.astype(jnp.float32) + gathered).astype(jnp.bfloat16)
        states.append(node_state)
        rims_now = neighbour_rims(node_state, rim_idx)
        node_state = lax.map(forward_one, (node_state, rims_now, src_blocks, dst_blocks, edge_scale))
    node_out = node_state.reshape(NODES, H)
    grad_state = node_cotangent.astype(jnp.float32).reshape(DEVICES, NODE_DEV, H)
    src_terms = [None] * LAYERS
    dst_terms = [None] * LAYERS
    msg_terms = [None] * LAYERS
    for layer_idx in reversed(range(LAYERS)):
        src_w = src_proj[layer_idx]
        dst_w = dst_proj[layer_idx]
        msg_w = msg_proj[layer_idx]

        def backward_one(pieces):
            own_rows, rim_rows, src_idx, dst_idx, scale_row, grad_out = pieces
            src_table = jnp.concatenate([own_rows, rim_rows], 0)
            from_src = jnp.dot(src_table, src_w, preferred_element_type=jnp.float32)
            from_dst = jnp.dot(own_rows, dst_w, preferred_element_type=jnp.float32)
            pre_edge = from_src[src_idx] + from_dst[dst_idx]
            act_edge = jax.nn.silu(pre_edge).astype(jnp.bfloat16)
            grad_msg = (grad_out[dst_idx] * scale_row[:, None]).astype(jnp.bfloat16)
            msg_term = outer_sum(act_edge, grad_msg)
            grad_act = times_transpose(grad_msg, msg_w)
            grad_pre = grad_act * silu_grad(pre_edge)
            grad_src = jax.ops.segment_sum(grad_pre, src_idx, num_segments=NODE_DEV + 4 * BND).astype(jnp.bfloat16)
            grad_dst = jax.ops.segment_sum(grad_pre, dst_idx, num_segments=NODE_DEV).astype(jnp.bfloat16)
            src_term = outer_sum(src_table, grad_src)
            dst_term = outer_sum(own_rows, grad_dst)
            grad_table = times_transpose(grad_src, src_w)
            grad_own = grad_out + grad_table[:NODE_DEV] + times_transpose(grad_dst, dst_w)
            return (grad_own, grad_table[NODE_DEV:].reshape(4, BND, H), src_term, dst_term, msg_term)
        own_state = states[layer_idx]
        rims_now = neighbour_rims(own_state, rim_idx)
        grad_own, grad_rims, src_all, dst_all, msg_all = lax.map(backward_one, (own_state, rims_now, src_blocks, dst_blocks, edge_scale, grad_state))
        src_terms[layer_idx] = lax.optimization_barrier(jnp.sum(src_all, 0))
        dst_terms[layer_idx] = lax.optimization_barrier(jnp.sum(dst_all, 0))
        msg_terms[layer_idx] = lax.optimization_barrier(jnp.sum(msg_all, 0))
        returned = grid_view(grad_rims)
        rim_grad = shifted(returned[:, :, 0], 0, -1) + shifted(returned[:, :, 1], 0, 1) + shifted(returned[:, :, 2], 1, -1) + shifted(returned[:, :, 3], 1, 1)
        grad_state = grad_own + jax.vmap(scatter_rows)(rim_grad.reshape(DEVICES, BND, H), rim_idx)
    grad_nodes = grad_state.astype(jnp.bfloat16)
    back_rows = jax.vmap(pick_rows)(grad_nodes, arrived_slots)
    grad_embed = back_rows.reshape(DEVICES, DEVICES, bucket, H).transpose(1, 0, 2, 3).reshape(DEVICES, COL_DEV, H)

    def encode_back(pieces):
        col_rows, col_scale, grad_rows = pieces
        enc_pre = jnp.dot(col_rows, enc_in, preferred_element_type=jnp.float32)
        enc_act = jax.nn.silu(enc_pre).astype(jnp.bfloat16)
        grad_enc = (grad_rows.astype(jnp.float32) * col_scale[:, None]).astype(jnp.bfloat16)
        out_term = outer_sum(enc_act, grad_enc)
        grad_act = times_transpose(grad_enc, enc_out)
        grad_pre = (grad_act * silu_grad(enc_pre)).astype(jnp.bfloat16)
        in_term = outer_sum(col_rows, grad_pre)
        return (in_term, out_term)
    in_all, out_all = lax.map(encode_back, (col_blocks, scale_blocks, grad_embed))
    enc_in_grad = lax.optimization_barrier(jnp.sum(in_all, 0))
    enc_out_grad = lax.optimization_barrier(jnp.sum(out_all, 0))
    return (node_out, enc_in_grad, enc_out_grad, jnp.stack(src_terms, 0), jnp.stack(dst_terms, 0), jnp.stack(msg_terms, 0))
```

```python
import jax
import jax.numpy as jnp
from jax import lax
from jax.sharding import PartitionSpec as P

AXES = ("grid", "dom")
BF = jnp.bfloat16
F32 = jnp.float32


def mm(left_side, right_side):
    return jnp.dot(left_side, right_side, preferred_element_type=F32)


def mm_t(left_side, right_side):
    return lax.dot_general(
        left_side, right_side, (((1,), (1,)), ((), ())), preferred_element_type=F32
    )


def t_mm(left_side, right_side):
    return lax.dot_general(
        left_side, right_side, (((0,), (0,)), ((), ())), preferred_element_type=F32
    )


def picks(indices, count, start=0):
    return (indices[:, None] == start + jnp.arange(count, dtype=jnp.int32)[None, :]).astype(BF)


def picks_t(indices, count, start=0):
    return (indices[None, :] == start + jnp.arange(count, dtype=jnp.int32)[:, None]).astype(BF)


def silu_grad(inputs):
    sigmoid_val = jax.nn.sigmoid(inputs)
    return sigmoid_val * (1.0 + inputs * (1.0 - sigmoid_val))


def passed_along(shard, axis, by):
    count = lax.axis_size(axis)
    pairs = [(i, i + by) for i in range(count) if 0 <= i + by < count]
    return lax.ppermute(shard, axis, pairs)


def exchange(shard, axes):
    count = shard.shape[0]
    return lax.all_to_all(shard, axes, split_axis=0, concat_axis=0, tiled=True)


def summed(rows):
    count = lax.axis_size(AXES)
    total, width = rows.shape
    share = -(-total // (16 * count)) * 16
    rows = jnp.pad(rows.astype(BF), ((0, share * count - total), (0, 0)))
    parts = exchange(rows.reshape(count, share, width), AXES)
    mine = jnp.sum(parts.astype(F32), 0).astype(BF)
    whole = exchange(jnp.broadcast_to(mine[None], (count, share, width)), AXES)
    return whole.reshape(count * share, width)[:total].astype(F32)


def per_device(
    columns,
    column_live,
    col_weight,
    col_slot,
    node_static,
    boundary_idx,
    edge_src,
    edge_dst,
    edge_live,
    edge_weight,
    enc_in,
    enc_out,
    src_proj,
    dst_proj,
    msg_proj,
    node_cotangent,
):
    peers = lax.axis_size(AXES)
    cols, fin = columns.shape
    nodes, width = node_static.shape
    rim = boundary_idx.shape[0]
    bucket = cols // peers
    layers = src_proj.shape[0]
    edge_scale = (edge_weight * edge_live.astype(F32))[:, None]

    scale = col_weight * column_live.astype(F32)
    scale_hi = lax.reduce_precision(scale, 8, 7)
    scale_lo = scale - scale_hi
    extra = jnp.stack(
        [
            (col_slot // 256).astype(BF).reshape(peers, bucket),
            (col_slot % 256).astype(BF).reshape(peers, bucket),
            scale_hi.astype(BF).reshape(peers, bucket),
            scale_lo.astype(BF).reshape(peers, bucket),
        ],
        1,
    ).reshape(peers, 4 * bucket)
    extra_rows = -(-4 * bucket // fin)
    extra = jnp.pad(extra, ((0, 0), (0, extra_rows * fin - 4 * bucket)))
    packed = jnp.concatenate(
        [columns.reshape(peers, bucket, fin), extra.reshape(peers, extra_rows, fin)], 1
    )
    packed = exchange(packed, AXES)
    got = packed[:, :bucket].reshape(cols, fin)
    extra = packed[:, bucket:].reshape(peers, extra_rows * fin)[:, : 4 * bucket]
    extra = extra.reshape(peers, 4, bucket).astype(F32).transpose(1, 0, 2).reshape(4, cols)
    slot = (extra[0] * 256.0 + extra[1]).astype(jnp.int32)
    got_scale = (extra[2] + extra[3])[:, None]

    enc_pre = mm(got, enc_in)
    pooled_act = mm(picks_t(slot, nodes), (jax.nn.silu(enc_pre) * got_scale).astype(BF)).astype(BF)
    state = (node_static.astype(F32) + mm(pooled_act, enc_out)).astype(BF)

    stored = []
    for layer in range(layers):
        from_src = mm(state, src_proj[layer]).astype(BF)
        from_dst = mm(state, dst_proj[layer]).astype(BF)
        rim_rows = mm(picks(boundary_idx, nodes), from_src).astype(BF)
        rims = jnp.concatenate(
            [
                passed_along(rim_rows, "grid", 1),
                passed_along(rim_rows, "grid", -1),
                passed_along(rim_rows, "dom", 1),
                passed_along(rim_rows, "dom", -1),
            ],
            0,
        )
        pre = (
            mm(picks(edge_src, nodes), from_src)
            + mm(picks(edge_dst, nodes), from_dst)
            + mm(picks(edge_src, 4 * rim, nodes), rims)
        )
        act = (jax.nn.silu(pre) * edge_scale).astype(BF)
        node_act = mm(picks_t(edge_dst, nodes), act).astype(BF)
        stored.append((state, pre, node_act))
        state = (state.astype(F32) + mm(node_act, msg_proj[layer])).astype(BF)

    grad = node_cotangent.astype(F32)
    terms = [None] * layers
    for layer in reversed(range(layers)):
        own, pre, node_act = stored[layer]
        grad_bf = grad.astype(BF)
        msg_term = t_mm(node_act, grad_bf)
        grad_act = mm(picks(edge_dst, nodes), mm_t(grad_bf, msg_proj[layer]).astype(BF))
        grad_pre = (grad_act * edge_scale * silu_grad(pre)).astype(BF)
        rim_sends = mm(picks_t(edge_src, 4 * rim, nodes), grad_pre).astype(BF)
        rim_sends = rim_sends.reshape(4, rim, width)
        returned = (
            passed_along(rim_sends[0], "grid", -1).astype(F32)
            + passed_along(rim_sends[1], "grid", 1).astype(F32)
            + passed_along(rim_sends[2], "dom", -1).astype(F32)
            + passed_along(rim_sends[3], "dom", 1).astype(F32)
        ).astype(BF)
        grad_src = mm(picks_t(edge_src, nodes), grad_pre) + mm(picks_t(boundary_idx, nodes), returned)
        grad_src = grad_src.astype(BF)
        grad_dst = mm(picks_t(edge_dst, nodes), grad_pre).astype(BF)
        terms[layer] = (t_mm(own, grad_src), t_mm(own, grad_dst), msg_term)
        grad = grad + mm_t(grad_src, src_proj[layer]) + mm_t(grad_dst, dst_proj[layer])

    grad_bf = grad.astype(BF)
    out_term = t_mm(pooled_act, grad_bf)
    grad_hidden = mm(picks(slot, nodes), mm_t(grad_bf, enc_out).astype(BF))
    grad_enc_pre = (grad_hidden * got_scale * silu_grad(enc_pre)).astype(BF)
    in_term = t_mm(got, grad_enc_pre)
    flat = [in_term, out_term]
    for entry in range(3):
        flat += [terms[layer][entry] for layer in range(layers)]
    whole = summed(jnp.concatenate(flat, 0))
    fin_rows = fin
    hid = enc_out.shape[0]
    rest = whole[fin_rows + hid :].reshape(3, layers, width, width)
    return (state, whole[:fin_rows], whole[fin_rows : fin_rows + hid], rest[0], rest[1], rest[2])


def solution(mesh):
    rows = P(AXES, None)
    flat = P(AXES)
    placed = (rows, flat, flat, flat, rows, flat, flat, flat, flat, flat, P(), P(), P(), P(), P(), rows)
    return jax.shard_map(
        per_device,
        mesh=mesh,
        in_specs=placed,
        out_specs=(rows, P(), P(), P(), P(), P()),
        check_vma=False,
    )
```

```python
import functools

import jax
import jax.numpy as jnp
from jax import lax
from jax.experimental import pallas as pl
from jax.experimental.pallas import tpu as pltpu
from jax.sharding import PartitionSpec as P

AXES = ("grid", "dom")
BF = jnp.bfloat16
F32 = jnp.float32
LANES = 128
TILE = 256
CHUNK = 512


def mm(left_side, right_side):
    return jnp.dot(left_side, right_side, preferred_element_type=F32)


def mm_t(left_side, right_side):
    return lax.dot_general(
        left_side, right_side, (((1,), (1,)), ((), ())), preferred_element_type=F32
    )


def t_mm(left_side, right_side):
    return lax.dot_general(
        left_side, right_side, (((0,), (0,)), ((), ())), preferred_element_type=F32
    )


def put_picks(out_ref, start, indices, count):
    rows = lax.broadcasted_iota(jnp.int32, (TILE, indices.shape[1]), 0).astype(F32).astype(BF)
    for base in range(0, count, TILE):
        shifted = (indices - float(base)).astype(BF)
        block = jnp.where(rows == shifted, jnp.ones((), BF), jnp.zeros((), BF))
        out_ref[start + base : start + base + TILE, :] = block


def sigmoid(values):
    return 0.5 * jnp.tanh(0.5 * values) + 0.5


def call(body, outs, scratch, name):
    vmem = pl.BlockSpec(memory_space=pltpu.VMEM)

    def run(*args):
        return pl.pallas_call(
            body,
            out_shape=tuple(jax.ShapeDtypeStruct(shape, dtype) for shape, dtype in outs),
            in_specs=[vmem] * len(args),
            out_specs=tuple(vmem for _ in outs),
            scratch_shapes=scratch,
            name=name,
        )(*args)

    return run


def chunks(total, size, body):
    if total == size:
        body(0)
        return

    def step(i, carry):
        body(pl.multiple_of(i * size, size))
        return carry

    lax.fori_loop(0, total // size, step, 0)


def pack_body(bucket, cols_ref, slot_ref, live_ref, weight_ref, out_ref):
    peers = out_ref.shape[0]
    per_row = LANES // bucket
    slot = slot_ref[...].astype(F32)
    high = jnp.floor(slot * (1.0 / 256.0))
    low = slot - 256.0 * high
    scale = weight_ref[...] * live_ref[...].astype(F32)
    scale_high = scale.astype(BF)
    scale_low = (scale - scale_high.astype(F32)).astype(BF)
    fields = [high.astype(BF), low.astype(BF), scale_high, scale_low]
    for peer in range(peers):
        out_ref[peer, :bucket, :] = cols_ref[peer * bucket : (peer + 1) * bucket, :]
        row = peer // per_row
        extra = jnp.concatenate([field[row : row + 1, :] for field in fields], 0)
        out_ref[peer, bucket : bucket + 4, :] = extra


def node_tables(state, state_ref, table_ref, src_t, dst_t, rim_ref, rim_picks):
    nodes, width = state.shape
    state_ref[...] = state.astype(BF)
    held = state_ref[...]
    table_ref[:, :nodes] = mm_t(src_t, held).astype(BF)
    table_ref[:, nodes:] = mm_t(dst_t, held).astype(BF)
    rim_ref[...] = t_mm(rim_picks[...], held).astype(BF)


def encode_body(
    bucket,
    packed_ref,
    rows_ref,
    enc_in_t_ref,
    enc_out_ref,
    static_ref,
    src_t_ref,
    dst_t_ref,
    bound_ref,
    pooled_ref,
    slope_ref,
    state_ref,
    table_ref,
    rim_ref,
    picks_ref,
    rim_picks,
    acc_ref,
):
    nodes = static_ref.shape[0]
    cols = rows_ref.shape[1]
    chunk = picks_ref.shape[1]
    peers_step = chunk // bucket
    acc_ref[...] = jnp.zeros_like(acc_ref)

    def step(start):
        first = start // bucket
        got = packed_ref[pl.ds(first, peers_step), :bucket, :].reshape(chunk, packed_ref.shape[2])
        pre = mm_t(enc_in_t_ref[...], got)
        slot = rows_ref[0:1, pl.ds(start, chunk)]
        scale = rows_ref[1:2, pl.ds(start, chunk)]
        sig = sigmoid(pre)
        act = (pre * sig * scale).astype(BF)
        slope_ref[:, pl.ds(start, chunk)] = (sig * (1.0 + pre * (1.0 - sig)) * scale).astype(BF)
        put_picks(picks_ref, 0, slot, nodes)
        acc_ref[...] += mm_t(picks_ref[...], act)

    chunks(cols, chunk, step)
    pooled_ref[...] = acc_ref[...].astype(BF)
    put_picks(rim_picks, 0, bound_ref[0:1, :], nodes)
    state = static_ref[...].astype(F32) + mm(pooled_ref[...], enc_out_ref[...])
    node_tables(state, state_ref, table_ref, src_t_ref[...], dst_t_ref[...], rim_ref, rim_picks)


def fill_table(full_ref, table_ref, src_t_ref, rims, flags_ref):
    width, both = table_ref.shape
    nodes = both // 2
    rim = rims[0].shape[0]
    full_ref[:, :nodes] = table_ref[:, :nodes]
    for side, rim_rows in enumerate(rims):
        start = nodes + side * rim
        part = mm_t(src_t_ref[...], rim_rows[...]) * flags_ref[side]
        full_ref[:, start : start + rim] = part.astype(BF)
    full_ref[:, nodes + 4 * rim :] = table_ref[:, nodes:]


def fill_picks(picks_ref, rows_ref, start, nodes, rim):
    chunk = picks_ref.shape[1]
    put_picks(picks_ref, 0, rows_ref[0:1, pl.ds(start, chunk)], nodes + 4 * rim)
    put_picks(picks_ref, nodes + 4 * rim, rows_ref[1:2, pl.ds(start, chunk)], nodes)


def forward_body(
    flags_ref,
    table_ref,
    up_ref,
    down_ref,
    left_ref,
    right_ref,
    rows_ref,
    state_ref,
    src_t_ref,
    msg_ref,
    next_src_t_ref,
    next_dst_t_ref,
    bound_ref,
    slope_ref,
    act_ref,
    next_state_ref,
    next_table_ref,
    rim_ref,
    full_ref,
    picks_ref,
    rim_picks,
    acc_ref,
):
    nodes = state_ref.shape[0]
    rim = up_ref.shape[0]
    ext = nodes + 4 * rim
    edges = rows_ref.shape[1]
    chunk = picks_ref.shape[1]
    fill_table(full_ref, table_ref, src_t_ref, (up_ref, down_ref, left_ref, right_ref), flags_ref)
    acc_ref[...] = jnp.zeros_like(acc_ref)

    def step(start):
        fill_picks(picks_ref, rows_ref, start, nodes, rim)
        pre = mm(full_ref[...], picks_ref[...])
        scale = rows_ref[2:3, pl.ds(start, chunk)]
        sig = sigmoid(pre)
        act = (pre * sig * scale).astype(BF)
        slope_ref[:, pl.ds(start, chunk)] = (sig * (1.0 + pre * (1.0 - sig)) * scale).astype(BF)
        acc_ref[...] += mm_t(picks_ref[ext:, :], act)

    chunks(edges, chunk, step)
    act_ref[...] = acc_ref[...].astype(BF)
    put_picks(rim_picks, 0, bound_ref[0:1, :], nodes)
    state = state_ref[...].astype(F32) + mm(act_ref[...], msg_ref[...])
    node_tables(
        state, next_state_ref, next_table_ref, next_src_t_ref[...], next_dst_t_ref[...], rim_ref, rim_picks
    )


def turn_body(
    flags_ref,
    table_ref,
    up_ref,
    down_ref,
    left_ref,
    right_ref,
    rows_ref,
    src_t_ref,
    msg_ref,
    grad_ref,
    act_ref,
    own_ref,
    rims_ref,
    full_ref,
    picks_ref,
    acc_ref,
    edge_acc_ref,
):
    nodes = grad_ref.shape[0]
    rim = up_ref.shape[0]
    ext = nodes + 4 * rim
    edges = rows_ref.shape[1]
    chunk = picks_ref.shape[1]
    fill_table(full_ref, table_ref, src_t_ref, (up_ref, down_ref, left_ref, right_ref), flags_ref)
    acc_ref[...] = jnp.zeros_like(acc_ref)
    edge_acc_ref[...] = jnp.zeros_like(edge_acc_ref)
    back = mm_t(msg_ref[...], grad_ref[...]).astype(BF)

    def step(start):
        fill_picks(picks_ref, rows_ref, start, nodes, rim)
        pre = mm(full_ref[...], picks_ref[...])
        scale = rows_ref[2:3, pl.ds(start, chunk)]
        sig = sigmoid(pre)
        act = (pre * sig * scale).astype(BF)
        acc_ref[...] += mm_t(picks_ref[ext:, :], act)
        slope = sig * (1.0 + pre * (1.0 - sig)) * scale
        grad_pre = (mm(back, picks_ref[ext:, :]) * slope).astype(BF)
        edge_acc_ref[...] += mm_t(picks_ref[...], grad_pre)

    chunks(edges, chunk, step)
    act_ref[...] = acc_ref[...].astype(BF)
    put_sums(edge_acc_ref, own_ref, rims_ref, nodes, rim)


def put_sums(edge_acc_ref, own_ref, rims_ref, nodes, rim):
    ext = nodes + 4 * rim
    own_ref[:nodes, :] = edge_acc_ref[:nodes, :].astype(BF)
    own_ref[nodes:, :] = edge_acc_ref[ext:, :].astype(BF)
    for side in range(4):
        first = nodes + side * rim
        rims_ref[side] = edge_acc_ref[first : first + rim, :].astype(BF)


def returned_sum(flags_ref, returned):
    total = returned[0][...].astype(F32) * flags_ref[4]
    for side in range(1, 4):
        total += returned[side][...].astype(F32) * flags_ref[4 + side]
    return total.astype(BF)


def merged_grad(grad, flags_ref, returned, own_ref, bound_ref, src_ref, dst_ref, rim_picks):
    nodes = grad.shape[0]
    put_picks(rim_picks, 0, bound_ref[0:1, :], nodes)
    back = mm(rim_picks[...], returned_sum(flags_ref, returned))
    grad_src = (own_ref[:nodes, :].astype(F32) + back).astype(BF)
    return grad + mm_t(grad_src, src_ref[...]) + mm_t(own_ref[nodes:, :], dst_ref[...])


def backward_body(
    flags_ref,
    up_ref,
    down_ref,
    left_ref,
    right_ref,
    own_ref,
    bound_ref,
    src_ref,
    dst_ref,
    grad_ref,
    rows_ref,
    msg_ref,
    slope_ref,
    next_grad_ref,
    next_own_ref,
    rims_ref,
    picks_ref,
    rim_picks,
    edge_acc_ref,
):
    nodes = grad_ref.shape[0]
    rim = up_ref.shape[0]
    ext = nodes + 4 * rim
    edges = rows_ref.shape[1]
    chunk = picks_ref.shape[1]
    returned = (up_ref, down_ref, left_ref, right_ref)
    grad = merged_grad(
        grad_ref[...].astype(F32), flags_ref, returned, own_ref, bound_ref, src_ref, dst_ref, rim_picks
    )
    next_grad_ref[...] = grad
    back = mm_t(msg_ref[...], grad.astype(BF)).astype(BF)
    edge_acc_ref[...] = jnp.zeros_like(edge_acc_ref)

    def step(start):
        fill_picks(picks_ref, rows_ref, start, nodes, rim)
        slope = slope_ref[:, pl.ds(start, chunk)].astype(F32)
        grad_pre = (mm(back, picks_ref[ext:, :]) * slope).astype(BF)
        edge_acc_ref[...] += mm_t(picks_ref[...], grad_pre)

    chunks(edges, chunk, step)
    put_sums(edge_acc_ref, next_own_ref, rims_ref, nodes, rim)


def terms_body(
    flags_ref, up_ref, down_ref, left_ref, right_ref, state_ref, own_ref, rims_ref, act_ref, grad_ref, out_ref
):
    nodes, width = state_ref.shape
    state = state_ref[...]
    src_term = t_mm(state, own_ref[:nodes, :])
    for side, rim_rows in enumerate((up_ref, down_ref, left_ref, right_ref)):
        src_term += t_mm(rim_rows[...], rims_ref[side]) * flags_ref[side]
    out_ref[:width, :] = src_term.astype(BF)
    out_ref[width : 2 * width, :] = t_mm(state, own_ref[nodes:, :]).astype(BF)
    out_ref[2 * width : 3 * width, :] = t_mm(act_ref[...], grad_ref[...].astype(BF)).astype(BF)
    if out_ref.shape[0] > 3 * width:
        out_ref[3 * width :, :] = jnp.zeros((out_ref.shape[0] - 3 * width, width), BF)


def last_body(
    bucket,
    flags_ref,
    up_ref,
    down_ref,
    left_ref,
    right_ref,
    own_ref,
    bound_ref,
    src_ref,
    dst_ref,
    grad_ref,
    rows_ref,
    packed_ref,
    enc_out_ref,
    pooled_ref,
    slope_ref,
    out_ref,
    picks_ref,
    rim_picks,
    acc_ref,
):
    nodes, width = grad_ref.shape
    cols = rows_ref.shape[1]
    chunk = picks_ref.shape[1]
    fin = packed_ref.shape[2]
    peers_step = chunk // bucket
    returned = (up_ref, down_ref, left_ref, right_ref)
    grad = merged_grad(
        grad_ref[...].astype(F32), flags_ref, returned, own_ref, bound_ref, src_ref, dst_ref, rim_picks
    ).astype(BF)
    back = mm_t(enc_out_ref[...], grad).astype(BF)
    acc_ref[...] = jnp.zeros_like(acc_ref)

    def step(start):
        first = start // bucket
        got = packed_ref[pl.ds(first, peers_step), :bucket, :].reshape(chunk, fin)
        put_picks(picks_ref, 0, rows_ref[0:1, pl.ds(start, chunk)], nodes)
        slope = slope_ref[:, pl.ds(start, chunk)].astype(F32)
        grad_pre = (mm(back, picks_ref[...]) * slope).astype(BF)
        acc_ref[...] += mm(grad_pre, got)

    chunks(cols, chunk, step)
    out_ref[:fin, :] = acc_ref[...].T.astype(BF)
    out_ref[fin : fin + width, :] = t_mm(pooled_ref[...], grad).astype(BF)
    if out_ref.shape[0] > fin + width:
        out_ref[fin + width :, :] = jnp.zeros((out_ref.shape[0] - fin - width, width), BF)


def state_body(state_ref, act_ref, msg_ref, out_ref):
    out_ref[...] = (state_ref[...].astype(F32) + mm(act_ref[...], msg_ref[...])).astype(BF)


def share_body(parts_ref, out_ref):
    count = parts_ref.shape[0]
    total = jnp.sum(parts_ref[...].astype(F32), 0).astype(BF)
    for peer in range(count):
        out_ref[peer] = total


def exchange(shard):
    return lax.all_to_all(shard, AXES, split_axis=0, concat_axis=0, tiled=True)


def rows_for(total, count):
    return -(-total // (8 * count)) * 8 * count


def summed(rows):
    count = lax.axis_size(AXES)
    total, width = rows.shape
    share = total // count
    parts = exchange(rows.reshape(count, share, width))
    (spread,) = call(share_body, [((count, share, width), BF)], [], "share")(parts)
    return exchange(spread).reshape(total, width)


def turned(shard, axis, by):
    count = lax.axis_size(axis)
    return lax.ppermute(shard, axis, [(i, (i + by) % count) for i in range(count)])


def from_neighbours(rim_rows):
    return (
        turned(rim_rows, "grid", 1),
        turned(rim_rows, "grid", -1),
        turned(rim_rows, "dom", 1),
        turned(rim_rows, "dom", -1),
    )


def to_neighbours(rims):
    return (
        turned(rims[0], "grid", -1),
        turned(rims[1], "grid", 1),
        turned(rims[2], "dom", -1),
        turned(rims[3], "dom", 1),
    )


def per_device(
    columns,
    column_live,
    col_weight,
    col_slot,
    node_static,
    boundary_idx,
    edge_src,
    edge_dst,
    edge_live,
    edge_weight,
    enc_in,
    enc_out,
    src_proj,
    dst_proj,
    msg_proj,
    node_cotangent,
):
    peers = lax.axis_size(AXES)
    cols, fin = columns.shape
    nodes, width = node_static.shape
    rim = boundary_idx.shape[0]
    edges = edge_src.shape[0]
    ext = nodes + 4 * rim
    bucket = cols // peers
    chunk = CHUNK

    lanes = (cols // LANES, LANES)
    (packed,) = call(
        functools.partial(pack_body, bucket), [((peers, bucket + 4, fin), BF)], [], "pack"
    )(columns, col_slot.reshape(lanes), column_live.reshape(lanes), col_weight.reshape(lanes))
    packed = exchange(packed)

    grid_at, grid_count = lax.axis_index("grid"), lax.axis_size("grid")
    dom_at, dom_count = lax.axis_index("dom"), lax.axis_size("dom")
    present = jnp.stack(
        [grid_at > 0, grid_at < grid_count - 1, dom_at > 0, dom_at < dom_count - 1]
    ).astype(F32)
    flags = jnp.concatenate([present, present[jnp.array([1, 0, 3, 2])]])
    edge_scale = edge_weight * edge_live.astype(F32)
    edge_rows = jnp.stack([edge_src.astype(F32), edge_dst.astype(F32), edge_scale])
    bound = boundary_idx.astype(F32)[None]
    enc_in_t = enc_in.T
    src_t = src_proj.transpose(0, 2, 1)
    dst_t = dst_proj.transpose(0, 2, 1)

    at = (grid_at * dom_count + dom_at) % (LANES // bucket)
    extra = lax.dynamic_slice_in_dim(packed[:, bucket : bucket + 4], at * bucket, bucket, 2)
    extra = extra.astype(F32).transpose(1, 0, 2).reshape(4, cols)
    col_rows = jnp.stack([extra[0] * 256.0 + extra[1], extra[2] + extra[3]])

    picks = pltpu.VMEM((ext + nodes, chunk), BF)
    slot_picks = pltpu.VMEM((nodes, chunk), BF)
    rim_picks = pltpu.VMEM((nodes, rim), BF)
    node_acc = pltpu.VMEM((nodes, width), F32)
    edge_acc = pltpu.VMEM((ext + nodes, width), F32)
    full = pltpu.VMEM((width, ext + nodes), BF)
    node_shape = ((nodes, width), BF)
    tables = [node_shape, ((width, 2 * nodes), BF), ((rim, width), BF)]
    slope_shape = ((width, edges), BF)
    sums = [((2 * nodes, width), BF), ((4, rim, width), BF)]
    smem = pl.BlockSpec(memory_space=pltpu.SMEM)

    def flagged(body, outs, scratch, name):
        vmem = pl.BlockSpec(memory_space=pltpu.VMEM)

        def run(*args):
            return pl.pallas_call(
                body,
                out_shape=tuple(jax.ShapeDtypeStruct(shape, dtype) for shape, dtype in outs),
                in_specs=[smem] + [vmem] * (len(args) - 1),
                out_specs=tuple(vmem for _ in outs),
                scratch_shapes=scratch,
                name=name,
            )(*args)

        return run

    pooled, col_slope, state0, table0, rim0 = call(
        functools.partial(encode_body, bucket),
        [node_shape, ((width, cols), BF)] + tables,
        [slot_picks, rim_picks, node_acc],
        "encode",
    )(packed, col_rows, enc_in_t, enc_out, node_static, src_t[0], dst_t[0], bound)

    rims0 = from_neighbours(rim0)
    slope0, act0, state1, table1, rim1 = flagged(
        forward_body, [slope_shape, node_shape] + tables, [full, picks, rim_picks, node_acc], "forward"
    )(flags, table0, *rims0, edge_rows, state0, src_t[0], msg_proj[0], src_t[1], dst_t[1], bound)

    rims1 = from_neighbours(rim1)
    act1, own1, sends1 = flagged(
        turn_body, [node_shape] + sums, [full, picks, node_acc, edge_acc], "turn"
    )(flags, table1, *rims1, edge_rows, src_t[1], msg_proj[1], node_cotangent)

    back1 = to_neighbours(sends1)
    (node_out,) = call(state_body, [node_shape], [], "state")(state1, act1, msg_proj[1])
    layer_rows = rows_for(3 * width, peers)
    (terms1,) = flagged(terms_body, [((layer_rows, width), BF)], [], "terms")(
        flags, *rims1, state1, own1, sends1, act1, node_cotangent
    )
    grad1, own0, sends0 = flagged(
        backward_body, [((nodes, width), F32)] + sums, [picks, rim_picks, edge_acc], "backward"
    )(flags, *back1, own1, bound, src_proj[1], dst_proj[1], node_cotangent, edge_rows, msg_proj[0], slope0)

    back0 = to_neighbours(sends0)
    (terms0,) = flagged(terms_body, [((layer_rows, width), BF)], [], "terms")(
        flags, *rims0, state0, own0, sends0, act0, grad1
    )
    enc_rows = rows_for(fin + enc_out.shape[0], peers)
    (terms_enc,) = flagged(
        functools.partial(last_body, bucket),
        [((enc_rows, width), BF)],
        [slot_picks, rim_picks, pltpu.VMEM((width, fin), F32)],
        "last",
    )(
        flags,
        *back0,
        own0,
        bound,
        src_proj[0],
        dst_proj[0],
        grad1,
        col_rows,
        packed,
        enc_out,
        pooled,
        col_slope,
    )

    whole1 = summed(terms1).astype(F32)
    whole0 = summed(terms0).astype(F32)
    whole_enc = summed(terms_enc).astype(F32)
    layers = [whole[: 3 * width].reshape(3, width, width) for whole in (whole0, whole1)]
    grads = [jnp.stack([layer[entry] for layer in layers], 0) for entry in range(3)]
    return (node_out, whole_enc[:fin], whole_enc[fin : fin + enc_out.shape[0]], grads[0], grads[1], grads[2])


def solution(mesh):
    rows = P(AXES, None)
    flat = P(AXES)
    placed = (rows, flat, flat, flat, rows, flat, flat, flat, flat, flat, P(), P(), P(), P(), P(), rows)
    return jax.shard_map(
        per_device,
        mesh=mesh,
        in_specs=placed,
        out_specs=(rows, P(), P(), P(), P(), P()),
        check_vma=False,
    )
```

```python
import functools

import jax
import jax.numpy as jnp
from jax import lax
from jax.experimental import pallas as pl
from jax.experimental.pallas import tpu as pltpu
from jax.sharding import PartitionSpec as P

AXES = ("grid", "dom")
BF = jnp.bfloat16
F32 = jnp.float32
LANES = 128
TILE = 256
CHUNK = 512
GRANT = 24 << 20


def mm(left_side, right_side):
    return jnp.dot(left_side, right_side, preferred_element_type=F32)


def mm_t(left_side, right_side):
    return lax.dot_general(
        left_side, right_side, (((1,), (1,)), ((), ())), preferred_element_type=F32
    )


def t_mm(left_side, right_side):
    return lax.dot_general(
        left_side, right_side, (((0,), (0,)), ((), ())), preferred_element_type=F32
    )


def put_picks(out_ref, start, indices, count):
    rows = lax.broadcasted_iota(jnp.int32, (TILE, indices.shape[1]), 0).astype(F32).astype(BF)
    for base in range(0, count, TILE):
        shifted = (indices - float(base)).astype(BF)
        block = jnp.where(rows == shifted, jnp.ones((), BF), jnp.zeros((), BF))
        out_ref[start + base : start + base + TILE, :] = block


def sigmoid(values):
    return 0.5 * jnp.tanh(0.5 * values) + 0.5


def call(body, outs, scratch, name, flagged=False):
    vmem = pl.BlockSpec(memory_space=pltpu.VMEM)
    first = pl.BlockSpec(memory_space=pltpu.SMEM) if flagged else vmem

    def run(*args):
        return pl.pallas_call(
            body,
            out_shape=tuple(jax.ShapeDtypeStruct(shape, dtype) for shape, dtype in outs),
            in_specs=[first] + [vmem] * (len(args) - 1),
            out_specs=tuple(vmem for _ in outs),
            scratch_shapes=scratch,
            compiler_params=pltpu.CompilerParams(vmem_limit_bytes=GRANT),
            name=name,
        )(*args)

    return run


def chunks(total, size, body):
    if total == size:
        body(0)
        return

    def step(i, carry):
        body(pl.multiple_of(i * size, size))
        return carry

    lax.fori_loop(0, total // size, step, 0)


def pack_body(bucket, cols_ref, slot_ref, live_ref, weight_ref, out_ref):
    peers = out_ref.shape[0]
    per_row = LANES // bucket
    slot = slot_ref[...].astype(F32)
    high = jnp.floor(slot * (1.0 / 256.0))
    low = slot - 256.0 * high
    scale = weight_ref[...] * live_ref[...].astype(F32)
    scale_high = scale.astype(BF)
    scale_low = (scale - scale_high.astype(F32)).astype(BF)
    fields = [high.astype(BF), low.astype(BF), scale_high, scale_low]
    for peer in range(peers):
        out_ref[peer, :bucket, :] = cols_ref[peer * bucket : (peer + 1) * bucket, :]
        row = peer // per_row
        extra = jnp.concatenate([field[row : row + 1, :] for field in fields], 0)
        out_ref[peer, bucket : bucket + 4, :] = extra


PAIR, ODD_GRID, ODD_DOM = 4, 6, 7


def put_tables(state, state_ref, table_ref, rim_ref, src_t_ref, dst_t_ref, bound_ref, rim_picks):
    nodes = state.shape[0]
    put_picks(rim_picks, 0, bound_ref[0:1, :], nodes)
    state_ref[...] = state.astype(BF)
    held = state_ref[...]
    rim_ref[...] = t_mm(rim_picks[...], held).astype(BF)
    table_ref[:, :nodes] = mm_t(src_t_ref[...], held).astype(BF)
    table_ref[:, nodes:] = mm_t(dst_t_ref[...], held).astype(BF)


def in_order(flags_ref, rims):
    first, second, left, right = (ref[...] for ref in rims)
    odd = flags_ref[ODD_GRID] > 0.5
    ordered = (jnp.where(odd, first, second), jnp.where(odd, second, first), left, right)
    return [rows * flags_ref[side].astype(BF) for side, rows in enumerate(ordered)]


def encode_body(
    bucket,
    packed_ref,
    rows_ref,
    enc_in_t_ref,
    enc_out_ref,
    static_ref,
    src_t_ref,
    dst_t_ref,
    bound_ref,
    pooled_ref,
    slope_ref,
    state_ref,
    table_ref,
    rim_ref,
    picks_ref,
    rim_picks,
    acc_ref,
):
    nodes = static_ref.shape[0]
    cols = rows_ref.shape[1]
    chunk = picks_ref.shape[1]
    peers_step = chunk // bucket
    acc_ref[...] = jnp.zeros_like(acc_ref)

    def step(start):
        first = start // bucket
        got = packed_ref[pl.ds(first, peers_step), :bucket, :].reshape(chunk, packed_ref.shape[2])
        pre = mm_t(enc_in_t_ref[...], got)
        slot = rows_ref[0:1, pl.ds(start, chunk)]
        scale = rows_ref[1:2, pl.ds(start, chunk)]
        sig = sigmoid(pre)
        act = (pre * sig * scale).astype(BF)
        slope_ref[:, pl.ds(start, chunk)] = (sig * (1.0 + pre * (1.0 - sig)) * scale).astype(BF)
        put_picks(picks_ref, 0, slot, nodes)
        acc_ref[...] += mm_t(picks_ref[...], act)

    chunks(cols, chunk, step)
    pooled_ref[...] = acc_ref[...].astype(BF)
    state = static_ref[...].astype(F32) + mm(pooled_ref[...], enc_out_ref[...])
    put_tables(state, state_ref, table_ref, rim_ref, src_t_ref, dst_t_ref, bound_ref, rim_picks)


def own_body(table_ref, rows_ref, out_ref, picks_ref):
    nodes = table_ref.shape[1] // 2
    chunk = picks_ref.shape[1]

    def step(start):
        put_picks(picks_ref, 0, rows_ref[0:1, pl.ds(start, chunk)], nodes)
        put_picks(picks_ref, nodes, rows_ref[1:2, pl.ds(start, chunk)], nodes)
        out_ref[:, pl.ds(start, chunk)] = mm(table_ref[...], picks_ref[...])

    chunks(rows_ref.shape[1], chunk, step)


def back_body(msg_ref, grad_ref, rows_ref, out_ref, picks_ref):
    nodes = grad_ref.shape[0]
    chunk = picks_ref.shape[1]
    back = mm_t(msg_ref[...], grad_ref[...]).astype(BF)

    def step(start):
        put_picks(picks_ref, 0, rows_ref[1:2, pl.ds(start, chunk)], nodes)
        out_ref[:, pl.ds(start, chunk)] = mm(back, picks_ref[...]) * rows_ref[2:3, pl.ds(start, chunk)]

    chunks(rows_ref.shape[1], chunk, step)


def fill_rims(full_ref, flags_ref, rims, src_t_ref):
    rim = rims[0].shape[0]
    for side, rim_rows in enumerate(in_order(flags_ref, rims)):
        full_ref[:, side * rim : (side + 1) * rim] = mm_t(src_t_ref[...], rim_rows).astype(BF)


def forward_body(
    flags_ref,
    first_ref,
    second_ref,
    left_ref,
    right_ref,
    own_pre_ref,
    rows_ref,
    state_ref,
    src_t_ref,
    msg_ref,
    next_src_t_ref,
    next_dst_t_ref,
    bound_ref,
    slope_ref,
    act_ref,
    next_state_ref,
    next_table_ref,
    rim_ref,
    full_ref,
    picks_ref,
    rim_picks,
    acc_ref,
):
    nodes = state_ref.shape[0]
    ext = full_ref.shape[1]
    chunk = picks_ref.shape[1]
    fill_rims(full_ref, flags_ref, (first_ref, second_ref, left_ref, right_ref), src_t_ref)
    acc_ref[...] = jnp.zeros_like(acc_ref)

    def step(start):
        put_picks(picks_ref, 0, rows_ref[0:1, pl.ds(start, chunk)] - float(nodes), ext)
        put_picks(picks_ref, ext, rows_ref[1:2, pl.ds(start, chunk)], nodes)
        pre = own_pre_ref[:, pl.ds(start, chunk)] + mm(full_ref[...], picks_ref[:ext, :])
        scale = rows_ref[2:3, pl.ds(start, chunk)]
        sig = sigmoid(pre)
        act = (pre * sig * scale).astype(BF)
        slope_ref[:, pl.ds(start, chunk)] = (sig * (1.0 + pre * (1.0 - sig)) * scale).astype(BF)
        acc_ref[...] += mm_t(picks_ref[ext:, :], act)

    chunks(rows_ref.shape[1], chunk, step)
    act_ref[...] = acc_ref[...].astype(BF)
    state = state_ref[...].astype(F32) + mm(act_ref[...], msg_ref[...])
    put_tables(
        state, next_state_ref, next_table_ref, rim_ref, next_src_t_ref, next_dst_t_ref, bound_ref, rim_picks
    )


def put_sends(flags_ref, acc_ref, sends):
    rim = acc_ref.shape[0] // 4
    up, down, left, right = (acc_ref[side * rim : (side + 1) * rim, :].astype(BF) for side in range(4))
    odd = flags_ref[ODD_GRID] > 0.5
    sends[0][...] = jnp.where(odd, up, down)
    sends[1][...] = jnp.where(odd, down, up)
    sends[2][...] = left
    sends[3][...] = right


def turn_body(
    flags_ref,
    first_ref,
    second_ref,
    left_ref,
    right_ref,
    own_pre_ref,
    back_ref,
    rows_ref,
    src_t_ref,
    act_ref,
    grad_pre_ref,
    send0_ref,
    send1_ref,
    send2_ref,
    send3_ref,
    full_ref,
    picks_ref,
    acc_ref,
    node_count=0,
):
    ext = full_ref.shape[1]
    chunk = picks_ref.shape[1]
    fill_rims(full_ref, flags_ref, (first_ref, second_ref, left_ref, right_ref), src_t_ref)
    acc_ref[...] = jnp.zeros_like(acc_ref)

    def step(start):
        at = pl.ds(start, chunk)
        put_picks(picks_ref, 0, rows_ref[0:1, at] - float(node_count), ext)
        pre = own_pre_ref[:, at] + mm(full_ref[...], picks_ref[...])
        sig = sigmoid(pre)
        act_ref[:, at] = (pre * sig * rows_ref[2:3, at]).astype(BF)
        grad_pre = (back_ref[:, at] * (sig * (1.0 + pre * (1.0 - sig)))).astype(BF)
        grad_pre_ref[:, at] = grad_pre
        acc_ref[...] += mm_t(picks_ref[...], grad_pre)

    chunks(rows_ref.shape[1], chunk, step)
    put_sends(flags_ref, acc_ref, (send0_ref, send1_ref, send2_ref, send3_ref))


def merged_grad(grad, flags_ref, returned, own_ref, bound_ref, src_ref, dst_ref, rim_picks):
    nodes = grad.shape[0]
    put_picks(rim_picks, 0, bound_ref[0:1, :], nodes)
    marks = (flags_ref[PAIR], flags_ref[PAIR + 1], flags_ref[3], flags_ref[2])
    total = returned[0][...].astype(F32) * marks[0]
    for side in range(1, 4):
        total += returned[side][...].astype(F32) * marks[side]
    back = mm(rim_picks[...], total.astype(BF))
    grad_src = (own_ref[:nodes, :].astype(F32) + back).astype(BF)
    return grad + mm_t(grad_src, src_ref[...]) + mm_t(own_ref[nodes:, :], dst_ref[...])


def backward_body(
    flags_ref,
    first_ref,
    second_ref,
    left_ref,
    right_ref,
    own_ref,
    bound_ref,
    src_ref,
    dst_ref,
    grad_ref,
    rows_ref,
    msg_ref,
    slope_ref,
    next_grad_ref,
    grad_pre_ref,
    send0_ref,
    send1_ref,
    send2_ref,
    send3_ref,
    picks_ref,
    rim_picks,
    acc_ref,
):
    nodes = grad_ref.shape[0]
    ext = acc_ref.shape[0]
    chunk = picks_ref.shape[1]
    returned = (first_ref, second_ref, left_ref, right_ref)
    grad = merged_grad(
        grad_ref[...].astype(F32), flags_ref, returned, own_ref, bound_ref, src_ref, dst_ref, rim_picks
    )
    next_grad_ref[...] = grad
    back = mm_t(msg_ref[...], grad.astype(BF)).astype(BF)
    acc_ref[...] = jnp.zeros_like(acc_ref)

    def step(start):
        at = pl.ds(start, chunk)
        put_picks(picks_ref, 0, rows_ref[0:1, at] - float(nodes), ext)
        put_picks(picks_ref, ext, rows_ref[1:2, at], nodes)
        grad_pre = (mm(back, picks_ref[ext:, :]) * slope_ref[:, at].astype(F32)).astype(BF)
        grad_pre_ref[:, at] = grad_pre
        acc_ref[...] += mm_t(picks_ref[:ext, :], grad_pre)

    chunks(rows_ref.shape[1], chunk, step)
    put_sends(flags_ref, acc_ref, (send0_ref, send1_ref, send2_ref, send3_ref))


def sums_body(rows_ref, grad_pre_ref, own_ref, picks_ref, acc_ref):
    nodes = own_ref.shape[0] // 2
    chunk = picks_ref.shape[1]
    acc_ref[...] = jnp.zeros_like(acc_ref)

    def step(start):
        at = pl.ds(start, chunk)
        put_picks(picks_ref, 0, rows_ref[0:1, at], nodes)
        put_picks(picks_ref, nodes, rows_ref[1:2, at], nodes)
        acc_ref[...] += mm_t(picks_ref[...], grad_pre_ref[:, at])

    chunks(rows_ref.shape[1], chunk, step)
    own_ref[...] = acc_ref[...].astype(BF)


def out_body(rows_ref, act_edges_ref, state_ref, msg_ref, act_ref, out_ref, picks_ref, acc_ref):
    nodes = state_ref.shape[0]
    chunk = picks_ref.shape[1]
    acc_ref[...] = jnp.zeros_like(acc_ref)

    def step(start):
        at = pl.ds(start, chunk)
        put_picks(picks_ref, 0, rows_ref[1:2, at], nodes)
        acc_ref[...] += mm_t(picks_ref[...], act_edges_ref[:, at])

    chunks(rows_ref.shape[1], chunk, step)
    act_ref[...] = acc_ref[...].astype(BF)
    out_ref[...] = (state_ref[...].astype(F32) + mm(act_ref[...], msg_ref[...])).astype(BF)


def put_halves(flags_ref, first, term, keep_ref, send_ref):
    half = term.shape[1] // 2
    odd = flags_ref[ODD_DOM] > 0.5
    low, high = term[:, :half].astype(BF), term[:, half:].astype(BF)
    keep_ref[first : first + term.shape[0], :] = jnp.where(odd, high, low)
    send_ref[first : first + term.shape[0], :] = jnp.where(odd, low, high)


def terms_body(
    flags_ref,
    first_ref,
    second_ref,
    left_ref,
    right_ref,
    send0_ref,
    send1_ref,
    send2_ref,
    send3_ref,
    state_ref,
    own_ref,
    act_ref,
    grad_ref,
    keep_ref,
    send_ref,
):
    nodes, width = state_ref.shape
    state = state_ref[...]
    src_term = t_mm(state, own_ref[:nodes, :])
    pairs = (
        (first_ref, send0_ref, flags_ref[PAIR]),
        (second_ref, send1_ref, flags_ref[PAIR + 1]),
        (left_ref, send2_ref, flags_ref[2]),
        (right_ref, send3_ref, flags_ref[3]),
    )
    for rim_ref, sums_ref, mark in pairs:
        src_term += t_mm(rim_ref[...], sums_ref[...]) * mark
    put_halves(flags_ref, 0, src_term, keep_ref, send_ref)
    put_halves(flags_ref, width, t_mm(state, own_ref[nodes:, :]), keep_ref, send_ref)
    put_halves(
        flags_ref, 2 * width, t_mm(act_ref[...], grad_ref[...].astype(BF)), keep_ref, send_ref
    )


def last_body(
    bucket,
    flags_ref,
    first_ref,
    second_ref,
    left_ref,
    right_ref,
    own_ref,
    bound_ref,
    src_ref,
    dst_ref,
    grad_ref,
    rows_ref,
    packed_ref,
    enc_out_ref,
    pooled_ref,
    slope_ref,
    keep_ref,
    send_ref,
    picks_ref,
    rim_picks,
    acc_ref,
):
    nodes = grad_ref.shape[0]
    cols = rows_ref.shape[1]
    chunk = picks_ref.shape[1]
    fin = packed_ref.shape[2]
    peers_step = chunk // bucket
    returned = (first_ref, second_ref, left_ref, right_ref)
    grad = merged_grad(
        grad_ref[...], flags_ref, returned, own_ref, bound_ref, src_ref, dst_ref, rim_picks
    ).astype(BF)
    back = mm_t(enc_out_ref[...], grad).astype(BF)
    acc_ref[...] = jnp.zeros_like(acc_ref)

    def step(start):
        first = start // bucket
        got = packed_ref[pl.ds(first, peers_step), :bucket, :].reshape(chunk, fin)
        put_picks(picks_ref, 0, rows_ref[0:1, pl.ds(start, chunk)], nodes)
        slope = slope_ref[:, pl.ds(start, chunk)].astype(F32)
        grad_pre = (mm(back, picks_ref[...]) * slope).astype(BF)
        acc_ref[...] += mm(grad_pre, got)

    chunks(cols, chunk, step)
    put_halves(flags_ref, 0, acc_ref[...].T, keep_ref, send_ref)
    put_halves(flags_ref, fin, t_mm(pooled_ref[...], grad), keep_ref, send_ref)


def merge_body(*refs):
    out_ref = refs[-1]
    first = 0
    for keep_ref, got_ref in zip(refs[:-1:2], refs[1:-1:2]):
        rows = keep_ref.shape[0]
        total = keep_ref[...].astype(F32) + got_ref[...].astype(F32)
        out_ref[first : first + rows, :] = total.astype(BF)
        first += rows
    if first < out_ref.shape[0]:
        out_ref[first:, :] = jnp.zeros((out_ref.shape[0] - first, out_ref.shape[1]), BF)


def share_body(parts_ref, out_ref):
    count = parts_ref.shape[0]
    for odd in range(2):
        total = parts_ref[odd].astype(F32)
        for peer in range(odd + 2, count, 2):
            total += parts_ref[peer].astype(F32)
        for peer in range(odd, count, 2):
            out_ref[peer] = total.astype(BF)


def unpack_body(flags_ref, mine_ref, other_ref, *outs):
    odd = flags_ref[ODD_DOM] > 0.5
    half = mine_ref.shape[1]
    first = 0

    def put(ref, rows):
        nonlocal first
        mine = mine_ref[first : first + rows, :].astype(F32)
        other = other_ref[first : first + rows, :].astype(F32)
        ref[:, :half] = jnp.where(odd, other, mine)
        ref[:, half:] = jnp.where(odd, mine, other)
        first += rows

    enc_in_ref, enc_out_ref, *layer_refs = outs
    for layer in reversed(range(layer_refs[0].shape[0])):
        for ref in layer_refs:
            put(ref.at[layer], ref.shape[1])
    put(enc_in_ref, enc_in_ref.shape[0])
    put(enc_out_ref, enc_out_ref.shape[0])


def exchange(shard):
    return lax.all_to_all(shard, AXES, split_axis=0, concat_axis=0, tiled=True)


def turned(shard, axis, by):
    count = lax.axis_size(axis)
    return lax.ppermute(shard, axis, [(i, (i + by) % count) for i in range(count)])


def swapped(shard, axis, offset):
    count = lax.axis_size(axis)
    partner = list(range(count))
    for i in range(offset, count - 1, 2):
        partner[i], partner[i + 1] = i + 1, i
    return lax.ppermute(shard, axis, list(enumerate(partner)))


def from_neighbours(rim_rows):
    return (
        swapped(rim_rows, "grid", 0),
        swapped(rim_rows, "grid", 1),
        turned(rim_rows, "dom", 1),
        turned(rim_rows, "dom", -1),
    )


def to_neighbours(sends):
    return (
        swapped(sends[0], "grid", 0),
        swapped(sends[1], "grid", 1),
        turned(sends[2], "dom", -1),
        turned(sends[3], "dom", 1),
    )


def per_device(
    columns,
    column_live,
    col_weight,
    col_slot,
    node_static,
    boundary_idx,
    edge_src,
    edge_dst,
    edge_live,
    edge_weight,
    enc_in,
    enc_out,
    src_proj,
    dst_proj,
    msg_proj,
    node_cotangent,
):
    peers = lax.axis_size(AXES)
    cols, fin = columns.shape
    nodes, width = node_static.shape
    rim = boundary_idx.shape[0]
    edges = edge_src.shape[0]
    ext = 4 * rim
    bucket = cols // peers
    chunk = CHUNK

    lanes = (cols // LANES, LANES)
    (packed,) = call(
        functools.partial(pack_body, bucket), [((peers, bucket + 4, fin), BF)], [], "pack"
    )(columns, col_slot.reshape(lanes), column_live.reshape(lanes), col_weight.reshape(lanes))
    packed = exchange(packed)

    grid_at, grid_count = lax.axis_index("grid"), lax.axis_size("grid")
    dom_at, dom_count = lax.axis_index("dom"), lax.axis_size("dom")
    odd_grid, odd_dom = grid_at % 2, dom_at % 2
    up, down = grid_at > 0, grid_at < grid_count - 1
    flags = jnp.stack(
        [
            up,
            down,
            dom_at > 0,
            dom_at < dom_count - 1,
            jnp.where(odd_grid == 1, up, down),
            jnp.where(odd_grid == 1, down, up),
            odd_grid == 1,
            odd_dom == 1,
        ]
    ).astype(F32)
    edge_scale = edge_weight * edge_live.astype(F32)
    edge_rows = jnp.stack([edge_src.astype(F32), edge_dst.astype(F32), edge_scale])
    bound = boundary_idx.astype(F32)[None]
    enc_in_t = enc_in.T
    src_t = src_proj.transpose(0, 2, 1)
    dst_t = dst_proj.transpose(0, 2, 1)

    node_picks = pltpu.VMEM((nodes, chunk), BF)
    own_picks = pltpu.VMEM((2 * nodes, chunk), BF)
    ext_picks = pltpu.VMEM((ext, chunk), BF)
    all_picks = pltpu.VMEM((ext + nodes, chunk), BF)
    rim_picks = pltpu.VMEM((nodes, rim), BF)
    node_acc = pltpu.VMEM((nodes, width), F32)
    own_acc = pltpu.VMEM((2 * nodes, width), F32)
    ext_acc = pltpu.VMEM((ext, width), F32)
    full = pltpu.VMEM((width, ext), BF)
    node_shape = ((nodes, width), BF)
    rim_shape = ((rim, width), BF)
    tables = [node_shape, ((width, 2 * nodes), BF), rim_shape]
    edge_shape = ((width, edges), BF)
    edge_wide = ((width, edges), F32)

    (back1,) = call(back_body, [edge_wide], [node_picks], "back")(
        msg_proj[1], node_cotangent, edge_rows
    )

    at = (grid_at * dom_count + dom_at) % (LANES // bucket)
    extra = lax.dynamic_slice_in_dim(packed[:, bucket : bucket + 4], at * bucket, bucket, 2)
    extra = extra.astype(F32).transpose(1, 0, 2).reshape(4, cols)
    col_rows = jnp.stack([extra[0] * 256.0 + extra[1], extra[2] + extra[3]])

    pooled, col_slope, state0, table0, rim0 = call(
        functools.partial(encode_body, bucket),
        [node_shape, ((width, cols), BF)] + tables,
        [node_picks, rim_picks, node_acc],
        "encode",
    )(packed, col_rows, enc_in_t, enc_out, node_static, src_t[0], dst_t[0], bound)

    rims0 = from_neighbours(rim0)
    (pre0,) = call(own_body, [edge_wide], [own_picks], "own")(table0, edge_rows)
    slope0, act0, state1, table1, rim1 = call(
        forward_body,
        [edge_shape, node_shape] + tables,
        [full, all_picks, rim_picks, node_acc],
        "forward",
        True,
    )(flags, *rims0, pre0, edge_rows, state0, src_t[0], msg_proj[0], src_t[1], dst_t[1], bound)

    rims1 = from_neighbours(rim1)
    (pre1,) = call(own_body, [edge_wide], [own_picks], "own")(table1, edge_rows)
    act_edges1, grad_pre1, *sends1 = call(
        functools.partial(turn_body, node_count=nodes),
        [edge_shape, edge_shape] + [rim_shape] * 4,
        [full, ext_picks, ext_acc],
        "turn",
        True,
    )(flags, *rims1, pre1, back1, edge_rows, src_t[1])

    returned1 = to_neighbours(sends1)
    own_shape = ((2 * nodes, width), BF)
    halves = [((3 * width, width // 2), BF)] * 2
    (own1,) = call(sums_body, [own_shape], [own_picks, own_acc], "sums")(edge_rows, grad_pre1)
    act1, node_out = call(out_body, [node_shape, node_shape], [node_picks, node_acc], "out")(
        edge_rows, act_edges1, state1, msg_proj[1]
    )
    keep1, send1 = call(terms_body, halves, [], "terms", True)(
        flags, *rims1, *sends1, state1, own1, act1, node_cotangent
    )
    grad1, grad_pre0, *sends0 = call(
        backward_body,
        [((nodes, width), F32), edge_shape] + [rim_shape] * 4,
        [all_picks, rim_picks, ext_acc],
        "backward",
        True,
    )(
        flags,
        *returned1,
        own1,
        bound,
        src_proj[1],
        dst_proj[1],
        node_cotangent,
        edge_rows,
        msg_proj[0],
        slope0,
    )

    returned0 = to_neighbours(sends0)
    (own0,) = call(sums_body, [own_shape], [own_picks, own_acc], "sums")(edge_rows, grad_pre0)
    keep0, send0 = call(terms_body, halves, [], "terms", True)(
        flags, *rims0, *sends0, state0, own0, act0, grad1
    )
    hidden = enc_out.shape[0]
    keep_enc, send_enc = call(
        functools.partial(last_body, bucket),
        [((fin + hidden, width // 2), BF)] * 2,
        [node_picks, rim_picks, pltpu.VMEM((width, fin), F32)],
        "last",
        True,
    )(
        flags,
        *returned0,
        own0,
        bound,
        src_proj[0],
        dst_proj[0],
        grad1,
        col_rows,
        packed,
        enc_out,
        pooled,
        col_slope,
    )

    total_rows = 2 * 3 * width + fin + hidden
    share = -(-total_rows // (16 * peers)) * 16
    rows = peers * share
    (merged,) = call(merge_body, [((rows, width // 2), BF)], [], "merge")(
        keep1,
        swapped(send1, "dom", 0),
        keep0,
        swapped(send0, "dom", 0),
        keep_enc,
        swapped(send_enc, "dom", 0),
    )
    parts = exchange(merged.reshape(peers, share, width // 2))
    (spread,) = call(share_body, [((peers, share, width // 2), BF)], [], "share")(parts)
    mine = exchange(spread).reshape(rows, width // 2)
    layer_shape = ((2, width, width), F32)
    grads = call(
        unpack_body,
        [((fin, width), F32), ((hidden, width), F32), layer_shape, layer_shape, layer_shape],
        [],
        "unpack",
        True,
    )(flags, mine, swapped(mine, "dom", 0))
    return (node_out, *grads)


def solution(mesh):
    rows = P(AXES, None)
    flat = P(AXES)
    placed = (rows, flat, flat, flat, rows, flat, flat, flat, flat, flat, P(), P(), P(), P(), P(), rows)
    return jax.shard_map(
        per_device,
        mesh=mesh,
        in_specs=placed,
        out_specs=(rows, P(), P(), P(), P(), P()),
        check_vma=False,
    )
```

```python
import functools

import jax
import jax.numpy as jnp
from jax import lax
from jax.experimental import pallas as pl
from jax.experimental.pallas import tpu as pltpu
from jax.sharding import PartitionSpec as P

AXES = ("grid", "dom")
BF = jnp.bfloat16
F32 = jnp.float32
LANES = 128
TILE = 256
CHUNK = 512
GRANT = 20 << 20


def mm(left_side, right_side):
    return jnp.dot(left_side, right_side, preferred_element_type=F32)


def mm_t(left_side, right_side):
    return lax.dot_general(
        left_side, right_side, (((1,), (1,)), ((), ())), preferred_element_type=F32
    )


def t_mm(left_side, right_side):
    return lax.dot_general(
        left_side, right_side, (((0,), (0,)), ((), ())), preferred_element_type=F32
    )


def put_picks(out_ref, start, indices, count):
    rows = lax.broadcasted_iota(jnp.int32, (TILE, indices.shape[1]), 0).astype(F32).astype(BF)
    for base in range(0, count, TILE):
        shifted = (indices - float(base)).astype(BF)
        block = jnp.where(rows == shifted, jnp.ones((), BF), jnp.zeros((), BF))
        out_ref[start + base : start + base + TILE, :] = block


def sigmoid(values):
    return 0.5 * jnp.tanh(0.5 * values) + 0.5


def call(body, outs, scratch, name, flagged=False, space=pltpu.VMEM):
    vmem = pl.BlockSpec(memory_space=pltpu.VMEM)
    operand = pl.BlockSpec(memory_space=space)
    first = pl.BlockSpec(memory_space=pltpu.SMEM) if flagged else operand

    def run(*args):
        return pl.pallas_call(
            body,
            out_shape=tuple(jax.ShapeDtypeStruct(shape, dtype) for shape, dtype in outs),
            in_specs=[first] + [operand] * (len(args) - 1),
            out_specs=tuple(vmem for _ in outs),
            scratch_shapes=scratch,
            compiler_params=pltpu.CompilerParams(vmem_limit_bytes=GRANT),
            name=name,
        )(*args)

    return run


def chunks(total, body):
    for start in range(0, total, CHUNK):
        body(start, pl.ds(start, CHUNK))


def pack_body(cols_ref, slot_ref, live_ref, weight_ref, out_ref, slot_buf, live_buf, weight_buf, sems):
    peers, bucket, _ = cols_ref.shape
    per_row = LANES // bucket
    copies = [
        pltpu.make_async_copy(cols_ref, out_ref.at[:, :bucket, :], sems.at[0]),
        pltpu.make_async_copy(slot_ref, slot_buf, sems.at[1]),
        pltpu.make_async_copy(live_ref, live_buf, sems.at[2]),
        pltpu.make_async_copy(weight_ref, weight_buf, sems.at[3]),
    ]
    for copy in copies:
        copy.start()
    for copy in copies[1:]:
        copy.wait()
    slot = slot_buf[...].astype(F32)
    high = jnp.floor(slot * (1.0 / 256.0))
    low = slot - 256.0 * high
    scale = weight_buf[...] * live_buf[...].astype(F32)
    scale_high = scale.astype(BF)
    scale_low = (scale - scale_high.astype(F32)).astype(BF)
    fields = [high.astype(BF), low.astype(BF), scale_high, scale_low]
    for peer in range(peers):
        row = peer // per_row
        extra = jnp.concatenate([field[row : row + 1, :] for field in fields], 0)
        out_ref[peer, bucket : bucket + 4, :] = extra
    copies[0].wait()


PAIR, ODD_GRID, ODD_DOM = 4, 6, 7


def picks_body(rows_ref, bound_ref, picks_ref, rim_picks, rim_picks_t):
    nodes = rim_picks.shape[0]
    ext = picks_ref.shape[0] - 2 * nodes
    for start in range(0, rows_ref.shape[1], CHUNK):
        at = pl.ds(start, CHUNK)
        block = picks_ref.at[:, at]
        put_picks(block, 0, rows_ref[1:2, at], nodes)
        put_picks(block, nodes, rows_ref[0:1, at], nodes + ext)
    put_picks(rim_picks, 0, bound_ref[0:1, :], nodes)
    rim_picks_t[...] = rim_picks[...].astype(F32).T.astype(BF)


def put_state(state, state_ref, rim_ref, rim_picks_t):
    state_ref[...] = state.astype(BF)
    rim_ref[...] = mm(rim_picks_t[...], state_ref[...]).astype(BF)


def in_order(flags_ref, rims):
    first, second, left, right = (ref[...] for ref in rims)
    odd = flags_ref[ODD_GRID] > 0.5
    ordered = (jnp.where(odd, first, second), jnp.where(odd, second, first), left, right)
    return [rows * flags_ref[side].astype(BF) for side, rows in enumerate(ordered)]


def encode_body(
    bucket,
    packed_ref,
    rows_ref,
    enc_in_t_ref,
    enc_out_ref,
    static_ref,
    rim_picks_t,
    pooled_ref,
    slope_ref,
    picks_ref,
    state_ref,
    rim_ref,
    act_ref,
):
    nodes = static_ref.shape[0]
    peers_step = CHUNK // bucket

    def step(start, at):
        first = start // bucket
        got = packed_ref[first : first + peers_step, :bucket, :].reshape(CHUNK, packed_ref.shape[2])
        pre = mm_t(enc_in_t_ref[...], got)
        scale = rows_ref[1:2, at]
        sig = sigmoid(pre)
        act_ref[:, at] = (pre * sig * scale).astype(BF)
        slope_ref[:, at] = (sig * (1.0 + pre * (1.0 - sig)) * scale).astype(BF)
        put_picks(picks_ref.at[:, at], 0, rows_ref[0:1, at], nodes)

    chunks(rows_ref.shape[1], step)
    pooled_ref[...] = mm_t(picks_ref[...], act_ref[...]).astype(BF)
    state = static_ref[...].astype(F32) + mm(pooled_ref[...], enc_out_ref[...])
    put_state(state, state_ref, rim_ref, rim_picks_t)


def own_body(state_ref, src_t_ref, dst_t_ref, picks_ref, out_ref, table_ref):
    nodes = state_ref.shape[0]
    held = state_ref[...]
    table_ref[:, :nodes] = mm_t(dst_t_ref[...], held).astype(BF)
    table_ref[:, nodes:] = mm_t(src_t_ref[...], held).astype(BF)
    out_ref[...] = mm(table_ref[...], picks_ref[: 2 * nodes, :])


def back_body(msg_ref, grad_ref, rows_ref, picks_ref, out_ref):
    nodes = grad_ref.shape[0]
    back = mm_t(msg_ref[...], grad_ref[...]).astype(BF)
    out_ref[...] = mm(back, picks_ref[:nodes, :]) * rows_ref[2:3, :]


def fill_rims(full_ref, flags_ref, rims, src_t_ref):
    rim = rims[0].shape[0]
    for side, rim_rows in enumerate(in_order(flags_ref, rims)):
        full_ref[:, side * rim : (side + 1) * rim] = mm_t(src_t_ref[...], rim_rows).astype(BF)


def forward_body(
    flags_ref,
    first_ref,
    second_ref,
    left_ref,
    right_ref,
    own_pre_ref,
    rows_ref,
    picks_ref,
    state_ref,
    src_t_ref,
    msg_ref,
    rim_picks_t,
    slope_ref,
    node_act_ref,
    next_state_ref,
    rim_ref,
    full_ref,
    act_ref,
):
    nodes = state_ref.shape[0]
    fill_rims(full_ref, flags_ref, (first_ref, second_ref, left_ref, right_ref), src_t_ref)

    def step(start, at):
        pre = own_pre_ref[:, at] + mm(full_ref[...], picks_ref[2 * nodes :, at])
        scale = rows_ref[2:3, at]
        sig = sigmoid(pre)
        act_ref[:, at] = (pre * sig * scale).astype(BF)
        slope_ref[:, at] = (sig * (1.0 + pre * (1.0 - sig)) * scale).astype(BF)

    chunks(rows_ref.shape[1], step)
    node_act_ref[...] = mm_t(picks_ref[:nodes, :], act_ref[...]).astype(BF)
    state = state_ref[...].astype(F32) + mm(node_act_ref[...], msg_ref[...])
    put_state(state, next_state_ref, rim_ref, rim_picks_t)


def put_sends(flags_ref, sums, sends):
    rim = sums.shape[0] // 4
    up, down, left, right = (sums[side * rim : (side + 1) * rim, :].astype(BF) for side in range(4))
    odd = flags_ref[ODD_GRID] > 0.5
    sends[0][...] = jnp.where(odd, up, down)
    sends[1][...] = jnp.where(odd, down, up)
    sends[2][...] = left
    sends[3][...] = right


def turn_body(
    flags_ref,
    first_ref,
    second_ref,
    left_ref,
    right_ref,
    own_pre_ref,
    back_ref,
    rows_ref,
    picks_ref,
    src_t_ref,
    act_ref,
    grad_pre_ref,
    send0_ref,
    send1_ref,
    send2_ref,
    send3_ref,
    full_ref,
):
    first = picks_ref.shape[0] - full_ref.shape[1]
    fill_rims(full_ref, flags_ref, (first_ref, second_ref, left_ref, right_ref), src_t_ref)

    def step(start, at):
        pre = own_pre_ref[:, at] + mm(full_ref[...], picks_ref[first:, at])
        sig = sigmoid(pre)
        act_ref[:, at] = (pre * sig * rows_ref[2:3, at]).astype(BF)
        grad_pre_ref[:, at] = (back_ref[:, at] * (sig * (1.0 + pre * (1.0 - sig)))).astype(BF)

    chunks(rows_ref.shape[1], step)
    sums = mm_t(picks_ref[first:, :], grad_pre_ref[...])
    put_sends(flags_ref, sums, (send0_ref, send1_ref, send2_ref, send3_ref))


def merged_grad(partial_ref, flags_ref, returned, src_ref, rim_picks):
    marks = (flags_ref[PAIR], flags_ref[PAIR + 1], flags_ref[3], flags_ref[2])
    total = returned[0][...].astype(F32) * marks[0]
    for side in range(1, 4):
        total += returned[side][...].astype(F32) * marks[side]
    back = mm(rim_picks[...], total.astype(BF)).astype(BF)
    return partial_ref[...] + mm_t(back, src_ref[...])


def backward_body(
    flags_ref,
    first_ref,
    second_ref,
    left_ref,
    right_ref,
    partial_ref,
    src_ref,
    rim_picks,
    msg_ref,
    slope_ref,
    picks_ref,
    grad_ref,
    grad_pre_ref,
    send0_ref,
    send1_ref,
    send2_ref,
    send3_ref,
):
    nodes = partial_ref.shape[0]
    returned = (first_ref, second_ref, left_ref, right_ref)
    grad = merged_grad(partial_ref, flags_ref, returned, src_ref, rim_picks)
    grad_ref[...] = grad
    back = mm_t(msg_ref[...], grad.astype(BF)).astype(BF)

    def step(start, at):
        grad_pre = mm(back, picks_ref[:nodes, at]) * slope_ref[:, at].astype(F32)
        grad_pre_ref[:, at] = grad_pre.astype(BF)

    chunks(picks_ref.shape[1], step)
    sums = mm_t(picks_ref[2 * nodes :, :], grad_pre_ref[...])
    put_sends(flags_ref, sums, (send0_ref, send1_ref, send2_ref, send3_ref))


def sums_body(picks_ref, grad_pre_ref, grad_ref, src_ref, dst_ref, own_ref, partial_ref):
    nodes = grad_ref.shape[0]
    own_ref[...] = mm_t(picks_ref[: 2 * nodes, :], grad_pre_ref[...]).astype(BF)
    partial_ref[...] = (
        grad_ref[...].astype(F32)
        + mm_t(own_ref[:nodes, :], dst_ref[...])
        + mm_t(own_ref[nodes:, :], src_ref[...])
    )


def out_body(picks_ref, act_edges_ref, state_ref, msg_ref, act_ref, out_ref):
    nodes = state_ref.shape[0]
    act_ref[...] = mm_t(picks_ref[:nodes, :], act_edges_ref[...]).astype(BF)
    out_ref[...] = (state_ref[...].astype(F32) + mm(act_ref[...], msg_ref[...])).astype(BF)


def put_halves(flags_ref, first, term, keep_ref, send_ref):
    half = term.shape[1] // 2
    odd = flags_ref[ODD_DOM] > 0.5
    low, high = term[:, :half].astype(BF), term[:, half:].astype(BF)
    keep_ref[first : first + term.shape[0], :] = jnp.where(odd, high, low)
    send_ref[first : first + term.shape[0], :] = jnp.where(odd, low, high)


def terms_body(
    flags_ref,
    first_ref,
    second_ref,
    left_ref,
    right_ref,
    send0_ref,
    send1_ref,
    send2_ref,
    send3_ref,
    state_ref,
    own_ref,
    act_ref,
    grad_ref,
    keep_ref,
    send_ref,
):
    nodes, width = state_ref.shape
    state = state_ref[...]
    src_term = t_mm(state, own_ref[nodes:, :])
    pairs = (
        (first_ref, send0_ref, flags_ref[PAIR]),
        (second_ref, send1_ref, flags_ref[PAIR + 1]),
        (left_ref, send2_ref, flags_ref[2]),
        (right_ref, send3_ref, flags_ref[3]),
    )
    for rim_ref, sums_ref, mark in pairs:
        src_term += t_mm(rim_ref[...], sums_ref[...]) * mark
    put_halves(flags_ref, 0, src_term, keep_ref, send_ref)
    put_halves(flags_ref, width, t_mm(state, own_ref[:nodes, :]), keep_ref, send_ref)
    put_halves(
        flags_ref, 2 * width, t_mm(act_ref[...], grad_ref[...].astype(BF)), keep_ref, send_ref
    )


def last_body(
    bucket,
    flags_ref,
    first_ref,
    second_ref,
    left_ref,
    right_ref,
    partial_ref,
    src_ref,
    rim_picks,
    packed_ref,
    enc_out_ref,
    pooled_ref,
    slope_ref,
    picks_ref,
    keep_ref,
    send_ref,
):
    fin = packed_ref.shape[2]
    peers_step = CHUNK // bucket
    returned = (first_ref, second_ref, left_ref, right_ref)
    grad = merged_grad(partial_ref, flags_ref, returned, src_ref, rim_picks).astype(BF)
    back = mm_t(enc_out_ref[...], grad).astype(BF)
    in_term = jnp.zeros((enc_out_ref.shape[0], fin), F32)
    for start in range(0, picks_ref.shape[1], CHUNK):
        at = pl.ds(start, CHUNK)
        first = start // bucket
        got = packed_ref[first : first + peers_step, :bucket, :].reshape(CHUNK, fin)
        grad_pre = mm(back, picks_ref[:, at]) * slope_ref[:, at].astype(F32)
        in_term += mm(grad_pre.astype(BF), got)
    put_halves(flags_ref, 0, in_term.T, keep_ref, send_ref)
    put_halves(flags_ref, fin, t_mm(pooled_ref[...], grad), keep_ref, send_ref)


def merge_body(*refs):
    out_ref = refs[-1]
    first = 0
    for keep_ref, got_ref in zip(refs[:-1:2], refs[1:-1:2]):
        rows = keep_ref.shape[0]
        total = keep_ref[...].astype(F32) + got_ref[...].astype(F32)
        out_ref[first : first + rows, :] = total.astype(BF)
        first += rows
    if first < out_ref.shape[0]:
        out_ref[first:, :] = jnp.zeros((out_ref.shape[0] - first, out_ref.shape[1]), BF)


def share_body(parts_ref, out_ref):
    count = parts_ref.shape[0]
    for odd in range(2):
        total = parts_ref[odd].astype(F32)
        for peer in range(odd + 2, count, 2):
            total += parts_ref[peer].astype(F32)
        for peer in range(odd, count, 2):
            out_ref[peer] = total.astype(BF)


def unpack_body(flags_ref, mine_ref, other_ref, *outs):
    odd = flags_ref[ODD_DOM] > 0.5
    half = mine_ref.shape[1]
    first = 0

    def put(ref, rows):
        nonlocal first
        mine = mine_ref[first : first + rows, :].astype(F32)
        other = other_ref[first : first + rows, :].astype(F32)
        ref[:, :half] = jnp.where(odd, other, mine)
        ref[:, half:] = jnp.where(odd, mine, other)
        first += rows

    enc_in_ref, enc_out_ref, *layer_refs = outs
    for layer in reversed(range(layer_refs[0].shape[0])):
        for ref in layer_refs:
            put(ref.at[layer], ref.shape[1])
    put(enc_in_ref, enc_in_ref.shape[0])
    put(enc_out_ref, enc_out_ref.shape[0])


def exchange(shard):
    return lax.all_to_all(shard, AXES, split_axis=0, concat_axis=0, tiled=True)


def turned(shard, axis, by):
    count = lax.axis_size(axis)
    return lax.ppermute(shard, axis, [(i, (i + by) % count) for i in range(count)])


def swapped(shard, axis, offset):
    count = lax.axis_size(axis)
    partner = list(range(count))
    for i in range(offset, count - 1, 2):
        partner[i], partner[i + 1] = i + 1, i
    return lax.ppermute(shard, axis, list(enumerate(partner)))


def from_neighbours(rim_rows):
    return (
        swapped(rim_rows, "grid", 0),
        swapped(rim_rows, "grid", 1),
        turned(rim_rows, "dom", 1),
        turned(rim_rows, "dom", -1),
    )


def to_neighbours(sends):
    return (
        swapped(sends[0], "grid", 0),
        swapped(sends[1], "grid", 1),
        turned(sends[2], "dom", -1),
        turned(sends[3], "dom", 1),
    )


def per_device(
    columns,
    column_live,
    col_weight,
    col_slot,
    node_static,
    boundary_idx,
    edge_src,
    edge_dst,
    edge_live,
    edge_weight,
    enc_in,
    enc_out,
    src_proj,
    dst_proj,
    msg_proj,
    node_cotangent,
):
    peers = lax.axis_size(AXES)
    cols, fin = columns.shape
    nodes, width = node_static.shape
    rim = boundary_idx.shape[0]
    edges = edge_src.shape[0]
    ext = 4 * rim
    bucket = cols // peers

    lanes = (cols // LANES, LANES)
    held = [pltpu.VMEM(lanes, jnp.int32), pltpu.VMEM(lanes, jnp.int32), pltpu.VMEM(lanes, F32)]
    (packed,) = call(
        pack_body,
        [((peers, bucket + 4, fin), BF)],
        held + [pltpu.SemaphoreType.DMA((4,))],
        "pack",
        space=pltpu.HBM,
    )(
        columns.reshape(peers, bucket, fin),
        col_slot.reshape(lanes),
        column_live.reshape(lanes),
        col_weight.reshape(lanes),
    )
    packed = exchange(packed)

    grid_at, grid_count = lax.axis_index("grid"), lax.axis_size("grid")
    dom_at, dom_count = lax.axis_index("dom"), lax.axis_size("dom")
    odd_grid, odd_dom = grid_at % 2, dom_at % 2
    up, down = grid_at > 0, grid_at < grid_count - 1
    flags = jnp.stack(
        [
            up,
            down,
            dom_at > 0,
            dom_at < dom_count - 1,
            jnp.where(odd_grid == 1, up, down),
            jnp.where(odd_grid == 1, down, up),
            odd_grid == 1,
            odd_dom == 1,
        ]
    ).astype(F32)
    edge_scale = edge_weight * edge_live.astype(F32)
    edge_rows = jnp.stack([edge_src.astype(F32), edge_dst.astype(F32), edge_scale])
    bound = boundary_idx.astype(F32)[None]
    enc_in_t = enc_in.T
    src_t = src_proj.transpose(0, 2, 1)
    dst_t = dst_proj.transpose(0, 2, 1)

    node_shape = ((nodes, width), BF)
    node_wide = ((nodes, width), F32)
    rim_shape = ((rim, width), BF)
    edge_shape = ((width, edges), BF)
    edge_wide = ((width, edges), F32)
    full = pltpu.VMEM((width, ext), BF)
    edge_buf = pltpu.VMEM((width, edges), BF)
    table_buf = pltpu.VMEM((width, 2 * nodes), BF)

    picks, rim_picks, rim_picks_t = call(
        picks_body,
        [((2 * nodes + ext, edges), BF), ((nodes, rim), BF), ((rim, nodes), BF)],
        [],
        "picks",
    )(edge_rows, bound)
    (back1,) = call(back_body, [edge_wide], [], "back")(msg_proj[1], node_cotangent, edge_rows, picks)
    packed, back1 = lax.optimization_barrier((packed, back1))

    at = (grid_at * dom_count + dom_at) % (LANES // bucket)
    extra = lax.dynamic_slice_in_dim(packed[:, bucket : bucket + 4], at * bucket, bucket, 2)
    extra = extra.astype(F32).transpose(1, 0, 2).reshape(4, cols)
    col_rows = jnp.stack([extra[0] * 256.0 + extra[1], extra[2] + extra[3]])

    pooled, col_slope, slot_picks, state0, rim0 = call(
        functools.partial(encode_body, bucket),
        [node_shape, ((width, cols), BF), ((nodes, cols), BF), node_shape, rim_shape],
        [pltpu.VMEM((width, cols), BF)],
        "encode",
    )(packed, col_rows, enc_in_t, enc_out, node_static, rim_picks_t)

    rims0 = from_neighbours(rim0)
    (pre0,) = call(own_body, [edge_wide], [table_buf], "own")(state0, src_t[0], dst_t[0], picks)
    slope0, act0, state1, rim1 = call(
        forward_body,
        [edge_shape, node_shape, node_shape, rim_shape],
        [full, edge_buf],
        "forward",
        True,
    )(flags, *rims0, pre0, edge_rows, picks, state0, src_t[0], msg_proj[0], rim_picks_t)

    rims1 = from_neighbours(rim1)
    (pre1,) = call(own_body, [edge_wide], [table_buf], "own")(state1, src_t[1], dst_t[1], picks)
    act_edges1, grad_pre1, *sends1 = call(
        turn_body, [edge_shape, edge_shape] + [rim_shape] * 4, [full], "turn", True
    )(flags, *rims1, pre1, back1, edge_rows, picks, src_t[1])

    returned1 = to_neighbours(sends1)
    own_shape = ((2 * nodes, width), BF)
    halves = [((3 * width, width // 2), BF)] * 2
    own1, partial1 = call(sums_body, [own_shape, node_wide], [], "sums")(
        picks, grad_pre1, node_cotangent, src_proj[1], dst_proj[1]
    )
    act1, node_out = call(out_body, [node_shape, node_shape], [], "out")(
        picks, act_edges1, state1, msg_proj[1]
    )
    keep1, send1 = call(terms_body, halves, [], "terms", True)(
        flags, *rims1, *sends1, state1, own1, act1, node_cotangent
    )
    partial1, keep1, send1 = lax.optimization_barrier((partial1, keep1, send1))
    grad1, grad_pre0, *sends0 = call(
        backward_body, [node_wide, edge_shape] + [rim_shape] * 4, [], "backward", True
    )(flags, *returned1, partial1, src_proj[1], rim_picks, msg_proj[0], slope0, picks)

    returned0 = to_neighbours(sends0)
    own0, partial0 = call(sums_body, [own_shape, node_wide], [], "sums")(
        picks, grad_pre0, grad1, src_proj[0], dst_proj[0]
    )
    keep0, send0 = call(terms_body, halves, [], "terms", True)(
        flags, *rims0, *sends0, state0, own0, act0, grad1
    )
    hidden = enc_out.shape[0]
    keep_enc, send_enc = call(
        functools.partial(last_body, bucket),
        [((fin + hidden, width // 2), BF)] * 2,
        [],
        "last",
        True,
    )(flags, *returned0, partial0, src_proj[0], rim_picks, packed, enc_out, pooled, col_slope, slot_picks)

    total_rows = 2 * 3 * width + fin + hidden
    share = -(-total_rows // (16 * peers)) * 16
    rows = peers * share
    (merged,) = call(merge_body, [((rows, width // 2), BF)], [], "merge")(
        keep1,
        swapped(send1, "dom", 0),
        keep0,
        swapped(send0, "dom", 0),
        keep_enc,
        swapped(send_enc, "dom", 0),
    )
    parts = exchange(merged.reshape(peers, share, width // 2))
    (spread,) = call(share_body, [((peers, share, width // 2), BF)], [], "share")(parts)
    mine = exchange(spread).reshape(rows, width // 2)
    layer_shape = ((2, width, width), F32)
    grads = call(
        unpack_body,
        [((fin, width), F32), ((hidden, width), F32), layer_shape, layer_shape, layer_shape],
        [],
        "unpack",
        True,
    )(flags, mine, swapped(mine, "dom", 0))
    return (node_out, *grads)


def solution(mesh):
    rows = P(AXES, None)
    flat = P(AXES)
    placed = (rows, flat, flat, flat, rows, flat, flat, flat, flat, flat, P(), P(), P(), P(), P(), rows)
    return jax.shard_map(
        per_device,
        mesh=mesh,
        in_specs=placed,
        out_specs=(rows, P(), P(), P(), P(), P()),
        check_vma=False,
    )
```

```python
import functools

import jax
import jax.numpy as jnp
from jax import lax
from jax.experimental import pallas as pl
from jax.experimental.pallas import tpu as pltpu
from jax.sharding import PartitionSpec as P

AXES = ("grid", "dom")
BF = jnp.bfloat16
F32 = jnp.float32
LANES = 128
TILE = 256
CHUNK = 512
GRANT = 20 << 20


def mm(left_side, right_side):
    return jnp.dot(left_side, right_side, preferred_element_type=F32)


def mm_t(left_side, right_side):
    return lax.dot_general(
        left_side, right_side, (((1,), (1,)), ((), ())), preferred_element_type=F32
    )


def t_mm(left_side, right_side):
    return lax.dot_general(
        left_side, right_side, (((0,), (0,)), ((), ())), preferred_element_type=F32
    )


def put_picks(out_ref, start, indices, count):
    rows = lax.broadcasted_iota(jnp.int32, (TILE, indices.shape[1]), 0).astype(F32).astype(BF)
    for base in range(0, count, TILE):
        shifted = (indices - float(base)).astype(BF)
        block = jnp.where(rows == shifted, jnp.ones((), BF), jnp.zeros((), BF))
        out_ref[start + base : start + base + TILE, :] = block


def sigmoid(values):
    return 0.5 * jnp.tanh(0.5 * values) + 0.5


def call(body, outs, scratch, name, flagged=False, far=()):
    vmem = pl.BlockSpec(memory_space=pltpu.VMEM)

    def run(*args):
        specs = [vmem] * len(args)
        if flagged:
            specs[0] = pl.BlockSpec(memory_space=pltpu.SMEM)
        args = list(args)
        for at in far:
            specs[at] = pl.BlockSpec(memory_space=pltpu.HBM)
            args[at] = pltpu.with_memory_space_constraint(args[at], pltpu.HBM)
        return pl.pallas_call(
            body,
            out_shape=tuple(jax.ShapeDtypeStruct(shape, dtype) for shape, dtype in outs),
            in_specs=specs,
            out_specs=tuple(vmem for _ in outs),
            scratch_shapes=scratch,
            compiler_params=pltpu.CompilerParams(vmem_limit_bytes=GRANT),
            name=name,
        )(*args)

    return run


def chunks(total, body):
    for start in range(0, total, CHUNK):
        body(start, pl.ds(start, CHUNK))


def pack_body(cols_ref, slot_ref, live_ref, weight_ref, out_ref, slot_buf, live_buf, weight_buf, sems):
    peers, bucket, _ = cols_ref.shape
    per_row = LANES // bucket
    copies = [
        pltpu.make_async_copy(cols_ref, out_ref.at[:, :bucket, :], sems.at[0]),
        pltpu.make_async_copy(slot_ref, slot_buf, sems.at[1]),
        pltpu.make_async_copy(live_ref, live_buf, sems.at[2]),
        pltpu.make_async_copy(weight_ref, weight_buf, sems.at[3]),
    ]
    for copy in copies:
        copy.start()
    for copy in copies[1:]:
        copy.wait()
    slot = slot_buf[...].astype(F32)
    high = jnp.floor(slot * (1.0 / 256.0))
    low = slot - 256.0 * high
    scale = weight_buf[...] * live_buf[...].astype(F32)
    scale_high = scale.astype(BF)
    scale_low = (scale - scale_high.astype(F32)).astype(BF)
    fields = [high.astype(BF), low.astype(BF), scale_high, scale_low]
    for peer in range(peers):
        row = peer // per_row
        extra = jnp.concatenate([field[row : row + 1, :] for field in fields], 0)
        out_ref[peer, bucket : bucket + 4, :] = extra
    copies[0].wait()


PAIR, ODD_GRID, ODD_DOM, PLACE = 4, 6, 7, 8


def picks_body(rows_ref, bound_ref, picks_ref, rim_picks, rim_picks_t):
    nodes = rim_picks.shape[0]
    ext = picks_ref.shape[0] - 2 * nodes
    for start in range(0, rows_ref.shape[1], CHUNK):
        at = pl.ds(start, CHUNK)
        block = picks_ref.at[:, at]
        put_picks(block, 0, rows_ref[1:2, at], nodes)
        put_picks(block, nodes, rows_ref[0:1, at], nodes + ext)
    put_picks(rim_picks, 0, bound_ref[0:1, :], nodes)
    rim_picks_t[...] = rim_picks[...].astype(F32).T.astype(BF)


def put_state(state, state_ref, rim_ref, rim_picks_t):
    state_ref[...] = state.astype(BF)
    rim_ref[...] = mm(rim_picks_t[...], state_ref[...]).astype(BF)


def in_order(flags_ref, rims):
    first, second, left, right = (ref[...] for ref in rims)
    odd = flags_ref[ODD_GRID] > 0.5
    ordered = (jnp.where(odd, first, second), jnp.where(odd, second, first), left, right)
    return [rows * flags_ref[side].astype(BF) for side, rows in enumerate(ordered)]


def put_col_rows(flags_ref, packed_ref, bucket, rows_ref):
    peers = packed_ref.shape[0]
    per_row = LANES // bucket
    place = flags_ref[PLACE].astype(jnp.int32)
    lane = lax.broadcasted_iota(jnp.int32, (4, LANES), 1)
    for row in range(peers // per_row):
        out = jnp.zeros((4, LANES), F32)
        for j in range(per_row):
            part = packed_ref[row * per_row + j, bucket : bucket + 4, :].astype(F32)
            shift = lax.rem((j - place + per_row) * bucket, LANES)
            part = pltpu.roll(part, shift, 1)
            here = (lane >= j * bucket) & (lane < (j + 1) * bucket)
            out = jnp.where(here, part, out)
        at = pl.ds(row * LANES, LANES)
        rows_ref[0:1, at] = out[0:1] * 256.0 + out[1:2]
        rows_ref[1:2, at] = out[2:3] + out[3:4]


def encode_body(
    bucket,
    flags_ref,
    packed_ref,
    enc_in_t_far,
    enc_out_far,
    static_far,
    bound_far,
    pooled_ref,
    slope_ref,
    picks_ref,
    state_ref,
    rim_ref,
    act_ref,
    rows_ref,
    enc_in_t_ref,
    enc_out_ref,
    static_ref,
    bound_ref,
    rim_picks,
    sems,
):
    nodes = static_ref.shape[0]
    peers_step = CHUNK // bucket
    copies = [
        pltpu.make_async_copy(enc_in_t_far, enc_in_t_ref, sems.at[0]),
        pltpu.make_async_copy(enc_out_far, enc_out_ref, sems.at[1]),
        pltpu.make_async_copy(static_far, static_ref, sems.at[2]),
        pltpu.make_async_copy(bound_far, bound_ref, sems.at[3]),
    ]
    for copy in copies:
        copy.start()
    put_col_rows(flags_ref, packed_ref, bucket, rows_ref)
    copies[0].wait()

    def step(start, at):
        first = start // bucket
        got = packed_ref[first : first + peers_step, :bucket, :].reshape(CHUNK, packed_ref.shape[2])
        pre = mm_t(enc_in_t_ref[...], got)
        scale = rows_ref[1:2, at]
        sig = sigmoid(pre)
        act_ref[:, at] = (pre * sig * scale).astype(BF)
        slope_ref[:, at] = (sig * (1.0 + pre * (1.0 - sig)) * scale).astype(BF)
        put_picks(picks_ref.at[:, at], 0, rows_ref[0:1, at], nodes)

    chunks(rows_ref.shape[1], step)
    pooled_ref[...] = mm_t(picks_ref[...], act_ref[...]).astype(BF)
    for copy in copies[1:]:
        copy.wait()
    put_picks(rim_picks, 0, bound_ref[0:1, :], nodes)
    state = static_ref[...].astype(F32) + mm(pooled_ref[...], enc_out_ref[...])
    state_ref[...] = state.astype(BF)
    rim_ref[...] = t_mm(rim_picks[...], state_ref[...]).astype(BF)


def own_body(layer, state_ref, src_t_ref, dst_t_ref, picks_ref, out_ref, table_ref):
    nodes = state_ref.shape[0]
    held = state_ref[...]
    table_ref[:, :nodes] = mm_t(dst_t_ref[layer], held).astype(BF)
    table_ref[:, nodes:] = mm_t(src_t_ref[layer], held).astype(BF)
    out_ref[...] = mm(table_ref[...], picks_ref[: 2 * nodes, :])


def back_body(layer, msg_ref, grad_ref, rows_ref, picks_ref, out_ref):
    nodes = grad_ref.shape[0]
    back = mm_t(msg_ref[layer], grad_ref[...]).astype(BF)
    out_ref[...] = mm(back, picks_ref[:nodes, :]) * rows_ref[2:3, :]


def fill_rims(full_ref, flags_ref, rims, src_t_ref):
    rim = rims[0].shape[0]
    for side, rim_rows in enumerate(in_order(flags_ref, rims)):
        full_ref[:, side * rim : (side + 1) * rim] = mm_t(src_t_ref[...], rim_rows).astype(BF)


def forward_body(
    layer,
    flags_ref,
    first_ref,
    second_ref,
    left_ref,
    right_ref,
    own_pre_ref,
    rows_ref,
    picks_ref,
    state_ref,
    src_t_ref,
    msg_ref,
    rim_picks_t,
    slope_ref,
    node_act_ref,
    next_state_ref,
    rim_ref,
    full_ref,
    act_ref,
):
    nodes = state_ref.shape[0]
    fill_rims(full_ref, flags_ref, (first_ref, second_ref, left_ref, right_ref), src_t_ref.at[layer])

    def step(start, at):
        pre = own_pre_ref[:, at] + mm(full_ref[...], picks_ref[2 * nodes :, at])
        scale = rows_ref[2:3, at]
        sig = sigmoid(pre)
        act_ref[:, at] = (pre * sig * scale).astype(BF)
        slope_ref[:, at] = (sig * (1.0 + pre * (1.0 - sig)) * scale).astype(BF)

    chunks(rows_ref.shape[1], step)
    node_act_ref[...] = mm_t(picks_ref[:nodes, :], act_ref[...]).astype(BF)
    state = state_ref[...].astype(F32) + mm(node_act_ref[...], msg_ref[layer])
    put_state(state, next_state_ref, rim_ref, rim_picks_t)


def put_sends(flags_ref, sums, sends):
    rim = sums.shape[0] // 4
    up, down, left, right = (sums[side * rim : (side + 1) * rim, :].astype(BF) for side in range(4))
    odd = flags_ref[ODD_GRID] > 0.5
    sends[0][...] = jnp.where(odd, up, down)
    sends[1][...] = jnp.where(odd, down, up)
    sends[2][...] = left
    sends[3][...] = right


def turn_body(
    layer,
    flags_ref,
    first_ref,
    second_ref,
    left_ref,
    right_ref,
    own_pre_ref,
    back_ref,
    rows_ref,
    picks_ref,
    src_t_ref,
    act_ref,
    grad_pre_ref,
    send0_ref,
    send1_ref,
    send2_ref,
    send3_ref,
    full_ref,
):
    first = picks_ref.shape[0] - full_ref.shape[1]
    fill_rims(full_ref, flags_ref, (first_ref, second_ref, left_ref, right_ref), src_t_ref.at[layer])

    def step(start, at):
        pre = own_pre_ref[:, at] + mm(full_ref[...], picks_ref[first:, at])
        sig = sigmoid(pre)
        act_ref[:, at] = (pre * sig * rows_ref[2:3, at]).astype(BF)
        grad_pre_ref[:, at] = (back_ref[:, at] * (sig * (1.0 + pre * (1.0 - sig)))).astype(BF)

    chunks(rows_ref.shape[1], step)
    sums = mm_t(picks_ref[first:, :], grad_pre_ref[...])
    put_sends(flags_ref, sums, (send0_ref, send1_ref, send2_ref, send3_ref))


def merged_grad(partial_ref, flags_ref, returned, src_ref, rim_picks):
    marks = (flags_ref[PAIR], flags_ref[PAIR + 1], flags_ref[3], flags_ref[2])
    total = returned[0][...].astype(F32) * marks[0]
    for side in range(1, 4):
        total += returned[side][...].astype(F32) * marks[side]
    back = mm(rim_picks[...], total.astype(BF)).astype(BF)
    return partial_ref[...] + mm_t(back, src_ref[...])


def backward_body(
    layer,
    flags_ref,
    first_ref,
    second_ref,
    left_ref,
    right_ref,
    partial_ref,
    src_ref,
    rim_picks,
    msg_ref,
    slope_ref,
    picks_ref,
    grad_ref,
    grad_pre_ref,
    send0_ref,
    send1_ref,
    send2_ref,
    send3_ref,
):
    nodes = partial_ref.shape[0]
    returned = (first_ref, second_ref, left_ref, right_ref)
    grad = merged_grad(partial_ref, flags_ref, returned, src_ref.at[layer], rim_picks)
    grad_ref[...] = grad
    back = mm_t(msg_ref[layer - 1], grad.astype(BF)).astype(BF)

    def step(start, at):
        grad_pre = mm(back, picks_ref[:nodes, at]) * slope_ref[:, at].astype(F32)
        grad_pre_ref[:, at] = grad_pre.astype(BF)

    chunks(picks_ref.shape[1], step)
    sums = mm_t(picks_ref[2 * nodes :, :], grad_pre_ref[...])
    put_sends(flags_ref, sums, (send0_ref, send1_ref, send2_ref, send3_ref))


def sums_body(layer, picks_ref, grad_pre_ref, grad_ref, src_ref, dst_ref, own_ref, partial_ref):
    nodes = grad_ref.shape[0]
    own_ref[...] = mm_t(picks_ref[: 2 * nodes, :], grad_pre_ref[...]).astype(BF)
    partial_ref[...] = (
        grad_ref[...].astype(F32)
        + mm_t(own_ref[:nodes, :], dst_ref[layer])
        + mm_t(own_ref[nodes:, :], src_ref[layer])
    )


def out_body(layer, picks_ref, act_edges_ref, state_ref, msg_ref, act_ref, out_ref):
    nodes = state_ref.shape[0]
    act_ref[...] = mm_t(picks_ref[:nodes, :], act_edges_ref[...]).astype(BF)
    out_ref[...] = (state_ref[...].astype(F32) + mm(act_ref[...], msg_ref[layer])).astype(BF)


def put_halves(flags_ref, first, term, keep_ref, send_ref):
    half = term.shape[1] // 2
    odd = flags_ref[ODD_DOM] > 0.5
    low, high = term[:, :half].astype(BF), term[:, half:].astype(BF)
    keep_ref[first : first + term.shape[0], :] = jnp.where(odd, high, low)
    send_ref[first : first + term.shape[0], :] = jnp.where(odd, low, high)


def terms_body(
    flags_ref,
    first_ref,
    second_ref,
    left_ref,
    right_ref,
    send0_ref,
    send1_ref,
    send2_ref,
    send3_ref,
    state_ref,
    own_ref,
    act_ref,
    grad_ref,
    keep_ref,
    send_ref,
):
    nodes, width = state_ref.shape
    state = state_ref[...]
    src_term = t_mm(state, own_ref[nodes:, :])
    pairs = (
        (first_ref, send0_ref, flags_ref[PAIR]),
        (second_ref, send1_ref, flags_ref[PAIR + 1]),
        (left_ref, send2_ref, flags_ref[2]),
        (right_ref, send3_ref, flags_ref[3]),
    )
    for rim_ref, sums_ref, mark in pairs:
        src_term += t_mm(rim_ref[...], sums_ref[...]) * mark
    put_halves(flags_ref, 0, src_term, keep_ref, send_ref)
    put_halves(flags_ref, width, t_mm(state, own_ref[:nodes, :]), keep_ref, send_ref)
    put_halves(
        flags_ref, 2 * width, t_mm(act_ref[...], grad_ref[...].astype(BF)), keep_ref, send_ref
    )


def last_body(
    bucket,
    flags_ref,
    first_ref,
    second_ref,
    left_ref,
    right_ref,
    partial_ref,
    src_ref,
    rim_picks,
    packed_ref,
    enc_out_ref,
    pooled_ref,
    slope_ref,
    picks_ref,
    keep_ref,
    send_ref,
):
    fin = packed_ref.shape[2]
    peers_step = CHUNK // bucket
    returned = (first_ref, second_ref, left_ref, right_ref)
    grad = merged_grad(partial_ref, flags_ref, returned, src_ref.at[0], rim_picks).astype(BF)
    back = mm_t(enc_out_ref[...], grad).astype(BF)
    in_term = jnp.zeros((enc_out_ref.shape[0], fin), F32)
    for start in range(0, picks_ref.shape[1], CHUNK):
        at = pl.ds(start, CHUNK)
        first = start // bucket
        got = packed_ref[first : first + peers_step, :bucket, :].reshape(CHUNK, fin)
        grad_pre = mm(back, picks_ref[:, at]) * slope_ref[:, at].astype(F32)
        in_term += mm(grad_pre.astype(BF), got)
    put_halves(flags_ref, 0, in_term.T, keep_ref, send_ref)
    put_halves(flags_ref, fin, t_mm(pooled_ref[...], grad), keep_ref, send_ref)


def merge_body(*refs):
    out_ref = refs[-1]
    first = 0
    for keep_ref, got_ref in zip(refs[:-1:2], refs[1:-1:2]):
        rows = keep_ref.shape[0]
        total = keep_ref[...].astype(F32) + got_ref[...].astype(F32)
        out_ref[first : first + rows, :] = total.astype(BF)
        first += rows
    if first < out_ref.shape[0]:
        out_ref[first:, :] = jnp.zeros((out_ref.shape[0] - first, out_ref.shape[1]), BF)


def share_body(parts_ref, out_ref):
    count = parts_ref.shape[0]
    for odd in range(2):
        total = parts_ref[odd].astype(F32)
        for peer in range(odd + 2, count, 2):
            total += parts_ref[peer].astype(F32)
        for peer in range(odd, count, 2):
            out_ref[peer] = total.astype(BF)


def unpack_body(flags_ref, mine_ref, other_ref, *outs):
    odd = flags_ref[ODD_DOM] > 0.5
    half = mine_ref.shape[1]
    first = 0

    def put(ref, rows):
        nonlocal first
        mine = mine_ref[first : first + rows, :].astype(F32)
        other = other_ref[first : first + rows, :].astype(F32)
        ref[:, :half] = jnp.where(odd, other, mine)
        ref[:, half:] = jnp.where(odd, mine, other)
        first += rows

    enc_in_ref, enc_out_ref, *layer_refs = outs
    for layer in reversed(range(layer_refs[0].shape[0])):
        for ref in layer_refs:
            put(ref.at[layer], ref.shape[1])
    put(enc_in_ref, enc_in_ref.shape[0])
    put(enc_out_ref, enc_out_ref.shape[0])


def exchange(shard):
    return lax.all_to_all(shard, AXES, split_axis=0, concat_axis=0, tiled=True)


def turned(shard, axis, by):
    count = lax.axis_size(axis)
    return lax.ppermute(shard, axis, [(i, (i + by) % count) for i in range(count)])


def swapped(shard, axis, offset):
    count = lax.axis_size(axis)
    partner = list(range(count))
    for i in range(offset, count - 1, 2):
        partner[i], partner[i + 1] = i + 1, i
    return lax.ppermute(shard, axis, list(enumerate(partner)))


def from_neighbours(rim_rows):
    return (
        swapped(rim_rows, "grid", 0),
        swapped(rim_rows, "grid", 1),
        turned(rim_rows, "dom", 1),
        turned(rim_rows, "dom", -1),
    )


def to_neighbours(sends):
    return (
        swapped(sends[0], "grid", 0),
        swapped(sends[1], "grid", 1),
        turned(sends[2], "dom", -1),
        turned(sends[3], "dom", 1),
    )


def floats(scalars):
    return jnp.stack([scalar.astype(F32) for scalar in scalars])


def per_device(
    columns,
    column_live,
    col_weight,
    col_slot,
    node_static,
    boundary_idx,
    edge_src,
    edge_dst,
    edge_live,
    edge_weight,
    enc_in,
    enc_out,
    src_proj,
    dst_proj,
    msg_proj,
    node_cotangent,
):
    peers = lax.axis_size(AXES)
    cols, fin = columns.shape
    nodes, width = node_static.shape
    rim = boundary_idx.shape[0]
    edges = edge_src.shape[0]
    ext = 4 * rim
    bucket = cols // peers

    lanes = (cols // LANES, LANES)
    held = [pltpu.VMEM(lanes, jnp.int32), pltpu.VMEM(lanes, jnp.int32), pltpu.VMEM(lanes, F32)]
    (packed,) = call(
        pack_body,
        [((peers, bucket + 4, fin), BF)],
        held + [pltpu.SemaphoreType.DMA((4,))],
        "pack",
        far=range(4),
    )(
        columns.reshape(peers, bucket, fin),
        col_slot.reshape(lanes),
        column_live.reshape(lanes),
        col_weight.reshape(lanes),
    )
    packed = exchange(packed)

    grid_at, grid_count = lax.axis_index("grid"), lax.axis_size("grid")
    dom_at, dom_count = lax.axis_index("dom"), lax.axis_size("dom")
    odd_grid, odd_dom = grid_at % 2, dom_at % 2
    up, down = grid_at > 0, grid_at < grid_count - 1
    flags = floats(
        [
            up,
            down,
            dom_at > 0,
            dom_at < dom_count - 1,
            jnp.where(odd_grid == 1, up, down),
            jnp.where(odd_grid == 1, down, up),
            odd_grid == 1,
            odd_dom == 1,
            (grid_at * dom_count + dom_at) % (LANES // bucket),
        ]
    )
    edge_scale = edge_weight * edge_live.astype(F32)
    edge_rows = jnp.stack([edge_src.astype(F32), edge_dst.astype(F32), edge_scale])
    bound = boundary_idx.astype(F32)[None]
    enc_in_t = enc_in.T
    src_t = src_proj.transpose(0, 2, 1)
    dst_t = dst_proj.transpose(0, 2, 1)

    node_shape = ((nodes, width), BF)
    node_wide = ((nodes, width), F32)
    rim_shape = ((rim, width), BF)
    edge_shape = ((width, edges), BF)
    edge_wide = ((width, edges), F32)
    full = pltpu.VMEM((width, ext), BF)
    edge_buf = pltpu.VMEM((width, edges), BF)
    table_buf = pltpu.VMEM((width, 2 * nodes), BF)

    flags, edge_rows, bound, enc_in_t, src_t, dst_t = lax.optimization_barrier(
        (flags, edge_rows, bound, enc_in_t, src_t, dst_t)
    )

    pooled, col_slope, slot_picks, state0, rim0 = call(
        functools.partial(encode_body, bucket),
        [node_shape, ((width, cols), BF), ((nodes, cols), BF), node_shape, rim_shape],
        [
            edge_buf,
            pltpu.VMEM((2, cols), F32),
            pltpu.VMEM((width, fin), BF),
            pltpu.VMEM(enc_out.shape, BF),
            pltpu.VMEM((nodes, width), BF),
            pltpu.VMEM((1, rim), F32),
            pltpu.VMEM((nodes, rim), BF),
            pltpu.SemaphoreType.DMA((4,)),
        ],
        "encode",
        True,
        far=range(2, 6),
    )(flags, packed, enc_in_t, enc_out, node_static, bound)

    state0, edge_rows, bound = lax.optimization_barrier((state0, edge_rows, bound))
    picks, rim_picks, rim_picks_t = call(
        picks_body,
        [((2 * nodes + ext, edges), BF), ((nodes, rim), BF), ((rim, nodes), BF)],
        [],
        "picks",
    )(edge_rows, bound)

    rims0 = from_neighbours(rim0)
    (pre0,) = call(functools.partial(own_body, 0), [edge_wide], [table_buf], "own")(
        state0, src_t, dst_t, picks
    )
    slope0, act0, state1, rim1 = call(
        functools.partial(forward_body, 0),
        [edge_shape, node_shape, node_shape, rim_shape],
        [full, edge_buf],
        "forward",
        True,
    )(flags, *rims0, pre0, edge_rows, picks, state0, src_t, msg_proj, rim_picks_t)

    rims1 = from_neighbours(rim1)
    (back1,) = call(functools.partial(back_body, 1), [edge_wide], [], "back")(
        msg_proj, node_cotangent, edge_rows, picks
    )
    (pre1,) = call(functools.partial(own_body, 1), [edge_wide], [table_buf], "own")(
        state1, src_t, dst_t, picks
    )
    act_edges1, grad_pre1, *sends1 = call(
        functools.partial(turn_body, 1), [edge_shape, edge_shape] + [rim_shape] * 4, [full], "turn", True
    )(flags, *rims1, pre1, back1, edge_rows, picks, src_t)

    returned1 = to_neighbours(sends1)
    own_shape = ((2 * nodes, width), BF)
    halves = [((3 * width, width // 2), BF)] * 2
    own1, partial1 = call(functools.partial(sums_body, 1), [own_shape, node_wide], [], "sums")(
        picks, grad_pre1, node_cotangent, src_proj, dst_proj
    )
    act1, node_out = call(functools.partial(out_body, 1), [node_shape, node_shape], [], "out")(
        picks, act_edges1, state1, msg_proj
    )
    keep1, send1 = call(terms_body, halves, [], "terms", True)(
        flags, *rims1, *sends1, state1, own1, act1, node_cotangent
    )
    partial1, keep1, send1 = lax.optimization_barrier((partial1, keep1, send1))
    grad1, grad_pre0, *sends0 = call(
        functools.partial(backward_body, 1),
        [node_wide, edge_shape] + [rim_shape] * 4,
        [],
        "backward",
        True,
    )(flags, *returned1, partial1, src_proj, rim_picks, msg_proj, slope0, picks)

    returned0 = to_neighbours(sends0)
    own0, partial0 = call(functools.partial(sums_body, 0), [own_shape, node_wide], [], "sums")(
        picks, grad_pre0, grad1, src_proj, dst_proj
    )
    keep0, send0 = call(terms_body, halves, [], "terms", True)(
        flags, *rims0, *sends0, state0, own0, act0, grad1
    )
    hidden = enc_out.shape[0]
    keep_enc, send_enc = call(
        functools.partial(last_body, bucket),
        [((fin + hidden, width // 2), BF)] * 2,
        [],
        "last",
        True,
    )(flags, *returned0, partial0, src_proj, rim_picks, packed, enc_out, pooled, col_slope, slot_picks)

    total_rows = 2 * 3 * width + fin + hidden
    share = -(-total_rows // (16 * peers)) * 16
    rows = peers * share
    (merged,) = call(merge_body, [((rows, width // 2), BF)], [], "merge")(
        keep1,
        swapped(send1, "dom", 0),
        keep0,
        swapped(send0, "dom", 0),
        keep_enc,
        swapped(send_enc, "dom", 0),
    )
    parts = exchange(merged.reshape(peers, share, width // 2))
    (spread,) = call(share_body, [((peers, share, width // 2), BF)], [], "share")(parts)
    mine = exchange(spread).reshape(rows, width // 2)
    layer_shape = ((2, width, width), F32)
    grads = call(
        unpack_body,
        [((fin, width), F32), ((hidden, width), F32), layer_shape, layer_shape, layer_shape],
        [],
        "unpack",
        True,
    )(flags, mine, swapped(mine, "dom", 0))
    return (node_out, *grads)


def solution(mesh):
    rows = P(AXES, None)
    flat = P(AXES)
    placed = (rows, flat, flat, flat, rows, flat, flat, flat, flat, flat, P(), P(), P(), P(), P(), rows)
    return jax.shard_map(
        per_device,
        mesh=mesh,
        in_specs=placed,
        out_specs=(rows, P(), P(), P(), P(), P()),
        check_vma=False,
    )
```

```python
import functools

import jax
import jax.numpy as jnp
from jax import lax
from jax.experimental import pallas as pl
from jax.experimental.pallas import tpu as pltpu
from jax.sharding import PartitionSpec as P

AXES = ("grid", "dom")
BF = jnp.bfloat16
F32 = jnp.float32
LANES = 128
TILE = 256
CHUNK = 512
GRANT = 20 << 20


def mm(left_side, right_side):
    return jnp.dot(left_side, right_side, preferred_element_type=F32)


def mm_t(left_side, right_side):
    return lax.dot_general(
        left_side, right_side, (((1,), (1,)), ((), ())), preferred_element_type=F32
    )


def t_mm(left_side, right_side):
    return lax.dot_general(
        left_side, right_side, (((0,), (0,)), ((), ())), preferred_element_type=F32
    )


def put_picks(out_ref, start, indices, count):
    rows = lax.broadcasted_iota(jnp.int32, (TILE, indices.shape[1]), 0).astype(F32).astype(BF)
    for base in range(0, count, TILE):
        shifted = (indices - float(base)).astype(BF)
        block = jnp.where(rows == shifted, jnp.ones((), BF), jnp.zeros((), BF))
        out_ref[start + base : start + base + TILE, :] = block


def sigmoid(values):
    return 0.5 * jnp.tanh(0.5 * values) + 0.5


def call(body, outs, scratch, name, flagged=False, far=()):
    vmem = pl.BlockSpec(memory_space=pltpu.VMEM)

    def run(*args):
        specs = [vmem] * len(args)
        if flagged:
            specs[0] = pl.BlockSpec(memory_space=pltpu.SMEM)
        args = list(args)
        for at in far:
            specs[at] = pl.BlockSpec(memory_space=pltpu.HBM)
            args[at] = pltpu.with_memory_space_constraint(args[at], pltpu.HBM)
        return pl.pallas_call(
            body,
            out_shape=tuple(jax.ShapeDtypeStruct(shape, dtype) for shape, dtype in outs),
            in_specs=specs,
            out_specs=tuple(vmem for _ in outs),
            scratch_shapes=scratch,
            compiler_params=pltpu.CompilerParams(vmem_limit_bytes=GRANT),
            name=name,
        )(*args)

    return run


def chunks(total, body):
    for start in range(0, total, CHUNK):
        body(start, pl.ds(start, CHUNK))


def pack_body(
    where_ref, cols_ref, slot_ref, live_ref, weight_ref, out_ref, slot_buf, live_buf, weight_buf, sems
):
    peers, bucket, _ = cols_ref.shape
    per_row = LANES // bucket
    copies = [
        pltpu.make_async_copy(cols_ref, out_ref.at[:, :bucket, :], sems.at[0]),
        pltpu.make_async_copy(slot_ref, slot_buf, sems.at[1]),
        pltpu.make_async_copy(live_ref, live_buf, sems.at[2]),
        pltpu.make_async_copy(weight_ref, weight_buf, sems.at[3]),
    ]
    for copy in copies[1:] + copies[:1]:
        copy.start()
    for copy in copies[1:]:
        copy.wait()
    slot = slot_buf[...].astype(F32)
    high = jnp.floor(slot * (1.0 / 256.0))
    scale = weight_buf[...] * live_buf[...].astype(F32)
    scale_high = scale.astype(BF).astype(F32)
    fields = [high, slot - 256.0 * high, scale_high, scale - scale_high]
    place = where_ref[PLACE]
    lane = lax.broadcasted_iota(jnp.int32, fields[0].shape, 1)
    here = (lane >= place * bucket) & (lane < (place + 1) * bucket)
    for j in range(per_row):
        shift = lax.rem((place - j + per_row) * bucket, LANES)
        moved = [jnp.where(here, pltpu.roll(field, shift, 1), 0.0).astype(BF) for field in fields]
        for row in range(peers // per_row):
            extra = jnp.concatenate([field[row : row + 1, :] for field in moved], 0)
            out_ref[row * per_row + j, bucket : bucket + 4, :] = extra
    copies[0].wait()


GRID_AT, DOM_AT, GRID_COUNT, DOM_COUNT, PLACE = range(5)


def mark(condition):
    return jnp.where(condition, jnp.float32(1.0), jnp.float32(0.0))


def is_odd(place):
    return lax.rem(place, 2) == 1


def side_marks(where_ref):
    grid_at, dom_at = where_ref[GRID_AT], where_ref[DOM_AT]
    return (
        mark(grid_at > 0),
        mark(grid_at < where_ref[GRID_COUNT] - 1),
        mark(dom_at > 0),
        mark(dom_at < where_ref[DOM_COUNT] - 1),
    )


def pair_marks(where_ref):
    up, down, _, _ = side_marks(where_ref)
    odd = is_odd(where_ref[GRID_AT])
    return jnp.where(odd, up, down), jnp.where(odd, down, up)


def picks_body(
    src_ref,
    dst_ref,
    live_ref,
    weight_ref,
    bound_ref,
    src_proj_ref,
    dst_proj_ref,
    picks_ref,
    rim_picks,
    rim_picks_t,
    scale_ref,
    src_t_ref,
    dst_t_ref,
):
    nodes = rim_picks.shape[0]
    ext = picks_ref.shape[0] - 2 * nodes
    src = long_row(src_ref[...].astype(F32))
    dst = long_row(dst_ref[...].astype(F32))
    scale_ref[...] = long_row(weight_ref[...] * live_ref[...].astype(F32))
    for start in range(0, picks_ref.shape[1], CHUNK):
        block = picks_ref.at[:, pl.ds(start, CHUNK)]
        put_picks(block, 0, dst[:, start : start + CHUNK], nodes)
        put_picks(block, nodes, src[:, start : start + CHUNK], nodes + ext)
    put_picks(rim_picks, 0, long_row(bound_ref[...].astype(F32)), nodes)
    rim_picks_t[...] = turned_over(rim_picks[...])
    for layer in range(src_t_ref.shape[0]):
        src_t_ref[layer] = turned_over(src_proj_ref[layer])
        dst_t_ref[layer] = turned_over(dst_proj_ref[layer])


def put_state(state, state_ref, rim_ref, rim_picks_t):
    state_ref[...] = state.astype(BF)
    rim_ref[...] = mm(rim_picks_t[...], state_ref[...]).astype(BF)


def in_order(where_ref, rims):
    first, second, left, right = (ref[...] for ref in rims)
    odd = is_odd(where_ref[GRID_AT])
    ordered = (jnp.where(odd, first, second), jnp.where(odd, second, first), left, right)
    return [rows * side.astype(BF) for rows, side in zip(ordered, side_marks(where_ref))]


def put_col_rows(packed_ref, bucket, rows_ref):
    peers = packed_ref.shape[0]
    per_row = LANES // bucket
    for row in range(peers // per_row):
        parts = [
            packed_ref[row * per_row + j, bucket : bucket + 4, :].astype(F32) for j in range(per_row)
        ]
        total = sum(parts[1:], parts[0])
        at = pl.ds(row * LANES, LANES)
        rows_ref[0:1, at] = total[0:1] * 256.0 + total[1:2]
        rows_ref[1:2, at] = total[2:3] + total[3:4]


def long_row(rows):
    return jnp.concatenate([rows[i : i + 1, :] for i in range(rows.shape[0])], 1)


def turned_over(rows):
    return rows.astype(F32).T.astype(BF)


def encode_body(
    bucket,
    packed_ref,
    enc_in_far,
    enc_out_far,
    static_far,
    bound_far,
    pooled_ref,
    slope_ref,
    picks_ref,
    state_ref,
    rim_ref,
    act_ref,
    rows_ref,
    enc_in_ref,
    enc_out_ref,
    static_ref,
    bound_ref,
    rim_picks,
    sems,
):
    nodes = static_ref.shape[0]
    peers_step = CHUNK // bucket
    copies = [
        pltpu.make_async_copy(enc_in_far, enc_in_ref, sems.at[0]),
        pltpu.make_async_copy(enc_out_far, enc_out_ref, sems.at[1]),
        pltpu.make_async_copy(static_far, static_ref, sems.at[2]),
        pltpu.make_async_copy(bound_far, bound_ref, sems.at[3]),
    ]
    for copy in copies:
        copy.start()
    put_col_rows(packed_ref, bucket, rows_ref)
    copies[0].wait()
    enc_in_t = turned_over(enc_in_ref[...])

    def step(start, at):
        first = start // bucket
        got = packed_ref[first : first + peers_step, :bucket, :].reshape(CHUNK, packed_ref.shape[2])
        pre = mm_t(enc_in_t, got)
        scale = rows_ref[1:2, at]
        sig = sigmoid(pre)
        act_ref[:, at] = (pre * sig * scale).astype(BF)
        slope_ref[:, at] = (sig * (1.0 + pre * (1.0 - sig)) * scale).astype(BF)
        put_picks(picks_ref.at[:, at], 0, rows_ref[0:1, at], nodes)

    chunks(rows_ref.shape[1], step)
    pooled_ref[...] = mm_t(picks_ref[...], act_ref[...]).astype(BF)
    for copy in copies[1:]:
        copy.wait()
    put_picks(rim_picks, 0, long_row(bound_ref[...].astype(F32)), nodes)
    state = static_ref[...].astype(F32) + mm(pooled_ref[...], enc_out_ref[...])
    state_ref[...] = state.astype(BF)
    rim_ref[...] = t_mm(rim_picks[...], state_ref[...]).astype(BF)


def own_body(layer, state_ref, src_t_ref, dst_t_ref, picks_ref, out_ref, table_ref):
    nodes = state_ref.shape[0]
    held = state_ref[...]
    table_ref[:, :nodes] = mm_t(dst_t_ref[layer], held).astype(BF)
    table_ref[:, nodes:] = mm_t(src_t_ref[layer], held).astype(BF)
    out_ref[...] = mm(table_ref[...], picks_ref[: 2 * nodes, :])


def back_body(layer, msg_ref, grad_ref, scale_ref, picks_ref, out_ref):
    nodes = grad_ref.shape[0]
    back = mm_t(msg_ref[layer], grad_ref[...]).astype(BF)
    out_ref[...] = mm(back, picks_ref[:nodes, :]) * scale_ref[...]


def fill_rims(full_ref, where_ref, rims, src_t_ref):
    rim = rims[0].shape[0]
    for side, rim_rows in enumerate(in_order(where_ref, rims)):
        full_ref[:, side * rim : (side + 1) * rim] = mm_t(src_t_ref[...], rim_rows).astype(BF)


def forward_body(
    layer,
    where_ref,
    first_ref,
    second_ref,
    left_ref,
    right_ref,
    own_pre_ref,
    scale_ref,
    picks_ref,
    state_ref,
    src_t_ref,
    msg_ref,
    rim_picks_t,
    slope_ref,
    node_act_ref,
    next_state_ref,
    rim_ref,
    full_ref,
    act_ref,
):
    nodes = state_ref.shape[0]
    fill_rims(full_ref, where_ref, (first_ref, second_ref, left_ref, right_ref), src_t_ref.at[layer])

    def step(start, at):
        pre = own_pre_ref[:, at] + mm(full_ref[...], picks_ref[2 * nodes :, at])
        scale = scale_ref[:, at]
        sig = sigmoid(pre)
        act_ref[:, at] = (pre * sig * scale).astype(BF)
        slope_ref[:, at] = (sig * (1.0 + pre * (1.0 - sig)) * scale).astype(BF)

    chunks(scale_ref.shape[1], step)
    node_act_ref[...] = mm_t(picks_ref[:nodes, :], act_ref[...]).astype(BF)
    state = state_ref[...].astype(F32) + mm(node_act_ref[...], msg_ref[layer])
    put_state(state, next_state_ref, rim_ref, rim_picks_t)


def put_sends(where_ref, sums, sends):
    rim = sums.shape[0] // 4
    up, down, left, right = (sums[side * rim : (side + 1) * rim, :].astype(BF) for side in range(4))
    odd = is_odd(where_ref[GRID_AT])
    sends[0][...] = jnp.where(odd, up, down)
    sends[1][...] = jnp.where(odd, down, up)
    sends[2][...] = left
    sends[3][...] = right


def turn_body(
    layer,
    where_ref,
    first_ref,
    second_ref,
    left_ref,
    right_ref,
    own_pre_ref,
    back_ref,
    scale_ref,
    picks_ref,
    src_t_ref,
    act_ref,
    grad_pre_ref,
    send0_ref,
    send1_ref,
    send2_ref,
    send3_ref,
    full_ref,
):
    first = picks_ref.shape[0] - full_ref.shape[1]
    fill_rims(full_ref, where_ref, (first_ref, second_ref, left_ref, right_ref), src_t_ref.at[layer])

    def step(start, at):
        pre = own_pre_ref[:, at] + mm(full_ref[...], picks_ref[first:, at])
        sig = sigmoid(pre)
        act_ref[:, at] = (pre * sig * scale_ref[:, at]).astype(BF)
        grad_pre_ref[:, at] = (back_ref[:, at] * (sig * (1.0 + pre * (1.0 - sig)))).astype(BF)

    chunks(scale_ref.shape[1], step)
    sums = mm_t(picks_ref[first:, :], grad_pre_ref[...])
    put_sends(where_ref, sums, (send0_ref, send1_ref, send2_ref, send3_ref))


def merged_grad(partial_ref, where_ref, returned, src_ref, rim_picks):
    sides = side_marks(where_ref)
    marks = (*pair_marks(where_ref), sides[3], sides[2])
    total = returned[0][...].astype(F32) * marks[0]
    for side in range(1, 4):
        total += returned[side][...].astype(F32) * marks[side]
    back = mm(rim_picks[...], total.astype(BF)).astype(BF)
    return partial_ref[...] + mm_t(back, src_ref[...])


def backward_body(
    layer,
    where_ref,
    first_ref,
    second_ref,
    left_ref,
    right_ref,
    partial_ref,
    src_ref,
    rim_picks,
    msg_ref,
    slope_ref,
    picks_ref,
    grad_ref,
    grad_pre_ref,
    send0_ref,
    send1_ref,
    send2_ref,
    send3_ref,
):
    nodes = partial_ref.shape[0]
    returned = (first_ref, second_ref, left_ref, right_ref)
    grad = merged_grad(partial_ref, where_ref, returned, src_ref.at[layer], rim_picks)
    grad_ref[...] = grad
    back = mm_t(msg_ref[layer - 1], grad.astype(BF)).astype(BF)

    def step(start, at):
        grad_pre = mm(back, picks_ref[:nodes, at]) * slope_ref[:, at].astype(F32)
        grad_pre_ref[:, at] = grad_pre.astype(BF)

    chunks(picks_ref.shape[1], step)
    sums = mm_t(picks_ref[2 * nodes :, :], grad_pre_ref[...])
    put_sends(where_ref, sums, (send0_ref, send1_ref, send2_ref, send3_ref))


def sums_body(layer, picks_ref, grad_pre_ref, grad_ref, src_ref, dst_ref, own_ref, partial_ref):
    nodes = grad_ref.shape[0]
    own_ref[...] = mm_t(picks_ref[: 2 * nodes, :], grad_pre_ref[...]).astype(BF)
    partial_ref[...] = (
        grad_ref[...].astype(F32)
        + mm_t(own_ref[:nodes, :], dst_ref[layer])
        + mm_t(own_ref[nodes:, :], src_ref[layer])
    )


def out_body(layer, picks_ref, act_edges_ref, state_ref, msg_ref, act_ref, out_ref):
    nodes = state_ref.shape[0]
    act_ref[...] = mm_t(picks_ref[:nodes, :], act_edges_ref[...]).astype(BF)
    out_ref[...] = (state_ref[...].astype(F32) + mm(act_ref[...], msg_ref[layer])).astype(BF)


def put_halves(where_ref, first, term, keep_ref, send_ref):
    half = term.shape[1] // 2
    odd = is_odd(where_ref[DOM_AT])
    low, high = term[:, :half].astype(BF), term[:, half:].astype(BF)
    keep_ref[first : first + term.shape[0], :] = jnp.where(odd, high, low)
    send_ref[first : first + term.shape[0], :] = jnp.where(odd, low, high)


def terms_body(
    where_ref,
    first_ref,
    second_ref,
    left_ref,
    right_ref,
    send0_ref,
    send1_ref,
    send2_ref,
    send3_ref,
    state_ref,
    own_ref,
    act_ref,
    grad_ref,
    keep_ref,
    send_ref,
):
    nodes, width = state_ref.shape
    state = state_ref[...]
    src_term = t_mm(state, own_ref[nodes:, :])
    marks = (*pair_marks(where_ref), *side_marks(where_ref)[2:])
    rims = (first_ref, second_ref, left_ref, right_ref)
    sends = (send0_ref, send1_ref, send2_ref, send3_ref)
    for rim_ref, sums_ref, present in zip(rims, sends, marks):
        src_term += t_mm(rim_ref[...], sums_ref[...]) * present
    put_halves(where_ref, 0, src_term, keep_ref, send_ref)
    put_halves(where_ref, width, t_mm(state, own_ref[:nodes, :]), keep_ref, send_ref)
    put_halves(
        where_ref, 2 * width, t_mm(act_ref[...], grad_ref[...].astype(BF)), keep_ref, send_ref
    )


def last_body(
    bucket,
    where_ref,
    first_ref,
    second_ref,
    left_ref,
    right_ref,
    partial_ref,
    src_ref,
    rim_picks,
    packed_ref,
    enc_out_ref,
    pooled_ref,
    slope_ref,
    picks_ref,
    keep_ref,
    send_ref,
):
    fin = packed_ref.shape[2]
    peers_step = CHUNK // bucket
    returned = (first_ref, second_ref, left_ref, right_ref)
    grad = merged_grad(partial_ref, where_ref, returned, src_ref.at[0], rim_picks).astype(BF)
    back = mm_t(enc_out_ref[...], grad).astype(BF)
    in_term = jnp.zeros((enc_out_ref.shape[0], fin), F32)
    for start in range(0, picks_ref.shape[1], CHUNK):
        at = pl.ds(start, CHUNK)
        first = start // bucket
        got = packed_ref[first : first + peers_step, :bucket, :].reshape(CHUNK, fin)
        grad_pre = mm(back, picks_ref[:, at]) * slope_ref[:, at].astype(F32)
        in_term += mm(grad_pre.astype(BF), got)
    put_halves(where_ref, 0, in_term.T, keep_ref, send_ref)
    put_halves(where_ref, fin, t_mm(pooled_ref[...], grad), keep_ref, send_ref)


def merge_body(*refs):
    out_ref = refs[-1]
    first = 0
    for keep_ref, got_ref in zip(refs[:-1:2], refs[1:-1:2]):
        rows = keep_ref.shape[0]
        total = keep_ref[...].astype(F32) + got_ref[...].astype(F32)
        out_ref[first : first + rows, :] = total.astype(BF)
        first += rows
    if first < out_ref.shape[0]:
        out_ref[first:, :] = jnp.zeros((out_ref.shape[0] - first, out_ref.shape[1]), BF)


def share_body(parts_ref, out_ref):
    count = parts_ref.shape[0]
    for odd in range(2):
        total = parts_ref[odd].astype(F32)
        for peer in range(odd + 2, count, 2):
            total += parts_ref[peer].astype(F32)
        for peer in range(odd, count, 2):
            out_ref[peer] = total.astype(BF)


def unpack_body(where_ref, mine_ref, other_ref, *outs):
    odd = is_odd(where_ref[DOM_AT])
    half = mine_ref.shape[1]
    first = 0

    def put(ref, rows):
        nonlocal first
        mine = mine_ref[first : first + rows, :].astype(F32)
        other = other_ref[first : first + rows, :].astype(F32)
        ref[:, :half] = jnp.where(odd, other, mine)
        ref[:, half:] = jnp.where(odd, mine, other)
        first += rows

    enc_in_ref, enc_out_ref, *layer_refs = outs
    for layer in reversed(range(layer_refs[0].shape[0])):
        for ref in layer_refs:
            put(ref.at[layer], ref.shape[1])
    put(enc_in_ref, enc_in_ref.shape[0])
    put(enc_out_ref, enc_out_ref.shape[0])


def exchange(shard):
    return lax.all_to_all(shard, AXES, split_axis=0, concat_axis=0, tiled=True)


def turned(shard, axis, by):
    count = lax.axis_size(axis)
    return lax.ppermute(shard, axis, [(i, (i + by) % count) for i in range(count)])


def swapped(shard, axis, offset):
    count = lax.axis_size(axis)
    partner = list(range(count))
    for i in range(offset, count - 1, 2):
        partner[i], partner[i + 1] = i + 1, i
    return lax.ppermute(shard, axis, list(enumerate(partner)))


def from_neighbours(rim_rows):
    return (
        swapped(rim_rows, "grid", 0),
        swapped(rim_rows, "grid", 1),
        turned(rim_rows, "dom", 1),
        turned(rim_rows, "dom", -1),
    )


def to_neighbours(sends):
    return (
        swapped(sends[0], "grid", 0),
        swapped(sends[1], "grid", 1),
        turned(sends[2], "dom", -1),
        turned(sends[3], "dom", 1),
    )


def per_device(
    columns,
    column_live,
    col_weight,
    col_slot,
    node_static,
    boundary_idx,
    edge_src,
    edge_dst,
    edge_live,
    edge_weight,
    enc_in,
    enc_out,
    src_proj,
    dst_proj,
    msg_proj,
    node_cotangent,
):
    peers = lax.axis_size(AXES)
    cols, fin = columns.shape
    nodes, width = node_static.shape
    rim = boundary_idx.shape[0]
    edges = edge_src.shape[0]
    ext = 4 * rim
    bucket = cols // peers

    grid_at, grid_count = lax.axis_index("grid"), lax.axis_size("grid")
    dom_at, dom_count = lax.axis_index("dom"), lax.axis_size("dom")
    place = (grid_at * dom_count + dom_at) % (LANES // bucket)
    where = jnp.stack([grid_at, dom_at, jnp.int32(grid_count), jnp.int32(dom_count), place])

    lanes = (cols // LANES, LANES)
    held = [pltpu.VMEM(lanes, jnp.int32), pltpu.VMEM(lanes, jnp.int32), pltpu.VMEM(lanes, F32)]
    (packed,) = call(
        pack_body,
        [((peers, bucket + 4, fin), BF)],
        held + [pltpu.SemaphoreType.DMA((4,))],
        "pack",
        True,
        far=range(1, 5),
    )(
        where,
        columns.reshape(peers, bucket, fin),
        col_slot.reshape(lanes),
        column_live.reshape(lanes),
        col_weight.reshape(lanes),
    )
    packed = exchange(packed)

    node_shape = ((nodes, width), BF)
    node_wide = ((nodes, width), F32)
    rim_shape = ((rim, width), BF)
    edge_shape = ((width, edges), BF)
    edge_wide = ((width, edges), F32)
    full = pltpu.VMEM((width, ext), BF)
    edge_buf = pltpu.VMEM((width, edges), BF)
    table_buf = pltpu.VMEM((width, 2 * nodes), BF)

    bound = boundary_idx.reshape(rim // LANES, LANES)
    pooled, col_slope, slot_picks, state0, rim0 = call(
        functools.partial(encode_body, bucket),
        [node_shape, ((width, cols), BF), ((nodes, cols), BF), node_shape, rim_shape],
        [
            edge_buf,
            pltpu.VMEM((2, cols), F32),
            pltpu.VMEM(enc_in.shape, BF),
            pltpu.VMEM(enc_out.shape, BF),
            pltpu.VMEM((nodes, width), BF),
            pltpu.VMEM(bound.shape, jnp.int32),
            pltpu.VMEM((nodes, rim), BF),
            pltpu.SemaphoreType.DMA((4,)),
        ],
        "encode",
        far=range(1, 5),
    )(packed, enc_in, enc_out, node_static, bound)

    edge_lanes = (edges // LANES, LANES)
    state0, edge_dst = lax.optimization_barrier((state0, edge_dst))
    layered = (src_proj.shape, BF)
    picks, rim_picks, rim_picks_t, edge_scale, src_t, dst_t = call(
        picks_body,
        [
            ((2 * nodes + ext, edges), BF),
            ((nodes, rim), BF),
            ((rim, nodes), BF),
            ((1, edges), F32),
            layered,
            layered,
        ],
        [],
        "picks",
    )(
        edge_src.reshape(edge_lanes),
        edge_dst.reshape(edge_lanes),
        edge_live.reshape(edge_lanes),
        edge_weight.reshape(edge_lanes),
        bound,
        src_proj,
        dst_proj,
    )

    rims0 = from_neighbours(rim0)
    (pre0,) = call(functools.partial(own_body, 0), [edge_wide], [table_buf], "own")(
        state0, src_t, dst_t, picks
    )
    slope0, act0, state1, rim1 = call(
        functools.partial(forward_body, 0),
        [edge_shape, node_shape, node_shape, rim_shape],
        [full, edge_buf],
        "forward",
        True,
    )(where, *rims0, pre0, edge_scale, picks, state0, src_t, msg_proj, rim_picks_t)

    rims1 = from_neighbours(rim1)
    (back1,) = call(functools.partial(back_body, 1), [edge_wide], [], "back")(
        msg_proj, node_cotangent, edge_scale, picks
    )
    (pre1,) = call(functools.partial(own_body, 1), [edge_wide], [table_buf], "own")(
        state1, src_t, dst_t, picks
    )
    act_edges1, grad_pre1, *sends1 = call(
        functools.partial(turn_body, 1), [edge_shape, edge_shape] + [rim_shape] * 4, [full], "turn", True
    )(where, *rims1, pre1, back1, edge_scale, picks, src_t)

    returned1 = to_neighbours(sends1)
    own_shape = ((2 * nodes, width), BF)
    halves = [((3 * width, width // 2), BF)] * 2
    own1, partial1 = call(functools.partial(sums_body, 1), [own_shape, node_wide], [], "sums")(
        picks, grad_pre1, node_cotangent, src_proj, dst_proj
    )
    act1, node_out = call(functools.partial(out_body, 1), [node_shape, node_shape], [], "out")(
        picks, act_edges1, state1, msg_proj
    )
    keep1, send1 = call(terms_body, halves, [], "terms", True)(
        where, *rims1, *sends1, state1, own1, act1, node_cotangent
    )
    partial1, keep1, send1 = lax.optimization_barrier((partial1, keep1, send1))
    grad1, grad_pre0, *sends0 = call(
        functools.partial(backward_body, 1),
        [node_wide, edge_shape] + [rim_shape] * 4,
        [],
        "backward",
        True,
    )(where, *returned1, partial1, src_proj, rim_picks, msg_proj, slope0, picks)

    returned0 = to_neighbours(sends0)
    own0, partial0 = call(functools.partial(sums_body, 0), [own_shape, node_wide], [], "sums")(
        picks, grad_pre0, grad1, src_proj, dst_proj
    )
    keep0, send0 = call(terms_body, halves, [], "terms", True)(
        where, *rims0, *sends0, state0, own0, act0, grad1
    )
    hidden = enc_out.shape[0]
    keep_enc, send_enc = call(
        functools.partial(last_body, bucket),
        [((fin + hidden, width // 2), BF)] * 2,
        [],
        "last",
        True,
    )(where, *returned0, partial0, src_proj, rim_picks, packed, enc_out, pooled, col_slope, slot_picks)

    total_rows = 2 * 3 * width + fin + hidden
    share = -(-total_rows // (16 * peers)) * 16
    rows = peers * share
    (merged,) = call(merge_body, [((rows, width // 2), BF)], [], "merge")(
        keep1,
        swapped(send1, "dom", 0),
        keep0,
        swapped(send0, "dom", 0),
        keep_enc,
        swapped(send_enc, "dom", 0),
    )
    parts = exchange(merged.reshape(peers, share, width // 2))
    (spread,) = call(share_body, [((peers, share, width // 2), BF)], [], "share")(parts)
    mine = exchange(spread).reshape(rows, width // 2)
    layer_shape = ((2, width, width), F32)
    grads = call(
        unpack_body,
        [((fin, width), F32), ((hidden, width), F32), layer_shape, layer_shape, layer_shape],
        [],
        "unpack",
        True,
    )(where, mine, swapped(mine, "dom", 0))
    return (node_out, *grads)


def solution(mesh):
    rows = P(AXES, None)
    flat = P(AXES)
    placed = (rows, flat, flat, flat, rows, flat, flat, flat, flat, flat, P(), P(), P(), P(), P(), rows)
    return jax.shard_map(
        per_device,
        mesh=mesh,
        in_specs=placed,
        out_specs=(rows, P(), P(), P(), P(), P()),
        check_vma=False,
    )
```

```python
import functools

import jax
import jax.numpy as jnp
from jax import lax
from jax.experimental import pallas as pl
from jax.experimental.pallas import tpu as pltpu
from jax.sharding import PartitionSpec as P

AXES = ("grid", "dom")
BF = jnp.bfloat16
F32 = jnp.float32
LANES = 128
TILE = 256
CHUNK = 512
GRANT = 20 << 20


def mm(left_side, right_side):
    return jnp.dot(left_side, right_side, preferred_element_type=F32)


def mm_t(left_side, right_side):
    return lax.dot_general(
        left_side, right_side, (((1,), (1,)), ((), ())), preferred_element_type=F32
    )


def t_mm(left_side, right_side):
    return lax.dot_general(
        left_side, right_side, (((0,), (0,)), ((), ())), preferred_element_type=F32
    )


def put_picks(out_ref, start, indices, count):
    rows = lax.broadcasted_iota(jnp.int32, (TILE, indices.shape[1]), 0).astype(F32).astype(BF)
    for base in range(0, count, TILE):
        shifted = (indices - float(base)).astype(BF)
        block = jnp.where(rows == shifted, jnp.ones((), BF), jnp.zeros((), BF))
        out_ref[start + base : start + base + TILE, :] = block


def sigmoid(values):
    return 0.5 * jnp.tanh(0.5 * values) + 0.5


def call(body, outs, scratch, name, flagged=False, far=()):
    vmem = pl.BlockSpec(memory_space=pltpu.VMEM)

    def run(*args):
        specs = [vmem] * len(args)
        if flagged:
            specs[0] = pl.BlockSpec(memory_space=pltpu.SMEM)
        args = list(args)
        for at in far:
            specs[at] = pl.BlockSpec(memory_space=pltpu.HBM)
            args[at] = pltpu.with_memory_space_constraint(args[at], pltpu.HBM)
        return pl.pallas_call(
            body,
            out_shape=tuple(jax.ShapeDtypeStruct(shape, dtype) for shape, dtype in outs),
            in_specs=specs,
            out_specs=tuple(vmem for _ in outs),
            scratch_shapes=scratch,
            compiler_params=pltpu.CompilerParams(vmem_limit_bytes=GRANT),
            name=name,
        )(*args)

    return run


def chunks(total, body):
    for start in range(0, total, CHUNK):
        body(start, pl.ds(start, CHUNK))


def pack_body(
    where_ref, cols_ref, slot_ref, live_ref, weight_ref, out_ref, slot_buf, live_buf, weight_buf, sems
):
    peers, bucket, _ = cols_ref.shape
    per_row = LANES // bucket
    copies = [
        pltpu.make_async_copy(cols_ref, out_ref.at[:, :bucket, :], sems.at[0]),
        pltpu.make_async_copy(slot_ref, slot_buf, sems.at[1]),
        pltpu.make_async_copy(live_ref, live_buf, sems.at[2]),
        pltpu.make_async_copy(weight_ref, weight_buf, sems.at[3]),
    ]
    for copy in copies[1:] + copies[:1]:
        copy.start()
    for copy in copies[1:]:
        copy.wait()
    slot = slot_buf[...].astype(F32)
    high = jnp.floor(slot * (1.0 / 256.0))
    scale = weight_buf[...] * live_buf[...].astype(F32)
    scale_high = scale.astype(BF).astype(F32)
    fields = [high, slot - 256.0 * high, scale_high, scale - scale_high]
    place = where_ref[PLACE]
    lane = lax.broadcasted_iota(jnp.int32, fields[0].shape, 1)
    here = (lane >= place * bucket) & (lane < (place + 1) * bucket)
    for j in range(per_row):
        shift = lax.rem((place - j + per_row) * bucket, LANES)
        moved = [jnp.where(here, pltpu.roll(field, shift, 1), 0.0).astype(BF) for field in fields]
        for row in range(peers // per_row):
            extra = jnp.concatenate([field[row : row + 1, :] for field in moved], 0)
            out_ref[row * per_row + j, bucket : bucket + 4, :] = extra
    copies[0].wait()


GRID_AT, DOM_AT, GRID_COUNT, DOM_COUNT, PLACE = range(5)


def mark(condition):
    return jnp.where(condition, jnp.float32(1.0), jnp.float32(0.0))


def is_odd(place):
    return lax.rem(place, 2) == 1


def side_marks(where_ref):
    grid_at, dom_at = where_ref[GRID_AT], where_ref[DOM_AT]
    return (
        mark(grid_at > 0),
        mark(grid_at < where_ref[GRID_COUNT] - 1),
        mark(dom_at > 0),
        mark(dom_at < where_ref[DOM_COUNT] - 1),
    )


def pair_marks(where_ref):
    up, down, _, _ = side_marks(where_ref)
    odd = is_odd(where_ref[GRID_AT])
    return jnp.where(odd, up, down), jnp.where(odd, down, up)


def picks_body(
    src_ref,
    dst_ref,
    live_ref,
    weight_ref,
    bound_ref,
    src_proj_ref,
    dst_proj_ref,
    picks_ref,
    rim_picks,
    rim_picks_t,
    scale_ref,
    src_t_ref,
    dst_t_ref,
):
    nodes, rim = rim_picks.shape
    src = long_row(src_ref[...].astype(F32))
    dst = long_row(dst_ref[...].astype(F32))
    scale_ref[...] = long_row(weight_ref[...] * live_ref[...].astype(F32))
    for start in range(0, picks_ref.shape[1], CHUNK):
        block = picks_ref.at[:, pl.ds(start, CHUNK)]
        here = src[:, start : start + CHUNK]
        put_picks(block, 0, here - float(nodes), 2 * rim)
        put_picks(block, 2 * rim, dst[:, start : start + CHUNK], nodes)
        put_picks(block, 2 * rim + nodes, here, nodes)
        put_picks(block, 2 * rim + 2 * nodes, here - float(nodes + 2 * rim), 2 * rim)
    put_picks(rim_picks, 0, long_row(bound_ref[...].astype(F32)), nodes)
    rim_picks_t[...] = turned_over(rim_picks[...])
    for layer in range(src_t_ref.shape[0]):
        src_t_ref[layer] = turned_over(src_proj_ref[layer])
        dst_t_ref[layer] = turned_over(dst_proj_ref[layer])


def put_state(state, state_ref, rim_ref, rim_picks_t):
    state_ref[...] = state.astype(BF)
    rim_ref[...] = mm(rim_picks_t[...], state_ref[...]).astype(BF)


def grid_rims(where_ref, first_ref, second_ref):
    odd = is_odd(where_ref[GRID_AT])
    up, down, _, _ = side_marks(where_ref)
    first, second = first_ref[...], second_ref[...]
    return (
        jnp.where(odd, first, second) * up.astype(BF),
        jnp.where(odd, second, first) * down.astype(BF),
    )


def dom_rims(where_ref, left_ref, right_ref):
    _, _, left, right = side_marks(where_ref)
    return left_ref[...] * left.astype(BF), right_ref[...] * right.astype(BF)


def put_col_rows(packed_ref, bucket, rows_ref):
    peers = packed_ref.shape[0]
    per_row = LANES // bucket
    for row in range(peers // per_row):
        parts = [
            packed_ref[row * per_row + j, bucket : bucket + 4, :].astype(F32) for j in range(per_row)
        ]
        total = sum(parts[1:], parts[0])
        at = pl.ds(row * LANES, LANES)
        rows_ref[0:1, at] = total[0:1] * 256.0 + total[1:2]
        rows_ref[1:2, at] = total[2:3] + total[3:4]


def long_row(rows):
    return jnp.concatenate([rows[i : i + 1, :] for i in range(rows.shape[0])], 1)


def turned_over(rows):
    return rows.astype(F32).T.astype(BF)


def encode_body(
    bucket,
    packed_ref,
    enc_in_ref,
    enc_out_ref,
    static_ref,
    bound_ref,
    pooled_ref,
    slope_ref,
    picks_ref,
    state_ref,
    rim_ref,
    act_ref,
    rows_ref,
    rim_picks,
):
    nodes = static_ref.shape[0]
    peers_step = CHUNK // bucket
    put_col_rows(packed_ref, bucket, rows_ref)
    enc_in_t = turned_over(enc_in_ref[...])

    def step(start, at):
        first = start // bucket
        got = packed_ref[first : first + peers_step, :bucket, :].reshape(CHUNK, packed_ref.shape[2])
        pre = mm_t(enc_in_t, got)
        scale = rows_ref[1:2, at]
        sig = sigmoid(pre)
        act_ref[:, at] = (pre * sig * scale).astype(BF)
        slope_ref[:, at] = (sig * (1.0 + pre * (1.0 - sig)) * scale).astype(BF)
        put_picks(picks_ref.at[:, at], 0, rows_ref[0:1, at], nodes)

    chunks(rows_ref.shape[1], step)
    pooled_ref[...] = mm_t(picks_ref[...], act_ref[...]).astype(BF)
    put_picks(rim_picks, 0, long_row(bound_ref[...].astype(F32)), nodes)
    state = static_ref[...].astype(F32) + mm(pooled_ref[...], enc_out_ref[...])
    state_ref[...] = state.astype(BF)
    rim_ref[...] = t_mm(rim_picks[...], state_ref[...]).astype(BF)


def own_body(
    layer, where_ref, left_ref, right_ref, state_ref, src_t_ref, dst_t_ref, picks_ref, out_ref, table_ref
):
    nodes = state_ref.shape[0]
    rim = left_ref.shape[0]
    held = state_ref[...]
    table_ref[:, :nodes] = mm_t(dst_t_ref[layer], held).astype(BF)
    table_ref[:, nodes : 2 * nodes] = mm_t(src_t_ref[layer], held).astype(BF)
    for side, rim_rows in enumerate(dom_rims(where_ref, left_ref, right_ref)):
        start = 2 * nodes + side * rim
        table_ref[:, start : start + rim] = mm_t(src_t_ref[layer], rim_rows).astype(BF)
    out_ref[...] = mm(table_ref[...], picks_ref[2 * rim :, :])


def by_target(picks_ref, nodes):
    return pl.ds((picks_ref.shape[0] - 2 * nodes) // 2, nodes)


def back_body(layer, msg_ref, grad_ref, scale_ref, picks_ref, out_ref):
    nodes = grad_ref.shape[0]
    back = mm_t(msg_ref[layer], grad_ref[...]).astype(BF)
    out_ref[...] = mm(back, picks_ref[by_target(picks_ref, nodes), :]) * scale_ref[...]


def fill_rims(full_ref, rims, src_t_ref):
    rim = rims[0].shape[0]
    for side, rim_rows in enumerate(rims):
        full_ref[:, side * rim : (side + 1) * rim] = mm_t(src_t_ref[...], rim_rows).astype(BF)


def forward_body(
    layer,
    where_ref,
    first_ref,
    second_ref,
    own_pre_ref,
    scale_ref,
    picks_ref,
    state_ref,
    src_t_ref,
    msg_ref,
    rim_picks_t,
    slope_ref,
    node_act_ref,
    next_state_ref,
    rim_ref,
    full_ref,
    act_ref,
):
    nodes = state_ref.shape[0]
    rims = grid_rims(where_ref, first_ref, second_ref)
    fill_rims(full_ref, rims, src_t_ref.at[layer])
    sides = pl.ds(0, full_ref.shape[1])

    def step(start, at):
        pre = own_pre_ref[:, at] + mm(full_ref[...], picks_ref[sides, at])
        scale = scale_ref[:, at]
        sig = sigmoid(pre)
        act_ref[:, at] = (pre * sig * scale).astype(BF)
        slope_ref[:, at] = (sig * (1.0 + pre * (1.0 - sig)) * scale).astype(BF)

    chunks(scale_ref.shape[1], step)
    node_act_ref[...] = mm_t(picks_ref[by_target(picks_ref, nodes), :], act_ref[...]).astype(BF)
    state = state_ref[...].astype(F32) + mm(node_act_ref[...], msg_ref[layer])
    put_state(state, next_state_ref, rim_ref, rim_picks_t)


def put_grid_sends(where_ref, sums, first_ref, second_ref):
    rim = sums.shape[0] // 2
    up, down = sums[:rim, :].astype(BF), sums[rim:, :].astype(BF)
    odd = is_odd(where_ref[GRID_AT])
    first_ref[...] = jnp.where(odd, up, down)
    second_ref[...] = jnp.where(odd, down, up)


def dom_sums_body(picks_ref, grad_pre_ref, left_ref, right_ref):
    rim = left_ref.shape[0]
    first = picks_ref.shape[0] - 2 * rim
    left_ref[...] = mm_t(picks_ref[first : first + rim, :], grad_pre_ref[...]).astype(BF)
    right_ref[...] = mm_t(picks_ref[first + rim :, :], grad_pre_ref[...]).astype(BF)


def turn_body(
    layer,
    where_ref,
    first_ref,
    second_ref,
    own_pre_ref,
    back_ref,
    scale_ref,
    picks_ref,
    src_t_ref,
    act_ref,
    grad_pre_ref,
    send0_ref,
    send1_ref,
    full_ref,
):
    rim = first_ref.shape[0]
    rims = grid_rims(where_ref, first_ref, second_ref)
    fill_rims(full_ref, rims, src_t_ref.at[layer])
    sides = pl.ds(0, 2 * rim)

    def step(start, at):
        pre = own_pre_ref[:, at] + mm(full_ref[...], picks_ref[sides, at])
        sig = sigmoid(pre)
        act_ref[:, at] = (pre * sig * scale_ref[:, at]).astype(BF)
        grad_pre_ref[:, at] = (back_ref[:, at] * (sig * (1.0 + pre * (1.0 - sig)))).astype(BF)

    chunks(scale_ref.shape[1], step)
    sums = mm_t(picks_ref[sides, :], grad_pre_ref[...])
    put_grid_sends(where_ref, sums, send0_ref, send1_ref)


def merged_grad(partial_ref, where_ref, returned, src_ref, rim_picks):
    sides = side_marks(where_ref)
    marks = (*pair_marks(where_ref), sides[3], sides[2])
    total = returned[0][...].astype(F32) * marks[0]
    for side in range(1, 4):
        total += returned[side][...].astype(F32) * marks[side]
    back = mm(rim_picks[...], total.astype(BF)).astype(BF)
    return partial_ref[...] + mm_t(back, src_ref[...])


def backward_body(
    layer,
    where_ref,
    first_ref,
    second_ref,
    left_ref,
    right_ref,
    partial_ref,
    src_ref,
    rim_picks,
    msg_ref,
    slope_ref,
    picks_ref,
    grad_ref,
    grad_pre_ref,
    send0_ref,
    send1_ref,
):
    nodes = partial_ref.shape[0]
    returned = (first_ref, second_ref, left_ref, right_ref)
    grad = merged_grad(partial_ref, where_ref, returned, src_ref.at[layer], rim_picks)
    grad_ref[...] = grad
    back = mm_t(msg_ref[layer - 1], grad.astype(BF)).astype(BF)

    def step(start, at):
        grad_pre = mm(back, picks_ref[by_target(picks_ref, nodes), at]) * slope_ref[:, at].astype(F32)
        grad_pre_ref[:, at] = grad_pre.astype(BF)

    chunks(picks_ref.shape[1], step)
    sides = pl.ds(0, 2 * first_ref.shape[0])
    sums = mm_t(picks_ref[sides, :], grad_pre_ref[...])
    put_grid_sends(where_ref, sums, send0_ref, send1_ref)


def sums_body(layer, picks_ref, grad_pre_ref, grad_ref, src_ref, dst_ref, own_ref, partial_ref):
    nodes = grad_ref.shape[0]
    first = by_target(picks_ref, nodes).start
    own_ref[...] = mm_t(picks_ref[first : first + 2 * nodes, :], grad_pre_ref[...]).astype(BF)
    partial_ref[...] = (
        grad_ref[...].astype(F32)
        + mm_t(own_ref[:nodes, :], dst_ref[layer])
        + mm_t(own_ref[nodes:, :], src_ref[layer])
    )


def out_body(layer, picks_ref, act_edges_ref, state_ref, msg_ref, act_ref, out_ref):
    nodes = state_ref.shape[0]
    act_ref[...] = mm_t(picks_ref[by_target(picks_ref, nodes), :], act_edges_ref[...]).astype(BF)
    out_ref[...] = (state_ref[...].astype(F32) + mm(act_ref[...], msg_ref[layer])).astype(BF)


def put_halves(where_ref, first, term, keep_ref, send_ref):
    half = term.shape[1] // 2
    odd = is_odd(where_ref[DOM_AT])
    low, high = term[:, :half].astype(BF), term[:, half:].astype(BF)
    keep_ref[first : first + term.shape[0], :] = jnp.where(odd, high, low)
    send_ref[first : first + term.shape[0], :] = jnp.where(odd, low, high)


def terms_body(where_ref, *refs):
    keep_ref, send_ref = refs[-2:]
    marks = (*pair_marks(where_ref), *side_marks(where_ref)[2:])
    for layer in range(len(refs) // 12):
        held = refs[12 * layer : 12 * layer + 12]
        rims, sends, (state_ref, own_ref, act_ref, grad_ref) = held[:4], held[4:8], held[8:]
        nodes, width = state_ref.shape
        first = 3 * width * layer
        state = state_ref[...]
        src_term = t_mm(state, own_ref[nodes:, :])
        for rim_ref, sums_ref, present in zip(rims, sends, marks):
            src_term += t_mm(rim_ref[...], sums_ref[...]) * present
        put_halves(where_ref, first, src_term, keep_ref, send_ref)
        put_halves(where_ref, first + width, t_mm(state, own_ref[:nodes, :]), keep_ref, send_ref)
        msg_term = t_mm(act_ref[...], grad_ref[...].astype(BF))
        put_halves(where_ref, first + 2 * width, msg_term, keep_ref, send_ref)


def last_body(
    bucket,
    where_ref,
    first_ref,
    second_ref,
    left_ref,
    right_ref,
    partial_ref,
    src_ref,
    rim_picks,
    packed_ref,
    enc_out_ref,
    pooled_ref,
    slope_ref,
    picks_ref,
    keep_ref,
    send_ref,
):
    fin = packed_ref.shape[2]
    peers_step = CHUNK // bucket
    returned = (first_ref, second_ref, left_ref, right_ref)
    grad = merged_grad(partial_ref, where_ref, returned, src_ref.at[0], rim_picks).astype(BF)
    back = mm_t(enc_out_ref[...], grad).astype(BF)
    in_term = jnp.zeros((enc_out_ref.shape[0], fin), F32)
    for start in range(0, picks_ref.shape[1], CHUNK):
        at = pl.ds(start, CHUNK)
        first = start // bucket
        got = packed_ref[first : first + peers_step, :bucket, :].reshape(CHUNK, fin)
        grad_pre = mm(back, picks_ref[:, at]) * slope_ref[:, at].astype(F32)
        in_term += mm(grad_pre.astype(BF), got)
    put_halves(where_ref, 0, in_term.T, keep_ref, send_ref)
    put_halves(where_ref, fin, t_mm(pooled_ref[...], grad), keep_ref, send_ref)


def merge_body(*refs):
    out_ref = refs[-1]
    first = 0
    for keep_ref, got_ref in zip(refs[:-1:2], refs[1:-1:2]):
        rows = keep_ref.shape[0]
        total = keep_ref[...].astype(F32) + got_ref[...].astype(F32)
        out_ref[first : first + rows, :] = total.astype(BF)
        first += rows
    if first < out_ref.shape[0]:
        out_ref[first:, :] = jnp.zeros((out_ref.shape[0] - first, out_ref.shape[1]), BF)


def share_body(parts_ref, out_ref):
    count = parts_ref.shape[0]
    for odd in range(2):
        total = parts_ref[odd].astype(F32)
        for peer in range(odd + 2, count, 2):
            total += parts_ref[peer].astype(F32)
        for peer in range(odd, count, 2):
            out_ref[peer] = total.astype(BF)


def unpack_body(where_ref, mine_ref, other_ref, *outs):
    odd = is_odd(where_ref[DOM_AT])
    half = mine_ref.shape[1]
    first = 0

    def put(ref, rows):
        nonlocal first
        mine = mine_ref[first : first + rows, :].astype(F32)
        other = other_ref[first : first + rows, :].astype(F32)
        ref[:, :half] = jnp.where(odd, other, mine)
        ref[:, half:] = jnp.where(odd, mine, other)
        first += rows

    enc_in_ref, enc_out_ref, *layer_refs = outs
    for layer in reversed(range(layer_refs[0].shape[0])):
        for ref in layer_refs:
            put(ref.at[layer], ref.shape[1])
    put(enc_in_ref, enc_in_ref.shape[0])
    put(enc_out_ref, enc_out_ref.shape[0])


def exchange(shard):
    return lax.all_to_all(shard, AXES, split_axis=0, concat_axis=0, tiled=True)


def turned(shard, axis, by):
    count = lax.axis_size(axis)
    return lax.ppermute(shard, axis, [(i, (i + by) % count) for i in range(count)])


def swapped(shard, axis, offset):
    count = lax.axis_size(axis)
    partner = list(range(count))
    for i in range(offset, count - 1, 2):
        partner[i], partner[i + 1] = i + 1, i
    return lax.ppermute(shard, axis, list(enumerate(partner)))


def from_neighbours(rim_rows):
    return (
        swapped(rim_rows, "grid", 0),
        swapped(rim_rows, "grid", 1),
        turned(rim_rows, "dom", 1),
        turned(rim_rows, "dom", -1),
    )


def to_neighbours(sends):
    return (
        swapped(sends[0], "grid", 0),
        swapped(sends[1], "grid", 1),
        turned(sends[2], "dom", -1),
        turned(sends[3], "dom", 1),
    )


def per_device(
    columns,
    column_live,
    col_weight,
    col_slot,
    node_static,
    boundary_idx,
    edge_src,
    edge_dst,
    edge_live,
    edge_weight,
    enc_in,
    enc_out,
    src_proj,
    dst_proj,
    msg_proj,
    node_cotangent,
):
    peers = lax.axis_size(AXES)
    cols, fin = columns.shape
    nodes, width = node_static.shape
    rim = boundary_idx.shape[0]
    edges = edge_src.shape[0]
    ext = 4 * rim
    bucket = cols // peers

    grid_at, grid_count = lax.axis_index("grid"), lax.axis_size("grid")
    dom_at, dom_count = lax.axis_index("dom"), lax.axis_size("dom")
    place = (grid_at * dom_count + dom_at) % (LANES // bucket)
    where = jnp.stack([grid_at, dom_at, jnp.int32(grid_count), jnp.int32(dom_count), place])

    lanes = (cols // LANES, LANES)
    held = [pltpu.VMEM(lanes, jnp.int32), pltpu.VMEM(lanes, jnp.int32), pltpu.VMEM(lanes, F32)]
    (packed,) = call(
        pack_body,
        [((peers, bucket + 4, fin), BF)],
        held + [pltpu.SemaphoreType.DMA((4,))],
        "pack",
        True,
        far=range(1, 5),
    )(
        where,
        columns.reshape(peers, bucket, fin),
        col_slot.reshape(lanes),
        column_live.reshape(lanes),
        col_weight.reshape(lanes),
    )
    packed = exchange(packed)

    node_shape = ((nodes, width), BF)
    node_wide = ((nodes, width), F32)
    rim_shape = ((rim, width), BF)
    edge_shape = ((width, edges), BF)
    edge_wide = ((width, edges), F32)
    full = pltpu.VMEM((width, 2 * rim), BF)
    edge_buf = pltpu.VMEM((width, edges), BF)
    table_buf = pltpu.VMEM((width, 2 * nodes + 2 * rim), BF)

    bound = boundary_idx.reshape(rim // LANES, LANES)
    pooled, col_slope, slot_picks, state0, rim0 = call(
        functools.partial(encode_body, bucket),
        [node_shape, ((width, cols), BF), ((nodes, cols), BF), node_shape, rim_shape],
        [
            edge_buf,
            pltpu.VMEM((2, cols), F32),
            pltpu.VMEM((nodes, rim), BF),
        ],
        "encode",
    )(packed, enc_in, enc_out, node_static, bound)

    edge_lanes = (edges // LANES, LANES)
    state0, edge_dst = lax.optimization_barrier((state0, edge_dst))
    layered = (src_proj.shape, BF)
    picks, rim_picks, rim_picks_t, edge_scale, src_t, dst_t = call(
        picks_body,
        [
            ((2 * nodes + ext, edges), BF),
            ((nodes, rim), BF),
            ((rim, nodes), BF),
            ((1, edges), F32),
            layered,
            layered,
        ],
        [],
        "picks",
    )(
        edge_src.reshape(edge_lanes),
        edge_dst.reshape(edge_lanes),
        edge_live.reshape(edge_lanes),
        edge_weight.reshape(edge_lanes),
        bound,
        src_proj,
        dst_proj,
    )

    rims0 = from_neighbours(rim0)
    (pre0,) = call(functools.partial(own_body, 0), [edge_wide], [table_buf], "own", True)(
        where, *rims0[2:], state0, src_t, dst_t, picks
    )
    slope0, act0, state1, rim1 = call(
        functools.partial(forward_body, 0),
        [edge_shape, node_shape, node_shape, rim_shape],
        [full, edge_buf],
        "forward",
        True,
    )(where, *rims0[:2], pre0, edge_scale, picks, state0, src_t, msg_proj, rim_picks_t)

    rims1 = from_neighbours(rim1)
    (back1,) = call(functools.partial(back_body, 1), [edge_wide], [], "back")(
        msg_proj, node_cotangent, edge_scale, picks
    )
    (pre1,) = call(functools.partial(own_body, 1), [edge_wide], [table_buf], "own", True)(
        where, *rims1[2:], state1, src_t, dst_t, picks
    )
    act_edges1, grad_pre1, *sends1 = call(
        functools.partial(turn_body, 1), [edge_shape, edge_shape] + [rim_shape] * 2, [full], "turn", True
    )(where, *rims1[:2], pre1, back1, edge_scale, picks, src_t)

    sends1 += call(dom_sums_body, [rim_shape] * 2, [], "sides")(picks, grad_pre1)
    returned1 = to_neighbours(sends1)
    own_shape = ((2 * nodes, width), BF)
    own1, partial1 = call(functools.partial(sums_body, 1), [own_shape, node_wide], [], "sums")(
        picks, grad_pre1, node_cotangent, src_proj, dst_proj
    )
    act1, node_out = call(functools.partial(out_body, 1), [node_shape, node_shape], [], "out")(
        picks, act_edges1, state1, msg_proj
    )
    partial1, act1 = lax.optimization_barrier((partial1, act1))
    grad1, grad_pre0, *sends0 = call(
        functools.partial(backward_body, 1),
        [node_wide, edge_shape] + [rim_shape] * 2,
        [],
        "backward",
        True,
    )(where, *returned1, partial1, src_proj, rim_picks, msg_proj, slope0, picks)

    sends0 += call(dom_sums_body, [rim_shape] * 2, [], "sides")(picks, grad_pre0)
    returned0 = to_neighbours(sends0)
    own0, partial0 = call(functools.partial(sums_body, 0), [own_shape, node_wide], [], "sums")(
        picks, grad_pre0, grad1, src_proj, dst_proj
    )
    keep, send = call(terms_body, [((2 * 3 * width, width // 2), BF)] * 2, [], "terms", True)(
        where,
        *(*rims1, *sends1, state1, own1, act1, node_cotangent),
        *(*rims0, *sends0, state0, own0, act0, grad1),
    )
    send, *returned0 = lax.optimization_barrier((send, *returned0))
    hidden = enc_out.shape[0]
    keep_enc, send_enc = call(
        functools.partial(last_body, bucket),
        [((fin + hidden, width // 2), BF)] * 2,
        [],
        "last",
        True,
    )(where, *returned0, partial0, src_proj, rim_picks, packed, enc_out, pooled, col_slope, slot_picks)

    total_rows = 2 * 3 * width + fin + hidden
    share = -(-total_rows // (16 * peers)) * 16
    rows = peers * share
    (merged,) = call(merge_body, [((rows, width // 2), BF)], [], "merge")(
        keep,
        swapped(send, "dom", 0),
        keep_enc,
        swapped(send_enc, "dom", 0),
    )
    parts = exchange(merged.reshape(peers, share, width // 2))
    (spread,) = call(share_body, [((peers, share, width // 2), BF)], [], "share")(parts)
    mine = exchange(spread).reshape(rows, width // 2)
    layer_shape = ((2, width, width), F32)
    grads = call(
        unpack_body,
        [((fin, width), F32), ((hidden, width), F32), layer_shape, layer_shape, layer_shape],
        [],
        "unpack",
        True,
    )(where, mine, swapped(mine, "dom", 0))
    return (node_out, *grads)


def solution(mesh):
    rows = P(AXES, None)
    flat = P(AXES)
    placed = (rows, flat, flat, flat, rows, flat, flat, flat, flat, flat, P(), P(), P(), P(), P(), rows)
    return jax.shard_map(
        per_device,
        mesh=mesh,
        in_specs=placed,
        out_specs=(rows, P(), P(), P(), P(), P()),
        check_vma=False,
    )
```

```python
import functools

import jax
import jax.numpy as jnp
from jax import lax
from jax.experimental import pallas as pl
from jax.experimental.pallas import tpu as pltpu
from jax.sharding import PartitionSpec as P

AXES = ("grid", "dom")
BF = jnp.bfloat16
F32 = jnp.float32
LANES = 128
TILE = 256
CHUNK = 512
GRANT = 20 << 20


def mm(left_side, right_side):
    return jnp.dot(left_side, right_side, preferred_element_type=F32)


def mm_t(left_side, right_side):
    return lax.dot_general(
        left_side, right_side, (((1,), (1,)), ((), ())), preferred_element_type=F32
    )


def t_mm(left_side, right_side):
    return lax.dot_general(
        left_side, right_side, (((0,), (0,)), ((), ())), preferred_element_type=F32
    )


def put_picks(out_ref, start, indices, count):
    rows = lax.broadcasted_iota(jnp.int32, (TILE, indices.shape[1]), 0).astype(F32).astype(BF)
    for base in range(0, count, TILE):
        shifted = (indices - float(base)).astype(BF)
        block = jnp.where(rows == shifted, jnp.ones((), BF), jnp.zeros((), BF))
        out_ref[start + base : start + base + TILE, :] = block


def sigmoid(values):
    return 0.5 * jnp.tanh(0.5 * values) + 0.5


def call(body, outs, scratch, name, flagged=False, far=()):
    vmem = pl.BlockSpec(memory_space=pltpu.VMEM)

    def run(*args):
        specs = [vmem] * len(args)
        if flagged:
            specs[0] = pl.BlockSpec(memory_space=pltpu.SMEM)
        args = list(args)
        for at in far:
            specs[at] = pl.BlockSpec(memory_space=pltpu.HBM)
            args[at] = pltpu.with_memory_space_constraint(args[at], pltpu.HBM)
        return pl.pallas_call(
            body,
            out_shape=tuple(jax.ShapeDtypeStruct(shape, dtype) for shape, dtype in outs),
            in_specs=specs,
            out_specs=tuple(vmem for _ in outs),
            scratch_shapes=scratch,
            compiler_params=pltpu.CompilerParams(vmem_limit_bytes=GRANT),
            name=name,
        )(*args)

    return run


def chunks(total, body):
    for start in range(0, total, CHUNK):
        body(start, pl.ds(start, CHUNK))


def pack_body(
    where_ref, cols_ref, slot_ref, live_ref, weight_ref, out_ref, slot_buf, live_buf, weight_buf, sems
):
    peers, bucket, _ = cols_ref.shape
    per_row = LANES // bucket
    copies = [
        pltpu.make_async_copy(cols_ref, out_ref.at[:, :bucket, :], sems.at[0]),
        pltpu.make_async_copy(slot_ref, slot_buf, sems.at[1]),
        pltpu.make_async_copy(live_ref, live_buf, sems.at[2]),
        pltpu.make_async_copy(weight_ref, weight_buf, sems.at[3]),
    ]
    for copy in copies[1:] + copies[:1]:
        copy.start()
    for copy in copies[1:]:
        copy.wait()
    slot = slot_buf[...].astype(F32)
    high = jnp.floor(slot * (1.0 / 256.0))
    scale = weight_buf[...] * live_buf[...].astype(F32)
    scale_high = scale.astype(BF).astype(F32)
    fields = [high, slot - 256.0 * high, scale_high, scale - scale_high]
    place = where_ref[PLACE]
    lane = lax.broadcasted_iota(jnp.int32, fields[0].shape, 1)
    here = (lane >= place * bucket) & (lane < (place + 1) * bucket)
    for j in range(per_row):
        shift = lax.rem((place - j + per_row) * bucket, LANES)
        moved = [jnp.where(here, pltpu.roll(field, shift, 1), 0.0).astype(BF) for field in fields]
        for row in range(peers // per_row):
            extra = jnp.concatenate([field[row : row + 1, :] for field in moved], 0)
            out_ref[row * per_row + j, bucket : bucket + 4, :] = extra
    copies[0].wait()


GRID_AT, DOM_AT, GRID_COUNT, DOM_COUNT, PLACE = range(5)


def mark(condition):
    return jnp.where(condition, jnp.float32(1.0), jnp.float32(0.0))


def is_odd(place):
    return lax.rem(place, 2) == 1


def side_marks(where_ref):
    grid_at, dom_at = where_ref[GRID_AT], where_ref[DOM_AT]
    return (
        mark(grid_at > 0),
        mark(grid_at < where_ref[GRID_COUNT] - 1),
        mark(dom_at > 0),
        mark(dom_at < where_ref[DOM_COUNT] - 1),
    )


def pair_marks(where_ref):
    up, down, _, _ = side_marks(where_ref)
    odd = is_odd(where_ref[GRID_AT])
    return jnp.where(odd, up, down), jnp.where(odd, down, up)


def picks_body(
    src_ref,
    dst_ref,
    live_ref,
    weight_ref,
    bound_ref,
    src_proj_ref,
    dst_proj_ref,
    picks_ref,
    rim_picks,
    rim_picks_t,
    scale_ref,
    src_t_ref,
    dst_t_ref,
):
    nodes, rim = rim_picks.shape
    src = long_row(src_ref[...].astype(F32))
    dst = long_row(dst_ref[...].astype(F32))
    scale_ref[...] = long_row(weight_ref[...] * live_ref[...].astype(F32))
    for start in range(0, picks_ref.shape[1], CHUNK):
        block = picks_ref.at[:, pl.ds(start, CHUNK)]
        here = src[:, start : start + CHUNK]
        put_picks(block, 0, here - float(nodes), 2 * rim)
        put_picks(block, 2 * rim, dst[:, start : start + CHUNK], nodes)
        put_picks(block, 2 * rim + nodes, here, nodes)
        put_picks(block, 2 * rim + 2 * nodes, here - float(nodes + 2 * rim), 2 * rim)
    put_picks(rim_picks, 0, long_row(bound_ref[...].astype(F32)), nodes)
    rim_picks_t[...] = turned_over(rim_picks[...])
    for layer in range(src_t_ref.shape[0]):
        src_t_ref[layer] = turned_over(src_proj_ref[layer])
        dst_t_ref[layer] = turned_over(dst_proj_ref[layer])


def put_state(state, state_ref, rim_ref, rim_picks_t):
    state_ref[...] = state.astype(BF)
    rim_ref[...] = mm(rim_picks_t[...], state_ref[...]).astype(BF)


def grid_rims(where_ref, first_ref, second_ref):
    odd = is_odd(where_ref[GRID_AT])
    up, down, _, _ = side_marks(where_ref)
    first, second = first_ref[...], second_ref[...]
    return (
        jnp.where(odd, first, second) * up.astype(BF),
        jnp.where(odd, second, first) * down.astype(BF),
    )


def dom_rims(where_ref, left_ref, right_ref):
    _, _, left, right = side_marks(where_ref)
    return left_ref[...] * left.astype(BF), right_ref[...] * right.astype(BF)


def put_col_rows(packed_ref, bucket, rows_ref):
    peers = packed_ref.shape[0]
    per_row = LANES // bucket
    for row in range(peers // per_row):
        parts = [
            packed_ref[row * per_row + j, bucket : bucket + 4, :].astype(F32) for j in range(per_row)
        ]
        total = sum(parts[1:], parts[0])
        at = pl.ds(row * LANES, LANES)
        rows_ref[0:1, at] = total[0:1] * 256.0 + total[1:2]
        rows_ref[1:2, at] = total[2:3] + total[3:4]


def long_row(rows):
    return jnp.concatenate([rows[i : i + 1, :] for i in range(rows.shape[0])], 1)


def turned_over(rows):
    return rows.astype(F32).T.astype(BF)


def encode_body(
    bucket,
    packed_ref,
    enc_in_ref,
    enc_out_ref,
    static_ref,
    bound_ref,
    pooled_ref,
    slope_ref,
    picks_ref,
    state_ref,
    rim_ref,
    act_ref,
    rows_ref,
    rim_picks,
):
    nodes = static_ref.shape[0]
    peers_step = CHUNK // bucket
    put_col_rows(packed_ref, bucket, rows_ref)
    enc_in_t = turned_over(enc_in_ref[...])

    def step(start, at):
        first = start // bucket
        got = packed_ref[first : first + peers_step, :bucket, :].reshape(CHUNK, packed_ref.shape[2])
        pre = mm_t(enc_in_t, got)
        scale = rows_ref[1:2, at]
        sig = sigmoid(pre)
        act = pre * sig
        act_ref[:, at] = (act * scale).astype(BF)
        slope_ref[:, at] = (sig + act * (1.0 - sig)) * scale
        put_picks(picks_ref.at[:, at], 0, rows_ref[0:1, at], nodes)

    chunks(rows_ref.shape[1], step)
    pooled_ref[...] = mm_t(picks_ref[...], act_ref[...]).astype(BF)
    put_picks(rim_picks, 0, long_row(bound_ref[...].astype(F32)), nodes)
    state = static_ref[...].astype(F32) + mm(pooled_ref[...], enc_out_ref[...])
    state_ref[...] = state.astype(BF)
    rim_ref[...] = t_mm(rim_picks[...], state_ref[...]).astype(BF)


def own_body(
    layer, where_ref, left_ref, right_ref, state_ref, src_t_ref, dst_t_ref, picks_ref, out_ref, table_ref
):
    nodes = state_ref.shape[0]
    rim = left_ref.shape[0]
    held = state_ref[...]
    table_ref[:, :nodes] = mm_t(dst_t_ref[layer], held).astype(BF)
    table_ref[:, nodes : 2 * nodes] = mm_t(src_t_ref[layer], held).astype(BF)
    for side, rim_rows in enumerate(dom_rims(where_ref, left_ref, right_ref)):
        start = 2 * nodes + side * rim
        table_ref[:, start : start + rim] = mm_t(src_t_ref[layer], rim_rows).astype(BF)
    out_ref[...] = mm(table_ref[...], picks_ref[2 * rim :, :])


def by_target(picks_ref, nodes):
    return pl.ds((picks_ref.shape[0] - 2 * nodes) // 2, nodes)


def back_body(layer, msg_ref, grad_ref, scale_ref, picks_ref, out_ref):
    nodes = grad_ref.shape[0]
    back = mm_t(msg_ref[layer], grad_ref[...]).astype(BF)
    out_ref[...] = mm(back, picks_ref[by_target(picks_ref, nodes), :]) * scale_ref[...]


def fill_rims(full_ref, rims, src_t_ref):
    rim = rims[0].shape[0]
    for side, rim_rows in enumerate(rims):
        full_ref[:, side * rim : (side + 1) * rim] = mm_t(src_t_ref[...], rim_rows).astype(BF)


def forward_body(
    layer,
    where_ref,
    first_ref,
    second_ref,
    own_pre_ref,
    scale_ref,
    picks_ref,
    state_ref,
    src_t_ref,
    msg_ref,
    rim_picks_t,
    slope_ref,
    node_act_ref,
    next_state_ref,
    rim_ref,
    full_ref,
    act_ref,
):
    nodes = state_ref.shape[0]
    rims = grid_rims(where_ref, first_ref, second_ref)
    fill_rims(full_ref, rims, src_t_ref.at[layer])
    sides = pl.ds(0, full_ref.shape[1])

    def step(start, at):
        pre = own_pre_ref[:, at] + mm(full_ref[...], picks_ref[sides, at])
        scale = scale_ref[:, at]
        sig = sigmoid(pre)
        act = pre * sig
        act_ref[:, at] = (act * scale).astype(BF)
        slope_ref[:, at] = (sig + act * (1.0 - sig)) * scale

    chunks(scale_ref.shape[1], step)
    node_act_ref[...] = mm_t(picks_ref[by_target(picks_ref, nodes), :], act_ref[...]).astype(BF)
    state = state_ref[...].astype(F32) + mm(node_act_ref[...], msg_ref[layer])
    put_state(state, next_state_ref, rim_ref, rim_picks_t)


def put_sums(odd, picks_ref, start, grad_pre_ref, first_ref, second_ref):
    rim = first_ref.shape[0]
    first = pl.multiple_of(start + jnp.where(odd, 0, rim), rim)
    second = pl.multiple_of(start + jnp.where(odd, rim, 0), rim)
    first_ref[...] = mm_t(picks_ref[pl.ds(first, rim), :], grad_pre_ref[...]).astype(BF)
    second_ref[...] = mm_t(picks_ref[pl.ds(second, rim), :], grad_pre_ref[...]).astype(BF)


def dom_sums_body(picks_ref, grad_pre_ref, left_ref, right_ref):
    rim = left_ref.shape[0]
    first = picks_ref.shape[0] - 2 * rim
    left_ref[...] = mm_t(picks_ref[first : first + rim, :], grad_pre_ref[...]).astype(BF)
    right_ref[...] = mm_t(picks_ref[first + rim :, :], grad_pre_ref[...]).astype(BF)


def turn_body(
    layer,
    where_ref,
    first_ref,
    second_ref,
    own_pre_ref,
    back_ref,
    scale_ref,
    picks_ref,
    src_t_ref,
    act_ref,
    grad_pre_ref,
    send0_ref,
    send1_ref,
    full_ref,
):
    rim = first_ref.shape[0]
    rims = grid_rims(where_ref, first_ref, second_ref)
    fill_rims(full_ref, rims, src_t_ref.at[layer])
    sides = pl.ds(0, 2 * rim)

    def step(start, at):
        pre = own_pre_ref[:, at] + mm(full_ref[...], picks_ref[sides, at])
        sig = sigmoid(pre)
        act = pre * sig
        act_ref[:, at] = (act * scale_ref[:, at]).astype(BF)
        grad_pre_ref[:, at] = (back_ref[:, at] * (sig + act * (1.0 - sig))).astype(BF)

    chunks(scale_ref.shape[1], step)
    put_sums(is_odd(where_ref[GRID_AT]), picks_ref, 0, grad_pre_ref, send0_ref, send1_ref)


def merged_grad(partial_ref, where_ref, returned, src_ref, rim_picks):
    sides = side_marks(where_ref)
    marks = (*pair_marks(where_ref), sides[3], sides[2])
    total = returned[0][...].astype(F32) * marks[0]
    for side in range(1, 4):
        total += returned[side][...].astype(F32) * marks[side]
    back = mm(rim_picks[...], total.astype(BF)).astype(BF)
    return partial_ref[...] + mm_t(back, src_ref[...])


def backward_body(
    layer,
    where_ref,
    first_ref,
    second_ref,
    left_ref,
    right_ref,
    partial_ref,
    src_ref,
    rim_picks,
    msg_ref,
    slope_ref,
    picks_ref,
    grad_ref,
    grad_pre_ref,
    send0_ref,
    send1_ref,
):
    nodes = partial_ref.shape[0]
    returned = (first_ref, second_ref, left_ref, right_ref)
    grad = merged_grad(partial_ref, where_ref, returned, src_ref.at[layer], rim_picks)
    grad_ref[...] = grad
    back = mm_t(msg_ref[layer - 1], grad.astype(BF)).astype(BF)

    def step(start, at):
        grad_pre = mm(back, picks_ref[by_target(picks_ref, nodes), at]) * slope_ref[:, at]
        grad_pre_ref[:, at] = grad_pre.astype(BF)

    chunks(picks_ref.shape[1], step)
    put_sums(is_odd(where_ref[GRID_AT]), picks_ref, 0, grad_pre_ref, send0_ref, send1_ref)


def sums_body(layer, picks_ref, grad_pre_ref, grad_ref, src_ref, dst_ref, own_ref, partial_ref):
    nodes = grad_ref.shape[0]
    first = by_target(picks_ref, nodes).start
    own_ref[...] = mm_t(picks_ref[first : first + 2 * nodes, :], grad_pre_ref[...]).astype(BF)
    partial_ref[...] = (
        grad_ref[...].astype(F32)
        + mm_t(own_ref[:nodes, :], dst_ref[layer])
        + mm_t(own_ref[nodes:, :], src_ref[layer])
    )


def out_body(layer, picks_ref, act_edges_ref, state_ref, msg_ref, act_ref, out_ref):
    nodes = state_ref.shape[0]
    act_ref[...] = mm_t(picks_ref[by_target(picks_ref, nodes), :], act_edges_ref[...]).astype(BF)
    out_ref[...] = (state_ref[...].astype(F32) + mm(act_ref[...], msg_ref[layer])).astype(BF)


def put_halves(where_ref, first, term, keep_ref, send_ref):
    half = term.shape[1] // 2
    odd = is_odd(where_ref[DOM_AT])
    low, high = term[:, :half], term[:, half:]
    keep_ref[first : first + term.shape[0], :] = jnp.where(odd, high, low)
    send_ref[first : first + term.shape[0], :] = jnp.where(odd, low, high).astype(BF)


def terms_body(where_ref, *refs):
    keep_ref, send_ref = refs[-2:]
    marks = (*pair_marks(where_ref), *side_marks(where_ref)[2:])
    for layer in range(len(refs) // 12):
        held = refs[12 * layer : 12 * layer + 12]
        rims, sends, (state_ref, own_ref, act_ref, grad_ref) = held[:4], held[4:8], held[8:]
        nodes, width = state_ref.shape
        first = 3 * width * layer
        state = state_ref[...]
        src_term = t_mm(state, own_ref[nodes:, :])
        for rim_ref, sums_ref, present in zip(rims, sends, marks):
            src_term += t_mm(rim_ref[...], sums_ref[...]) * present
        put_halves(where_ref, first, src_term, keep_ref, send_ref)
        put_halves(where_ref, first + width, t_mm(state, own_ref[:nodes, :]), keep_ref, send_ref)
        msg_term = t_mm(act_ref[...], grad_ref[...].astype(BF))
        put_halves(where_ref, first + 2 * width, msg_term, keep_ref, send_ref)


def last_body(
    bucket,
    where_ref,
    first_ref,
    second_ref,
    left_ref,
    right_ref,
    partial_ref,
    src_ref,
    rim_picks,
    packed_ref,
    enc_out_ref,
    pooled_ref,
    slope_ref,
    picks_ref,
    keep_ref,
    send_ref,
):
    fin = packed_ref.shape[2]
    peers_step = CHUNK // bucket
    returned = (first_ref, second_ref, left_ref, right_ref)
    grad = merged_grad(partial_ref, where_ref, returned, src_ref.at[0], rim_picks).astype(BF)
    back = mm_t(enc_out_ref[...], grad).astype(BF)
    in_term = jnp.zeros((enc_out_ref.shape[0], fin), F32)
    for start in range(0, picks_ref.shape[1], CHUNK):
        at = pl.ds(start, CHUNK)
        first = start // bucket
        got = packed_ref[first : first + peers_step, :bucket, :].reshape(CHUNK, fin)
        grad_pre = mm(back, picks_ref[:, at]) * slope_ref[:, at]
        in_term += mm(grad_pre.astype(BF), got)
    put_halves(where_ref, 0, in_term.T, keep_ref, send_ref)
    put_halves(where_ref, fin, t_mm(pooled_ref[...], grad), keep_ref, send_ref)


def merge_body(*refs):
    out_ref = refs[-1]
    first = 0
    for keep_ref, got_ref in zip(refs[:-1:2], refs[1:-1:2]):
        rows = keep_ref.shape[0]
        total = keep_ref[...] + got_ref[...].astype(F32)
        out_ref[first : first + rows, :] = total.astype(BF)
        first += rows
    if first < out_ref.shape[0]:
        out_ref[first:, :] = jnp.zeros((out_ref.shape[0] - first, out_ref.shape[1]), BF)


def share_body(parts_ref, out_ref):
    count = parts_ref.shape[0]
    for odd in range(2):
        total = parts_ref[odd].astype(F32)
        for peer in range(odd + 2, count, 2):
            total += parts_ref[peer].astype(F32)
        for peer in range(odd, count, 2):
            out_ref[peer] = total.astype(BF)


def unpack_body(where_ref, mine_ref, other_ref, *outs):
    odd = is_odd(where_ref[DOM_AT])
    half = mine_ref.shape[1]
    first = 0

    def put(ref, rows):
        nonlocal first
        mine = mine_ref[first : first + rows, :].astype(F32)
        other = other_ref[first : first + rows, :].astype(F32)
        ref[:, :half] = jnp.where(odd, other, mine)
        ref[:, half:] = jnp.where(odd, mine, other)
        first += rows

    enc_in_ref, enc_out_ref, *layer_refs = outs
    for layer in reversed(range(layer_refs[0].shape[0])):
        for ref in layer_refs:
            put(ref.at[layer], ref.shape[1])
    put(enc_in_ref, enc_in_ref.shape[0])
    put(enc_out_ref, enc_out_ref.shape[0])


def exchange(shard):
    return lax.all_to_all(shard, AXES, split_axis=0, concat_axis=0, tiled=True)


def turned(shard, axis, by):
    count = lax.axis_size(axis)
    return lax.ppermute(shard, axis, [(i, (i + by) % count) for i in range(count)])


def swapped(shard, axis, offset):
    count = lax.axis_size(axis)
    partner = list(range(count))
    for i in range(offset, count - 1, 2):
        partner[i], partner[i + 1] = i + 1, i
    return lax.ppermute(shard, axis, list(enumerate(partner)))


def from_neighbours(rim_rows):
    return (
        swapped(rim_rows, "grid", 0),
        swapped(rim_rows, "grid", 1),
        turned(rim_rows, "dom", 1),
        turned(rim_rows, "dom", -1),
    )


def to_neighbours(sends):
    return (
        swapped(sends[0], "grid", 0),
        swapped(sends[1], "grid", 1),
        turned(sends[2], "dom", -1),
        turned(sends[3], "dom", 1),
    )


def per_device(
    columns,
    column_live,
    col_weight,
    col_slot,
    node_static,
    boundary_idx,
    edge_src,
    edge_dst,
    edge_live,
    edge_weight,
    enc_in,
    enc_out,
    src_proj,
    dst_proj,
    msg_proj,
    node_cotangent,
):
    peers = lax.axis_size(AXES)
    cols, fin = columns.shape
    nodes, width = node_static.shape
    rim = boundary_idx.shape[0]
    edges = edge_src.shape[0]
    ext = 4 * rim
    bucket = cols // peers

    grid_at, grid_count = lax.axis_index("grid"), lax.axis_size("grid")
    dom_at, dom_count = lax.axis_index("dom"), lax.axis_size("dom")
    place = (grid_at * dom_count + dom_at) % (LANES // bucket)
    where = jnp.stack([grid_at, dom_at, jnp.int32(grid_count), jnp.int32(dom_count), place])

    lanes = (cols // LANES, LANES)
    held = [pltpu.VMEM(lanes, jnp.int32), pltpu.VMEM(lanes, jnp.int32), pltpu.VMEM(lanes, F32)]
    (packed,) = call(
        pack_body,
        [((peers, bucket + 4, fin), BF)],
        held + [pltpu.SemaphoreType.DMA((4,))],
        "pack",
        True,
        far=range(1, 5),
    )(
        where,
        columns.reshape(peers, bucket, fin),
        col_slot.reshape(lanes),
        column_live.reshape(lanes),
        col_weight.reshape(lanes),
    )
    packed = exchange(packed)

    node_shape = ((nodes, width), BF)
    node_wide = ((nodes, width), F32)
    rim_shape = ((rim, width), BF)
    edge_shape = ((width, edges), BF)
    edge_wide = ((width, edges), F32)
    full = pltpu.VMEM((width, 2 * rim), BF)
    edge_buf = pltpu.VMEM((width, edges), BF)
    table_buf = pltpu.VMEM((width, 2 * nodes + 2 * rim), BF)

    bound = boundary_idx.reshape(rim // LANES, LANES)
    pooled, col_slope, slot_picks, state0, rim0 = call(
        functools.partial(encode_body, bucket),
        [node_shape, ((width, cols), F32), ((nodes, cols), BF), node_shape, rim_shape],
        [
            edge_buf,
            pltpu.VMEM((2, cols), F32),
            pltpu.VMEM((nodes, rim), BF),
        ],
        "encode",
    )(packed, enc_in, enc_out, node_static, bound)

    edge_lanes = (edges // LANES, LANES)
    state0, edge_dst = lax.optimization_barrier((state0, edge_dst))
    layered = (src_proj.shape, BF)
    picks, rim_picks, rim_picks_t, edge_scale, src_t, dst_t = call(
        picks_body,
        [
            ((2 * nodes + ext, edges), BF),
            ((nodes, rim), BF),
            ((rim, nodes), BF),
            ((1, edges), F32),
            layered,
            layered,
        ],
        [],
        "picks",
    )(
        edge_src.reshape(edge_lanes),
        edge_dst.reshape(edge_lanes),
        edge_live.reshape(edge_lanes),
        edge_weight.reshape(edge_lanes),
        bound,
        src_proj,
        dst_proj,
    )

    rims0 = from_neighbours(rim0)
    (pre0,) = call(functools.partial(own_body, 0), [edge_wide], [table_buf], "own", True)(
        where, *rims0[2:], state0, src_t, dst_t, picks
    )
    slope0, act0, state1, rim1 = call(
        functools.partial(forward_body, 0),
        [edge_wide, node_shape, node_shape, rim_shape],
        [full, edge_buf],
        "forward",
        True,
    )(where, *rims0[:2], pre0, edge_scale, picks, state0, src_t, msg_proj, rim_picks_t)

    rims1 = from_neighbours(rim1)
    (back1,) = call(functools.partial(back_body, 1), [edge_wide], [], "back")(
        msg_proj, node_cotangent, edge_scale, picks
    )
    (pre1,) = call(functools.partial(own_body, 1), [edge_wide], [table_buf], "own", True)(
        where, *rims1[2:], state1, src_t, dst_t, picks
    )
    act_edges1, grad_pre1, *sends1 = call(
        functools.partial(turn_body, 1), [edge_shape, edge_shape] + [rim_shape] * 2, [full], "turn", True
    )(where, *rims1[:2], pre1, back1, edge_scale, picks, src_t)

    sends1 += call(dom_sums_body, [rim_shape] * 2, [], "sides")(picks, grad_pre1)
    returned1 = to_neighbours(sends1)
    own_shape = ((2 * nodes, width), BF)
    own1, partial1 = call(functools.partial(sums_body, 1), [own_shape, node_wide], [], "sums")(
        picks, grad_pre1, node_cotangent, src_proj, dst_proj
    )
    act1, node_out = call(functools.partial(out_body, 1), [node_shape, node_shape], [], "out")(
        picks, act_edges1, state1, msg_proj
    )
    partial1, act1 = lax.optimization_barrier((partial1, act1))
    grad1, grad_pre0, *sends0 = call(
        functools.partial(backward_body, 1),
        [node_wide, edge_shape] + [rim_shape] * 2,
        [],
        "backward",
        True,
    )(where, *returned1, partial1, src_proj, rim_picks, msg_proj, slope0, picks)

    sends0 += call(dom_sums_body, [rim_shape] * 2, [], "sides")(picks, grad_pre0)
    returned0 = to_neighbours(sends0)
    own0, partial0 = call(functools.partial(sums_body, 0), [own_shape, node_wide], [], "sums")(
        picks, grad_pre0, grad1, src_proj, dst_proj
    )
    keep, send = call(
        terms_body,
        [((2 * 3 * width, width // 2), dtype) for dtype in (F32, BF)],
        [],
        "terms",
        True,
    )(
        where,
        *(*rims1, *sends1, state1, own1, act1, node_cotangent),
        *(*rims0, *sends0, state0, own0, act0, grad1),
    )
    send, *returned0 = lax.optimization_barrier((send, *returned0))
    hidden = enc_out.shape[0]
    keep_enc, send_enc = call(
        functools.partial(last_body, bucket),
        [((fin + hidden, width // 2), dtype) for dtype in (F32, BF)],
        [],
        "last",
        True,
    )(where, *returned0, partial0, src_proj, rim_picks, packed, enc_out, pooled, col_slope, slot_picks)

    total_rows = 2 * 3 * width + fin + hidden
    share = -(-total_rows // (16 * peers)) * 16
    rows = peers * share
    (merged,) = call(merge_body, [((rows, width // 2), BF)], [], "merge")(
        keep,
        swapped(send, "dom", 0),
        keep_enc,
        swapped(send_enc, "dom", 0),
    )
    parts = exchange(merged.reshape(peers, share, width // 2))
    (spread,) = call(share_body, [((peers, share, width // 2), BF)], [], "share")(parts)
    mine = exchange(spread).reshape(rows, width // 2)
    layer_shape = ((2, width, width), F32)
    grads = call(
        unpack_body,
        [((fin, width), F32), ((hidden, width), F32), layer_shape, layer_shape, layer_shape],
        [],
        "unpack",
        True,
    )(where, mine, swapped(mine, "dom", 0))
    return (node_out, *grads)


def solution(mesh):
    rows = P(AXES, None)
    flat = P(AXES)
    placed = (rows, flat, flat, flat, rows, flat, flat, flat, flat, flat, P(), P(), P(), P(), P(), rows)
    return jax.shard_map(
        per_device,
        mesh=mesh,
        in_specs=placed,
        out_specs=(rows, P(), P(), P(), P(), P()),
        check_vma=False,
    )
```

```python
import functools

import jax
import jax.numpy as jnp
from jax import lax
from jax.experimental import pallas as pl
from jax.experimental.pallas import tpu as pltpu
from jax.sharding import PartitionSpec as P

AXES = ("grid", "dom")
BF = jnp.bfloat16
F32 = jnp.float32
LANES = 128
TILE = 256
CHUNK = 1024
GRANT = 20 << 20


def mm(left_side, right_side):
    return jnp.dot(left_side, right_side, preferred_element_type=F32)


def mm_t(left_side, right_side):
    return lax.dot_general(
        left_side, right_side, (((1,), (1,)), ((), ())), preferred_element_type=F32
    )


def t_mm(left_side, right_side):
    return lax.dot_general(
        left_side, right_side, (((0,), (0,)), ((), ())), preferred_element_type=F32
    )


def put_picks(out_ref, start, indices, count):
    rows = lax.broadcasted_iota(jnp.int32, (TILE, indices.shape[1]), 0).astype(F32).astype(BF)
    for base in range(0, count, TILE):
        shifted = (indices - float(base)).astype(BF)
        block = jnp.where(rows == shifted, jnp.ones((), BF), jnp.zeros((), BF))
        out_ref[start + base : start + base + TILE, :] = block


def sigmoid(values):
    return 0.5 * jnp.tanh(0.5 * values) + 0.5


def call(body, outs, scratch, name, flagged=False, far=()):
    vmem = pl.BlockSpec(memory_space=pltpu.VMEM)

    def run(*args):
        specs = [vmem] * len(args)
        if flagged:
            specs[0] = pl.BlockSpec(memory_space=pltpu.SMEM)
        args = list(args)
        for at in far:
            specs[at] = pl.BlockSpec(memory_space=pltpu.HBM)
            args[at] = pltpu.with_memory_space_constraint(args[at], pltpu.HBM)
        return pl.pallas_call(
            body,
            out_shape=tuple(jax.ShapeDtypeStruct(shape, dtype) for shape, dtype in outs),
            in_specs=specs,
            out_specs=tuple(vmem for _ in outs),
            scratch_shapes=scratch,
            compiler_params=pltpu.CompilerParams(vmem_limit_bytes=GRANT),
            name=name,
        )(*args)

    return run


def chunks(total, body):
    for start in range(0, total, CHUNK):
        body(start, pl.ds(start, CHUNK))


def pack_body(
    where_ref, cols_ref, slot_ref, live_ref, weight_ref, out_ref, slot_buf, live_buf, weight_buf, sems
):
    peers, bucket, _ = cols_ref.shape
    per_row = LANES // bucket
    copies = [
        pltpu.make_async_copy(cols_ref, out_ref.at[:, :bucket, :], sems.at[0]),
        pltpu.make_async_copy(slot_ref, slot_buf, sems.at[1]),
        pltpu.make_async_copy(live_ref, live_buf, sems.at[2]),
        pltpu.make_async_copy(weight_ref, weight_buf, sems.at[3]),
    ]
    for copy in copies[1:] + copies[:1]:
        copy.start()
    for copy in copies[1:]:
        copy.wait()
    slot = slot_buf[...].astype(F32)
    high = jnp.floor(slot * (1.0 / 256.0))
    scale = weight_buf[...] * live_buf[...].astype(F32)
    scale_high = scale.astype(BF).astype(F32)
    fields = [high, slot - 256.0 * high, scale_high, scale - scale_high]
    place = where_ref[PLACE]
    lane = lax.broadcasted_iota(jnp.int32, fields[0].shape, 1)
    here = (lane >= place * bucket) & (lane < (place + 1) * bucket)
    for j in range(per_row):
        shift = lax.rem((place - j + per_row) * bucket, LANES)
        moved = [jnp.where(here, pltpu.roll(field, shift, 1), 0.0).astype(BF) for field in fields]
        for row in range(peers // per_row):
            extra = jnp.concatenate([field[row : row + 1, :] for field in moved], 0)
            out_ref[row * per_row + j, bucket : bucket + 4, :] = extra
    copies[0].wait()


GRID_AT, DOM_AT, GRID_COUNT, DOM_COUNT, PLACE = range(5)


def mark(condition):
    return jnp.where(condition, jnp.float32(1.0), jnp.float32(0.0))


def is_odd(place):
    return lax.rem(place, 2) == 1


def side_marks(where_ref):
    grid_at, dom_at = where_ref[GRID_AT], where_ref[DOM_AT]
    return (
        mark(grid_at > 0),
        mark(grid_at < where_ref[GRID_COUNT] - 1),
        mark(dom_at > 0),
        mark(dom_at < where_ref[DOM_COUNT] - 1),
    )


def pair_marks(where_ref):
    up, down, _, _ = side_marks(where_ref)
    odd = is_odd(where_ref[GRID_AT])
    return jnp.where(odd, up, down), jnp.where(odd, down, up)


def picks_body(
    src_ref,
    dst_ref,
    live_ref,
    weight_ref,
    bound_ref,
    src_proj_ref,
    dst_proj_ref,
    picks_ref,
    rim_picks,
    rim_picks_t,
    scale_ref,
    src_t_ref,
    dst_t_ref,
):
    nodes, rim = rim_picks.shape
    src = long_row(src_ref[...].astype(F32))
    dst = long_row(dst_ref[...].astype(F32))
    scale_ref[...] = long_row(weight_ref[...] * live_ref[...].astype(F32))
    for start in range(0, picks_ref.shape[1], CHUNK):
        block = picks_ref.at[:, pl.ds(start, CHUNK)]
        here = src[:, start : start + CHUNK]
        put_picks(block, 0, here - float(nodes), 2 * rim)
        put_picks(block, 2 * rim, dst[:, start : start + CHUNK], nodes)
        put_picks(block, 2 * rim + nodes, here, nodes)
        put_picks(block, 2 * rim + 2 * nodes, here - float(nodes + 2 * rim), 2 * rim)
    put_picks(rim_picks, 0, long_row(bound_ref[...].astype(F32)), nodes)
    rim_picks_t[...] = turned_over(rim_picks[...])
    for layer in range(src_t_ref.shape[0]):
        src_t_ref[layer] = turned_over(src_proj_ref[layer])
        dst_t_ref[layer] = turned_over(dst_proj_ref[layer])


def put_state(state, state_ref, rim_ref, rim_picks_t):
    state_ref[...] = state.astype(BF)
    rim_ref[...] = mm(rim_picks_t[...], state_ref[...]).astype(BF)


def grid_rims(where_ref, first_ref, second_ref):
    odd = is_odd(where_ref[GRID_AT])
    up, down, _, _ = side_marks(where_ref)
    first, second = first_ref[...], second_ref[...]
    return (
        jnp.where(odd, first, second) * up.astype(BF),
        jnp.where(odd, second, first) * down.astype(BF),
    )


def dom_rims(where_ref, left_ref, right_ref):
    _, _, left, right = side_marks(where_ref)
    return left_ref[...] * left.astype(BF), right_ref[...] * right.astype(BF)


def put_col_rows(packed_ref, bucket, rows_ref):
    peers = packed_ref.shape[0]
    per_row = LANES // bucket
    for row in range(peers // per_row):
        parts = [
            packed_ref[row * per_row + j, bucket : bucket + 4, :].astype(F32) for j in range(per_row)
        ]
        total = sum(parts[1:], parts[0])
        at = pl.ds(row * LANES, LANES)
        rows_ref[0:1, at] = total[0:1] * 256.0 + total[1:2]
        rows_ref[1:2, at] = total[2:3] + total[3:4]


def long_row(rows):
    return jnp.concatenate([rows[i : i + 1, :] for i in range(rows.shape[0])], 1)


def turned_over(rows):
    return rows.astype(F32).T.astype(BF)


def encode_body(
    bucket,
    packed_ref,
    enc_in_ref,
    enc_out_ref,
    static_ref,
    bound_ref,
    pooled_ref,
    slope_ref,
    picks_ref,
    state_ref,
    rim_ref,
    act_ref,
    rows_ref,
    rim_picks,
):
    nodes = static_ref.shape[0]
    peers_step = CHUNK // bucket
    put_col_rows(packed_ref, bucket, rows_ref)
    enc_in_t = turned_over(enc_in_ref[...])

    def step(start, at):
        first = start // bucket
        got = packed_ref[first : first + peers_step, :bucket, :].reshape(CHUNK, packed_ref.shape[2])
        pre = mm_t(enc_in_t, got)
        scale = rows_ref[1:2, at]
        sig = sigmoid(pre)
        act = pre * sig
        act_ref[:, at] = (act * scale).astype(BF)
        slope_ref[:, at] = (sig + act * (1.0 - sig)) * scale
        put_picks(picks_ref.at[:, at], 0, rows_ref[0:1, at], nodes)

    chunks(rows_ref.shape[1], step)
    pooled_ref[...] = mm_t(picks_ref[...], act_ref[...]).astype(BF)
    put_picks(rim_picks, 0, long_row(bound_ref[...].astype(F32)), nodes)
    state = static_ref[...].astype(F32) + mm(pooled_ref[...], enc_out_ref[...])
    state_ref[...] = state.astype(BF)
    rim_ref[...] = t_mm(rim_picks[...], state_ref[...]).astype(BF)


def own_body(
    layer, where_ref, left_ref, right_ref, state_ref, src_t_ref, dst_t_ref, picks_ref, out_ref, table_ref
):
    nodes = state_ref.shape[0]
    rim = left_ref.shape[0]
    held = state_ref[...]
    table_ref[:, :nodes] = mm_t(dst_t_ref[layer], held).astype(BF)
    table_ref[:, nodes : 2 * nodes] = mm_t(src_t_ref[layer], held).astype(BF)
    for side, rim_rows in enumerate(dom_rims(where_ref, left_ref, right_ref)):
        start = 2 * nodes + side * rim
        table_ref[:, start : start + rim] = mm_t(src_t_ref[layer], rim_rows).astype(BF)
    out_ref[...] = mm(table_ref[...], picks_ref[2 * rim :, :])


def by_target(picks_ref, nodes):
    return pl.ds((picks_ref.shape[0] - 2 * nodes) // 2, nodes)


def back_body(layer, msg_ref, grad_ref, scale_ref, picks_ref, out_ref):
    nodes = grad_ref.shape[0]
    back = mm_t(msg_ref[layer], grad_ref[...]).astype(BF)
    out_ref[...] = mm(back, picks_ref[by_target(picks_ref, nodes), :]) * scale_ref[...]


def fill_rims(full_ref, rims, src_t_ref):
    rim = rims[0].shape[0]
    for side, rim_rows in enumerate(rims):
        full_ref[:, side * rim : (side + 1) * rim] = mm_t(src_t_ref[...], rim_rows).astype(BF)


def forward_body(
    layer,
    where_ref,
    first_ref,
    second_ref,
    own_pre_ref,
    scale_ref,
    picks_ref,
    state_ref,
    src_t_ref,
    msg_ref,
    rim_picks_t,
    slope_ref,
    node_act_ref,
    next_state_ref,
    rim_ref,
    full_ref,
    act_ref,
):
    nodes = state_ref.shape[0]
    rims = grid_rims(where_ref, first_ref, second_ref)
    fill_rims(full_ref, rims, src_t_ref.at[layer])
    sides = pl.ds(0, full_ref.shape[1])

    def step(start, at):
        pre = own_pre_ref[:, at] + mm(full_ref[...], picks_ref[sides, at])
        scale = scale_ref[:, at]
        sig = sigmoid(pre)
        act = pre * sig
        act_ref[:, at] = (act * scale).astype(BF)
        slope_ref[:, at] = (sig + act * (1.0 - sig)) * scale

    chunks(scale_ref.shape[1], step)
    node_act_ref[...] = mm_t(picks_ref[by_target(picks_ref, nodes), :], act_ref[...]).astype(BF)
    state = state_ref[...].astype(F32) + mm(node_act_ref[...], msg_ref[layer])
    put_state(state, next_state_ref, rim_ref, rim_picks_t)


def put_sums(odd, picks_ref, start, grad_pre_ref, first_ref, second_ref):
    rim = first_ref.shape[0]
    first = pl.multiple_of(start + jnp.where(odd, 0, rim), rim)
    second = pl.multiple_of(start + jnp.where(odd, rim, 0), rim)
    first_ref[...] = mm_t(picks_ref[pl.ds(first, rim), :], grad_pre_ref[...]).astype(BF)
    second_ref[...] = mm_t(picks_ref[pl.ds(second, rim), :], grad_pre_ref[...]).astype(BF)


def dom_sums_body(picks_ref, grad_pre_ref, left_ref, right_ref):
    rim = left_ref.shape[0]
    first = picks_ref.shape[0] - 2 * rim
    left_ref[...] = mm_t(picks_ref[first : first + rim, :], grad_pre_ref[...]).astype(BF)
    right_ref[...] = mm_t(picks_ref[first + rim :, :], grad_pre_ref[...]).astype(BF)


def turn_body(
    layer,
    where_ref,
    first_ref,
    second_ref,
    own_pre_ref,
    back_ref,
    scale_ref,
    picks_ref,
    src_t_ref,
    act_ref,
    grad_pre_ref,
    send0_ref,
    send1_ref,
    full_ref,
):
    rim = first_ref.shape[0]
    rims = grid_rims(where_ref, first_ref, second_ref)
    fill_rims(full_ref, rims, src_t_ref.at[layer])
    sides = pl.ds(0, 2 * rim)

    def step(start, at):
        pre = own_pre_ref[:, at] + mm(full_ref[...], picks_ref[sides, at])
        sig = sigmoid(pre)
        act = pre * sig
        act_ref[:, at] = (act * scale_ref[:, at]).astype(BF)
        grad_pre_ref[:, at] = (back_ref[:, at] * (sig + act * (1.0 - sig))).astype(BF)

    chunks(scale_ref.shape[1], step)
    put_sums(is_odd(where_ref[GRID_AT]), picks_ref, 0, grad_pre_ref, send0_ref, send1_ref)


def merged_grad(partial_ref, where_ref, returned, src_ref, rim_picks):
    sides = side_marks(where_ref)
    marks = (*pair_marks(where_ref), sides[3], sides[2])
    total = returned[0][...].astype(F32) * marks[0]
    for side in range(1, 4):
        total += returned[side][...].astype(F32) * marks[side]
    back = mm(rim_picks[...], total.astype(BF)).astype(BF)
    return partial_ref[...] + mm_t(back, src_ref[...]), back


def backward_body(
    layer,
    where_ref,
    first_ref,
    second_ref,
    left_ref,
    right_ref,
    partial_ref,
    src_ref,
    rim_picks,
    msg_ref,
    slope_ref,
    picks_ref,
    grad_ref,
    back_src_ref,
    grad_pre_ref,
    send0_ref,
    send1_ref,
):
    nodes = partial_ref.shape[0]
    returned = (first_ref, second_ref, left_ref, right_ref)
    grad, back_src = merged_grad(partial_ref, where_ref, returned, src_ref.at[layer], rim_picks)
    back_src_ref[...] = back_src
    grad_ref[...] = grad
    back = mm_t(msg_ref[layer - 1], grad.astype(BF)).astype(BF)

    def step(start, at):
        grad_pre = mm(back, picks_ref[by_target(picks_ref, nodes), at]) * slope_ref[:, at]
        grad_pre_ref[:, at] = grad_pre.astype(BF)

    chunks(picks_ref.shape[1], step)
    put_sums(is_odd(where_ref[GRID_AT]), picks_ref, 0, grad_pre_ref, send0_ref, send1_ref)


def sums_body(layer, picks_ref, grad_pre_ref, grad_ref, src_ref, dst_ref, own_ref, partial_ref):
    nodes = grad_ref.shape[0]
    first = by_target(picks_ref, nodes).start
    own_ref[...] = mm_t(picks_ref[first : first + 2 * nodes, :], grad_pre_ref[...]).astype(BF)
    partial_ref[...] = (
        grad_ref[...].astype(F32)
        + mm_t(own_ref[:nodes, :], dst_ref[layer])
        + mm_t(own_ref[nodes:, :], src_ref[layer])
    )


def out_body(layer, picks_ref, act_edges_ref, state_ref, msg_ref, act_ref, out_ref):
    nodes = state_ref.shape[0]
    act_ref[...] = mm_t(picks_ref[by_target(picks_ref, nodes), :], act_edges_ref[...]).astype(BF)
    out_ref[...] = (state_ref[...].astype(F32) + mm(act_ref[...], msg_ref[layer])).astype(BF)


def put_halves(where_ref, first, term, keep_ref, send_ref):
    half = term.shape[1] // 2
    odd = is_odd(where_ref[DOM_AT])
    low, high = term[:, :half], term[:, half:]
    keep_ref[first : first + term.shape[0], :] = jnp.where(odd, high, low)
    send_ref[first : first + term.shape[0], :] = jnp.where(odd, low, high).astype(BF)


def terms_body(where_ref, *refs):
    keep_ref, send_ref = refs[-2:]
    marks = (*pair_marks(where_ref), *side_marks(where_ref)[2:])
    later, first_layer = refs[:5], refs[5:-2]
    for layer, held in enumerate((later, first_layer)):
        rims, sends = (held[:4], held[4:8]) if layer else ((), ())
        state_ref, own_ref, act_ref, grad_ref = held[-4:]
        nodes, width = state_ref.shape
        first = 3 * width * layer
        state = state_ref[...]
        own_src = own_ref[nodes:, :]
        if not layer:
            own_src = (own_src.astype(F32) + held[0][...].astype(F32)).astype(BF)
        src_term = t_mm(state, own_src)
        for rim_ref, sums_ref, present in zip(rims, sends, marks):
            src_term += t_mm(rim_ref[...], sums_ref[...]) * present
        put_halves(where_ref, first, src_term, keep_ref, send_ref)
        put_halves(where_ref, first + width, t_mm(state, own_ref[:nodes, :]), keep_ref, send_ref)
        msg_term = t_mm(act_ref[...], grad_ref[...].astype(BF))
        put_halves(where_ref, first + 2 * width, msg_term, keep_ref, send_ref)


def last_body(
    bucket,
    where_ref,
    first_ref,
    second_ref,
    left_ref,
    right_ref,
    partial_ref,
    src_ref,
    rim_picks,
    packed_ref,
    enc_out_ref,
    pooled_ref,
    slope_ref,
    picks_ref,
    keep_ref,
    send_ref,
):
    fin = packed_ref.shape[2]
    peers_step = CHUNK // bucket
    returned = (first_ref, second_ref, left_ref, right_ref)
    grad, _ = merged_grad(partial_ref, where_ref, returned, src_ref.at[0], rim_picks)
    grad = grad.astype(BF)
    back = mm_t(enc_out_ref[...], grad).astype(BF)
    in_term = jnp.zeros((enc_out_ref.shape[0], fin), F32)
    for start in range(0, picks_ref.shape[1], CHUNK):
        at = pl.ds(start, CHUNK)
        first = start // bucket
        got = packed_ref[first : first + peers_step, :bucket, :].reshape(CHUNK, fin)
        grad_pre = mm(back, picks_ref[:, at]) * slope_ref[:, at]
        in_term += mm(grad_pre.astype(BF), got)
    put_halves(where_ref, 0, in_term.T, keep_ref, send_ref)
    put_halves(where_ref, fin, t_mm(pooled_ref[...], grad), keep_ref, send_ref)


def merge_body(*refs):
    out_ref = refs[-1]
    first = 0
    for keep_ref, got_ref in zip(refs[:-1:2], refs[1:-1:2]):
        rows = keep_ref.shape[0]
        total = keep_ref[...] + got_ref[...].astype(F32)
        out_ref[first : first + rows, :] = total.astype(BF)
        first += rows
    if first < out_ref.shape[0]:
        out_ref[first:, :] = jnp.zeros((out_ref.shape[0] - first, out_ref.shape[1]), BF)


def share_body(parts_ref, out_ref):
    count = parts_ref.shape[0]
    for odd in range(2):
        total = parts_ref[odd].astype(F32)
        for peer in range(odd + 2, count, 2):
            total += parts_ref[peer].astype(F32)
        for peer in range(odd, count, 2):
            out_ref[peer] = total.astype(BF)


def unpack_body(where_ref, mine_ref, other_ref, *outs):
    odd = is_odd(where_ref[DOM_AT])
    half = mine_ref.shape[1]
    first = 0

    def put(ref, rows):
        nonlocal first
        mine = mine_ref[first : first + rows, :].astype(F32)
        other = other_ref[first : first + rows, :].astype(F32)
        ref[:, :half] = jnp.where(odd, other, mine)
        ref[:, half:] = jnp.where(odd, mine, other)
        first += rows

    enc_in_ref, enc_out_ref, *layer_refs = outs
    for layer in reversed(range(layer_refs[0].shape[0])):
        for ref in layer_refs:
            put(ref.at[layer], ref.shape[1])
    put(enc_in_ref, enc_in_ref.shape[0])
    put(enc_out_ref, enc_out_ref.shape[0])


def exchange(shard):
    return lax.all_to_all(shard, AXES, split_axis=0, concat_axis=0, tiled=True)


def turned(shard, axis, by):
    count = lax.axis_size(axis)
    return lax.ppermute(shard, axis, [(i, (i + by) % count) for i in range(count)])


def swapped(shard, axis, offset):
    count = lax.axis_size(axis)
    partner = list(range(count))
    for i in range(offset, count - 1, 2):
        partner[i], partner[i + 1] = i + 1, i
    return lax.ppermute(shard, axis, list(enumerate(partner)))


def from_neighbours(rim_rows):
    return (
        swapped(rim_rows, "grid", 0),
        swapped(rim_rows, "grid", 1),
        turned(rim_rows, "dom", 1),
        turned(rim_rows, "dom", -1),
    )


def to_neighbours(sends):
    return (
        swapped(sends[0], "grid", 0),
        swapped(sends[1], "grid", 1),
        turned(sends[2], "dom", -1),
        turned(sends[3], "dom", 1),
    )


def per_device(
    columns,
    column_live,
    col_weight,
    col_slot,
    node_static,
    boundary_idx,
    edge_src,
    edge_dst,
    edge_live,
    edge_weight,
    enc_in,
    enc_out,
    src_proj,
    dst_proj,
    msg_proj,
    node_cotangent,
):
    peers = lax.axis_size(AXES)
    cols, fin = columns.shape
    nodes, width = node_static.shape
    rim = boundary_idx.shape[0]
    edges = edge_src.shape[0]
    ext = 4 * rim
    bucket = cols // peers

    grid_at, grid_count = lax.axis_index("grid"), lax.axis_size("grid")
    dom_at, dom_count = lax.axis_index("dom"), lax.axis_size("dom")
    place = (grid_at * dom_count + dom_at) % (LANES // bucket)
    where = jnp.stack([grid_at, dom_at, jnp.int32(grid_count), jnp.int32(dom_count), place])

    lanes = (cols // LANES, LANES)
    held = [pltpu.VMEM(lanes, jnp.int32), pltpu.VMEM(lanes, jnp.int32), pltpu.VMEM(lanes, F32)]
    (packed,) = call(
        pack_body,
        [((peers, bucket + 4, fin), BF)],
        held + [pltpu.SemaphoreType.DMA((4,))],
        "pack",
        True,
        far=range(1, 5),
    )(
        where,
        columns.reshape(peers, bucket, fin),
        col_slot.reshape(lanes),
        column_live.reshape(lanes),
        col_weight.reshape(lanes),
    )
    packed = exchange(packed)

    node_shape = ((nodes, width), BF)
    node_wide = ((nodes, width), F32)
    rim_shape = ((rim, width), BF)
    edge_shape = ((width, edges), BF)
    edge_wide = ((width, edges), F32)
    full = pltpu.VMEM((width, 2 * rim), BF)
    edge_buf = pltpu.VMEM((width, edges), BF)
    table_buf = pltpu.VMEM((width, 2 * nodes + 2 * rim), BF)

    bound = boundary_idx.reshape(rim // LANES, LANES)
    pooled, col_slope, slot_picks, state0, rim0 = call(
        functools.partial(encode_body, bucket),
        [node_shape, ((width, cols), F32), ((nodes, cols), BF), node_shape, rim_shape],
        [
            edge_buf,
            pltpu.VMEM((2, cols), F32),
            pltpu.VMEM((nodes, rim), BF),
        ],
        "encode",
    )(packed, enc_in, enc_out, node_static, bound)

    edge_lanes = (edges // LANES, LANES)
    state0, edge_dst = lax.optimization_barrier((state0, edge_dst))
    layered = (src_proj.shape, BF)
    picks, rim_picks, rim_picks_t, edge_scale, src_t, dst_t = call(
        picks_body,
        [
            ((2 * nodes + ext, edges), BF),
            ((nodes, rim), BF),
            ((rim, nodes), BF),
            ((1, edges), F32),
            layered,
            layered,
        ],
        [],
        "picks",
    )(
        edge_src.reshape(edge_lanes),
        edge_dst.reshape(edge_lanes),
        edge_live.reshape(edge_lanes),
        edge_weight.reshape(edge_lanes),
        bound,
        src_proj,
        dst_proj,
    )

    rims0 = from_neighbours(rim0)
    (pre0,) = call(functools.partial(own_body, 0), [edge_wide], [table_buf], "own", True)(
        where, *rims0[2:], state0, src_t, dst_t, picks
    )
    slope0, act0, state1, rim1 = call(
        functools.partial(forward_body, 0),
        [edge_wide, node_shape, node_shape, rim_shape],
        [full, edge_buf],
        "forward",
        True,
    )(where, *rims0[:2], pre0, edge_scale, picks, state0, src_t, msg_proj, rim_picks_t)

    rims1 = from_neighbours(rim1)
    (back1,) = call(functools.partial(back_body, 1), [edge_wide], [], "back")(
        msg_proj, node_cotangent, edge_scale, picks
    )
    (pre1,) = call(functools.partial(own_body, 1), [edge_wide], [table_buf], "own", True)(
        where, *rims1[2:], state1, src_t, dst_t, picks
    )
    act_edges1, grad_pre1, *sends1 = call(
        functools.partial(turn_body, 1), [edge_shape, edge_shape] + [rim_shape] * 2, [full], "turn", True
    )(where, *rims1[:2], pre1, back1, edge_scale, picks, src_t)

    sends1 += call(dom_sums_body, [rim_shape] * 2, [], "sides")(picks, grad_pre1)
    returned1 = to_neighbours(sends1)
    own_shape = ((2 * nodes, width), BF)
    own1, partial1 = call(functools.partial(sums_body, 1), [own_shape, node_wide], [], "sums")(
        picks, grad_pre1, node_cotangent, src_proj, dst_proj
    )
    act1, node_out = call(functools.partial(out_body, 1), [node_shape, node_shape], [], "out")(
        picks, act_edges1, state1, msg_proj
    )
    partial1, act1 = lax.optimization_barrier((partial1, act1))
    grad1, back_src1, grad_pre0, *sends0 = call(
        functools.partial(backward_body, 1),
        [node_wide, node_shape, edge_shape] + [rim_shape] * 2,
        [],
        "backward",
        True,
    )(where, *returned1, partial1, src_proj, rim_picks, msg_proj, slope0, picks)

    sends0 += call(dom_sums_body, [rim_shape] * 2, [], "sides")(picks, grad_pre0)
    returned0 = to_neighbours(sends0)
    own0, partial0 = call(functools.partial(sums_body, 0), [own_shape, node_wide], [], "sums")(
        picks, grad_pre0, grad1, src_proj, dst_proj
    )
    keep, send = call(
        terms_body,
        [((2 * 3 * width, width // 2), dtype) for dtype in (F32, BF)],
        [],
        "terms",
        True,
    )(
        where,
        *(back_src1, state1, own1, act1, node_cotangent),
        *(*rims0, *sends0, state0, own0, act0, grad1),
    )
    send, *returned0 = lax.optimization_barrier((send, *returned0))
    hidden = enc_out.shape[0]
    keep_enc, send_enc = call(
        functools.partial(last_body, bucket),
        [((fin + hidden, width // 2), dtype) for dtype in (F32, BF)],
        [],
        "last",
        True,
    )(where, *returned0, partial0, src_proj, rim_picks, packed, enc_out, pooled, col_slope, slot_picks)

    total_rows = 2 * 3 * width + fin + hidden
    share = -(-total_rows // (16 * peers)) * 16
    rows = peers * share
    (merged,) = call(merge_body, [((rows, width // 2), BF)], [], "merge")(
        keep,
        swapped(send, "dom", 0),
        keep_enc,
        swapped(send_enc, "dom", 0),
    )
    parts = exchange(merged.reshape(peers, share, width // 2))
    (spread,) = call(share_body, [((peers, share, width // 2), BF)], [], "share")(parts)
    mine = exchange(spread).reshape(rows, width // 2)
    layer_shape = ((2, width, width), F32)
    grads = call(
        unpack_body,
        [((fin, width), F32), ((hidden, width), F32), layer_shape, layer_shape, layer_shape],
        [],
        "unpack",
        True,
    )(where, mine, swapped(mine, "dom", 0))
    return (node_out, *grads)


def solution(mesh):
    rows = P(AXES, None)
    flat = P(AXES)
    placed = (rows, flat, flat, flat, rows, flat, flat, flat, flat, flat, P(), P(), P(), P(), P(), rows)
    return jax.shard_map(
        per_device,
        mesh=mesh,
        in_specs=placed,
        out_specs=(rows, P(), P(), P(), P(), P()),
        check_vma=False,
    )
```
